32 devices in a mesh: dp: 8 (over y, x, core), seq: 4 (over z).
Axes of the slice: x: 2, y: 2, z: 4, core: 2. Of those that a mesh axis runs over, the one named last changes fastest.
Arguments:
- tokens: bfloat16 [32, 1024, 1024], P('dp', 'seq'), may hold values from -6 to 6
- prefix_len: int32 [32], P('dp'), may hold values from 102 to 960, as said below
- norm1_gain: bfloat16 [1024], P(('dp', 'seq')), may hold values from 0.5 to 1.5
- query_weight: bfloat16 [1024, 512], P(('dp', 'seq')), may hold values from -0.1875 to 0.1875
- key_weight: bfloat16 [1024, 512], P(('dp', 'seq')), may hold values from -0.1875 to 0.1875
- value_weight: bfloat16 [1024, 1024], P(('dp', 'seq')), may hold values from -0.1875 to 0.1875
- gate_weight: bfloat16 [1024, 1024], P(('dp', 'seq')), may hold values from -0.1875 to 0.1875
- decay_down: bfloat16 [1024, 16], P(('dp', 'seq')), may hold values from -0.1875 to 0.1875
- decay_up: bfloat16 [16, 512], P(None, ('dp', 'seq')), may hold values from -1.5 to 1.5
- decay_bias: bfloat16 [512], P(('dp', 'seq')), may hold values from 0 to 10
- group_gain: bfloat16 [256], P(('dp', 'seq')), may hold values from 0.5 to 1.5
- out_weight: bfloat16 [1024, 1024], P(('dp', 'seq')), may hold values from -0.25 to 0.25
- norm2_gain: bfloat16 [1024], P(('dp', 'seq')), may hold values from 0.5 to 1.5
- ffn_gate: bfloat16 [1024, 2816], P(('dp', 'seq')), may hold values from -0.1875 to 0.1875
- ffn_up: bfloat16 [1024, 2816], P(('dp', 'seq')), may hold values from -0.1875 to 0.1875
- ffn_down: bfloat16 [2816, 1024], P(None, ('dp', 'seq')), may hold values from -0.21875 to 0.21875
- out_grad: bfloat16 [32, 1024, 1024], P('dp', 'seq'), may hold values from -6 to 6
Outputs:
- layer_out: bfloat16 [32, 1024, 1024], P('dp', 'seq')
- tokens_grad: float32 [32, 1024, 1024], P('dp', 'seq')
- norm1_gain_grad: float32 [1024], P(('dp', 'seq'))
- query_weight_grad: float32 [1024, 512], P(('dp', 'seq'))
- key_weight_grad: float32 [1024, 512], P(('dp', 'seq'))
- value_weight_grad: float32 [1024, 1024], P(('dp', 'seq'))
- gate_weight_grad: float32 [1024, 1024], P(('dp', 'seq'))
- decay_down_grad: float32 [1024, 16], P(('dp', 'seq'))
- decay_up_grad: float32 [16, 512], P(None, ('dp', 'seq'))
- decay_bias_grad: float32 [512], P(('dp', 'seq'))
- group_gain_grad: float32 [256], P(('dp', 'seq'))
- out_weight_grad: float32 [1024, 1024], P(('dp', 'seq'))
- norm2_gain_grad: float32 [1024], P(('dp', 'seq'))
- ffn_gate_grad: float32 [1024, 2816], P(('dp', 'seq'))
- ffn_up_grad: float32 [1024, 2816], P(('dp', 'seq'))
- ffn_down_grad: float32 [2816, 1024], P(None, ('dp', 'seq'))
The draws below stay inside these ranges and needn't reach their ends.
Inputs may be any that keep to these rules, and one draw needn't show every extreme that they name: `prefix_len`: some sequence has a prefix of exactly 960 tokens.
All inputs are finite; a program needn't handle non-finite values.
Results may differ from the reference program's by a relative error of at most 0.033.
Values may be sent and summed in bfloat16 or wider, within the bound.
A program may use at most 256 MiB of HBM per device.

```python
import jax
import jax.numpy as jnp
from jax import lax

D = 1024
KEYS = 512
VALS = 1024
HEADS = 4
RANK = 16
FF = 2816
SPAN = 64
HEAD_K = 128
HEAD_V = 256
SEQS = 32
LENGTH = 1024


def draw_prefix_len(key, part):
    key_values, key_place = jax.random.split(key)
    lengths = jax.random.randint(key_values, (SEQS,), LENGTH // 10, LENGTH - SPAN + 1)
    chosen = jax.random.randint(key_place, (), 0, SEQS)
    return jnp.where(jnp.arange(SEQS) == chosen, LENGTH - SPAN, lengths).astype(jnp.int32)


def block_levels(rng, extent, cuts, low, largest):
    def one(axis_at, parts):
        draws = jax.random.uniform(jax.random.fold_in(jax.random.fold_in(rng, 6), axis_at), (parts,), jnp.float32, low / len(cuts), largest / len(cuts))
        return jnp.repeat(jnp.exp(draws), extent[axis_at] // parts).reshape((-1,) + (1,) * (len(extent) - axis_at - 1))

    gain = one(*cuts[0])
    for cut in cuts[1:]:
        gain = gain * one(*cut)
    return gain


def bell_draw(own_key, extent, scale, most, cuts=(), held_as=jnp.bfloat16):
    array = scale * jax.random.normal(own_key, extent, jnp.float32)
    if cuts:
        array = array * block_levels(own_key, extent, cuts, -0.22, 0.18)
    return jnp.clip(array, -most, most).astype(held_as)


def setup_inputs(seed: int = 0) -> dict:
    keys = jax.random.split(jax.random.key(seed), 18)
    return {
        "tokens": bell_draw(keys[0], (SEQS, LENGTH, D), 1.0, 6.0, ((0, 8), (1, 4))),
        "prefix_len": draw_prefix_len(jax.random.fold_in(keys[17], 71), 0),
        "norm1_gain": jnp.clip(1.0 + 0.1 * jax.random.normal(keys[2], (D,), jnp.float32), 0.5, 1.5).astype(jnp.bfloat16),
        "query_weight": bell_draw(keys[3], (D, KEYS), D ** -0.5, 0.1875, ((0, 32),)),
        "key_weight": bell_draw(keys[4], (D, KEYS), D ** -0.5, 0.1875, ((0, 32),)),
        "value_weight": bell_draw(keys[5], (D, VALS), D ** -0.5, 0.1875, ((0, 32),)),
        "gate_weight": bell_draw(keys[6], (D, VALS), D ** -0.5, 0.1875, ((0, 32),)),
        "decay_down": bell_draw(keys[7], (D, RANK), D ** -0.5, 0.1875, ((0, 32),)),
        "decay_up": bell_draw(keys[8], (RANK, KEYS), RANK ** -0.5, 1.5, ((1, 32),)),
        "decay_bias": jnp.clip(10.0 * jax.random.uniform(keys[9], (KEYS,), jnp.float32) ** block_levels(keys[9], (KEYS,), ((0, 32),), -0.2, 0.2), 0.0, 10.0).astype(jnp.bfloat16),
        "group_gain": jnp.clip(1.0 + 0.1 * jax.random.normal(keys[10], (HEAD_V,), jnp.float32), 0.5, 1.5).astype(jnp.bfloat16),
        "out_weight": bell_draw(keys[11], (VALS, D), (VALS // 2) ** -0.5, 0.25, ((0, 32),)),
        "norm2_gain": jnp.clip(1.0 + 0.1 * jax.random.normal(keys[12], (D,), jnp.float32), 0.5, 1.5).astype(jnp.bfloat16),
        "ffn_gate": bell_draw(keys[13], (D, FF), D ** -0.5, 0.1875, ((0, 32),)),
        "ffn_up": bell_draw(keys[14], (D, FF), D ** -0.5, 0.1875, ((0, 32),)),
        "ffn_down": bell_draw(keys[15], (FF, D), (FF // 4) ** -0.5, 0.21875, ((1, 32),)),
        "out_grad": bell_draw(keys[16], (SEQS, LENGTH, D), 1.0, 6.0, ((0, 8), (1, 4))),
    }


norm_eps = 1e-05

@jax.custom_vjp
def low(v):
    return lax.optimization_barrier(v.astype(jnp.bfloat16)).astype(jnp.float32)

@jax.custom_vjp
def low_back(v):
    return v

def low_keep(v):
    return (low(v), None)

def low_pass(kept, grad):
    return (grad,)

def back_keep(v):
    return (v, None)

def back_low(kept, grad):
    return (low(grad),)
low.defvjp(low_keep, low_pass)
low_back.defvjp(back_keep, back_low)

def exact_dot(left_side, right_side):
    return jnp.dot(left_side, right_side, precision=lax.Precision.HIGHEST, preferred_element_type=jnp.float32)

def precise_summation(pattern, *operands):
    return jnp.einsum(pattern, *operands, precision=lax.Precision.HIGHEST, preferred_element_type=jnp.float32)

def rms_norm(values, gain_row):
    return values * lax.rsqrt(lax.optimization_barrier(jnp.mean(values * values, axis=-1, keepdims=True)) + norm_eps) * gain_row

def block_step(carried_state, pieces):
    query_block, key_tile, value_tile, decay_block = pieces
    cumulative_decay = jnp.cumsum(decay_block, axis=0)
    running_totals = cumulative_decay[-1]
    query_input = query_block * jnp.exp(cumulative_decay)
    key_in = key_tile * jnp.exp(-cumulative_decay)
    lower_mask = jnp.tril(jnp.ones((SPAN, SPAN), jnp.float32))
    attention_scores = precise_summation('ihk,jhk->hij', query_input, key_in) * lower_mask
    block_output = precise_summation('ubn,nup->bup', attention_scores, value_tile) + precise_summation('yes,esp->yep', query_input, carried_state)
    carried_state = jnp.exp(running_totals)[:, :, None] * carried_state + precise_summation('ndp,ndq->dpq', key_tile * jnp.exp(running_totals - cumulative_decay), value_tile)
    return (carried_state, block_output)

def mixer_heads(query_matrix, key_matrix, value_matrix, decays, prefix):
    length = query_matrix.shape[0]
    blocks = length // SPAN
    shaped = (query_matrix.reshape(blocks, SPAN, HEADS, HEAD_K), key_matrix.reshape(blocks, SPAN, HEADS, HEAD_K), value_matrix.reshape(blocks, SPAN, HEADS, HEAD_V), decays.reshape(blocks, SPAN, HEADS, HEAD_K))
    start_state = jnp.zeros((HEADS, HEAD_K, HEAD_V), jnp.float32)
    final_state, causal = lax.scan(jax.checkpoint(block_step), start_state, shaped)
    causal = causal.reshape(length, HEADS, HEAD_V)
    places = jnp.arange(length, dtype=jnp.int32)
    running = jnp.cumsum(decays, axis=0)
    at_end = (places == prefix - 1).astype(jnp.float32)
    end_cum = lax.optimization_barrier(jnp.sum(at_end[:, None, None] * running, axis=0))
    keep_mask = places <= prefix - 1
    exponent = jnp.where(keep_mask[:, None, None], end_cum[None] - running, 0.0)
    weight_bundle = jnp.exp(exponent) * keep_mask.astype(jnp.float32)[:, None, None]
    prefix_carry_state = precise_summation('ndp,ndq->dpq', key_matrix * weight_bundle, value_matrix)
    prefix_output = precise_summation('yes,esp->yep', query_matrix, prefix_carry_state)
    inside = (places < prefix).astype(jnp.float32)[:, None, None]
    return inside * prefix_output + (1.0 - inside) * causal

def forward_sequence(tokens, prefix, params):
    gain_one, weight_q, weight_k, weight_v, weight_g, weight_down, weight_up, bias_row, gain_group, weight_o, gain_two, weight_gate, weight_upper, weight_lower = params
    length = tokens.shape[0]
    normed = low(rms_norm(tokens, gain_one))
    queries = low_back(low(exact_dot(normed, weight_q)))
    key_matrix = low_back(low(exact_dot(normed, weight_k)))
    value_matrix = low_back(low(exact_dot(normed, weight_v)))
    gate_out = low_back(exact_dot(normed, weight_g))
    lowrank = low_back(low(exact_dot(normed, weight_down)))
    logits = low_back(exact_dot(lowrank, weight_up) + bias_row)
    decays = jax.nn.log_sigmoid(logits) / 16.0
    mixed = mixer_heads(queries.reshape(length, HEADS, HEAD_K), key_matrix.reshape(length, HEADS, HEAD_K), value_matrix.reshape(length, HEADS, HEAD_V), decays.reshape(length, HEADS, HEAD_K), prefix)
    normed_group = rms_norm(mixed, gain_group)
    gated_rows = low(normed_group.reshape(length, VALS) * jax.nn.silu(gate_out))
    branch = low_back(exact_dot(gated_rows, weight_o))
    resid_mid = tokens + branch
    normed_two = low(rms_norm(resid_mid, gain_two))
    gate_part = low_back(exact_dot(normed_two, weight_gate))
    up_part = low_back(exact_dot(normed_two, weight_upper))
    hidden = low(jax.nn.silu(gate_part) * up_part)
    ffn_out = low_back(exact_dot(hidden, weight_lower))
    return resid_mid + ffn_out

def add_pair(first_term, second_term):
    return first_term + second_term

def reference(tokens, prefix_len, norm1_gain, query_weight, key_weight, value_weight, gate_weight, decay_down, decay_up, decay_bias, group_gain, out_weight, norm2_gain, ffn_gate, ffn_up, ffn_down, out_grad):
    params = tuple((weight.astype(jnp.float32) for weight in (norm1_gain, query_weight, key_weight, value_weight, gate_weight, decay_down, decay_up, decay_bias, group_gain, out_weight, norm2_gain, ffn_gate, ffn_up, ffn_down)))

    def per_sequence(running_totals, seq_items):
        seq_tokens, seq_prefix, seq_grad = seq_items

        def forward_of(token_values, weight_set):
            return forward_sequence(token_values, seq_prefix, weight_set)
        outputs, pullback = jax.vjp(forward_of, seq_tokens.astype(jnp.float32), params)
        grad_tokens, grad_params = pullback(seq_grad.astype(jnp.float32))
        running_totals = jax.tree.map(add_pair, running_totals, grad_params)
        return (running_totals, (outputs.astype(jnp.bfloat16), grad_tokens))
    zero_grads = jax.tree.map(jnp.zeros_like, params)
    running_totals, stacked = lax.scan(per_sequence, zero_grads, (tokens, prefix_len, out_grad))
    return (stacked[0], stacked[1], running_totals[0], running_totals[1], running_totals[2], running_totals[3], running_totals[4], running_totals[5], running_totals[6], running_totals[7], running_totals[8], running_totals[9], running_totals[10], running_totals[11], running_totals[12], running_totals[13])
```

```python
from functools import partial

import jax
import jax.numpy as jnp
import numpy as np
from jax import lax
from jax.sharding import Mesh
from jax.sharding import PartitionSpec as P

KEYS = 512
VALS = 1024
HEADS = 4
SPAN = 64
HEAD_K = 128
HEAD_V = 256
FF = 2816


norm_eps = 1e-05


def entering(part, axis, combine, identity):
    place = lax.axis_index(axis)
    gathered = jax.tree.map(lambda a: lax.all_gather(a, axis), part)
    state = jax.tree.map(lambda a, e: jnp.zeros_like(a) + jnp.asarray(e, a.dtype), part, identity)

    def entering_one(lap, state):
        return combine(
            state, jax.tree.map(lambda a: lax.dynamic_index_in_dim(a, lap, 0, False), gathered)
        )

    return lax.fori_loop(0, place, entering_one, state)


def carried_in(x, axis, join, neutral):
    count = lax.axis_size(axis)
    place = lax.axis_index(axis)
    ahead = count - 1 - place
    gathered = jax.tree.map(
        lambda a, kind: lax.all_gather(a.astype(kind), axis),
        x,
        jax.tree.map(lambda a: jnp.bfloat16 if a.dtype == jnp.float32 else a.dtype, x),
    )
    state = jax.tree.map(lambda a, e: jnp.zeros_like(a) + jnp.asarray(e, a.dtype), x, neutral)

    def carried_one(lap, state):
        source = count - 1 - lap
        return join(
            state,
            jax.tree.map(
                lambda a, own: lax.dynamic_index_in_dim(a, source, 0, False).astype(own.dtype),
                gathered,
                x,
            ),
        )

    return lax.fori_loop(0, ahead, carried_one, state)


def precise_summation(pattern, *operands):
    return jnp.einsum(
        pattern, *operands, precision=lax.Precision.HIGHEST, preferred_element_type=jnp.float32
    )


def project(inputs, weight):
    return jnp.einsum("std,de->ste", inputs, weight, preferred_element_type=jnp.float32)


def back_project(gradient, weight):
    return jnp.einsum("ste,de->std", gradient, weight, preferred_element_type=jnp.float32)


def weight_grad(inputs, gradient):
    return jnp.einsum("std,ste->de", inputs, gradient, preferred_element_type=jnp.float32)


def rms_scale(values):
    return lax.rsqrt(jnp.mean(values * values, axis=-1, keepdims=True) + norm_eps)


def rms_back(grad_unit, unit_rows, scale_rows):
    return scale_rows * (
        grad_unit - unit_rows * jnp.mean(grad_unit * unit_rows, axis=-1, keepdims=True)
    )


def silu_slope(values):
    logistic = jax.nn.sigmoid(values)
    return logistic * (1.0 + values * (1.0 - logistic))


def chain_combine(earlier, later):
    return (earlier[0] + later[0], jnp.exp(later[0])[..., None] * earlier[1] + later[1])


def lower_ones(extent):
    indices = jnp.arange(extent)
    return (indices[:, None] >= indices[None, :]).astype(jnp.float32)


def local_states(key_matrix, valued, decays):
    seq_count, tok_count, head_count, key_width = key_matrix.shape
    blocks = tok_count // SPAN
    key_blocks = key_matrix.reshape(seq_count, blocks, SPAN, head_count, key_width)
    value_blocks = valued.reshape(seq_count, blocks, SPAN, head_count, valued.shape[-1])
    decay_blocks = decays.reshape(seq_count, blocks, SPAN, head_count, key_width)
    cumulative_decay = precise_summation("ij,snjhk->snihk", lower_ones(SPAN), decay_blocks)
    running_totals = cumulative_decay[:, :, -1]
    shares = precise_summation(
        "snjhk,snjhv->snhkv",
        key_blocks * jnp.exp(running_totals[:, :, None] - cumulative_decay),
        value_blocks,
    )
    carried_state = jnp.zeros_like(shares[:, 0])
    starts = []
    for number in range(blocks):
        starts.append(carried_state)
        carried_state = (
            jnp.exp(running_totals[:, number])[..., None] * carried_state + shares[:, number]
        )
    return (
        jnp.sum(running_totals, axis=1),
        carried_state,
        jnp.stack(starts, axis=1),
        cumulative_decay,
        running_totals,
    )


def local_outputs(
    queries,
    key_matrix,
    valued,
    incoming,
    starts,
    cumulative_decay,
    running_totals,
    end_local=None,
    is_owner=None,
):
    seq_count, tok_count, head_count, key_width = queries.shape
    val_width = valued.shape[-1]
    blocks = tok_count // SPAN
    query_blocks = queries.reshape(seq_count, blocks, SPAN, head_count, key_width)
    key_blocks = key_matrix.reshape(seq_count, blocks, SPAN, head_count, key_width)
    value_blocks = valued.reshape(seq_count, blocks, SPAN, head_count, val_width)
    before = jnp.cumsum(running_totals, axis=1) - running_totals
    block_states = jnp.exp(before)[..., None] * incoming[:, None] + starts
    query_input = query_blocks * jnp.exp(cumulative_decay)
    key_in = key_blocks * jnp.exp(-cumulative_decay)
    attention_scores = precise_summation("snihk,snjhk->snhij", query_input, key_in) * lower_ones(
        SPAN
    )
    causal = precise_summation(
        "snhij,snjhv->snihv", attention_scores, value_blocks
    ) + precise_summation("snihk,snhkv->snihv", query_input, block_states)
    causal = causal.reshape(seq_count, tok_count, head_count, val_width)
    position_cum = (cumulative_decay + before[:, :, None]).reshape(
        seq_count, tok_count, head_count, key_width
    )
    places = jnp.arange(tok_count)
    select = (places[None, :] == end_local[:, None]).astype(jnp.float32)
    end_cum = precise_summation("st,sthk->shk", select, position_cum)
    keep_mask = (places[None, :] <= end_local[:, None]) & is_owner[:, None]
    exponent = jnp.where(keep_mask[:, :, None, None], end_cum[:, None] - position_cum, 0.0)
    weight_bundle = jnp.exp(exponent) * keep_mask.astype(jnp.float32)[:, :, None, None]
    partial_state = precise_summation("sthk,sthv->shkv", key_matrix * weight_bundle, valued)
    owner_weight = is_owner.astype(jnp.float32)[:, None, None, None]
    partial_state = partial_state + owner_weight * jnp.exp(end_cum)[..., None] * incoming
    return (causal, partial_state)


def chain_forward(total_dev, state_dev, seq):
    identity = (jnp.zeros_like(total_dev), jnp.zeros_like(state_dev))
    return entering((total_dev, state_dev), seq, chain_combine, identity)[1]


def chain_backward(total_dev, grad_in, seq):
    identity = (jnp.zeros_like(total_dev), jnp.zeros_like(grad_in))
    return carried_in((total_dev, grad_in), seq, chain_combine, identity)[1]


EXTRA = 128


def physical_axes(mesh):
    shape = mesh.devices.shape
    names = []
    sizes = []
    for axis, extent in enumerate(shape):
        line = np.moveaxis(mesh.devices, axis, 0).reshape(extent, -1)[:, 0]
        places = [tuple(d.coords) + (d.core_on_chip,) for d in line]
        parts = []
        for dim, label in enumerate(("x", "y", "z", "core")):
            values = [p[dim] for p in places]
            if len(set(values)) > 1:
                step = next(i for i in range(extent) if values[i] != values[0])
                parts.append((step, label, len(set(values))))
        for step, label, size in sorted(parts, reverse=True):
            names.append(label)
            sizes.append(size)
    return tuple(names), tuple(sizes)


def pack_mixer(norm1_gain, norm2_gain, query, key, value, gate, down, up, bias, group, out):
    rows = query.shape[0]
    small = jnp.zeros((rows, EXTRA), query.dtype)
    small = small.at[:, :16].set(down)
    small = small.at[:, 16].set(norm1_gain)
    small = small.at[:, 17].set(norm2_gain)
    small = small.at[: bias.shape[0], 18].set(bias)
    small = small.at[: group.shape[0], 19].set(group)
    small = small.at[:, 24:32].set(up.T.reshape(rows, 8))
    return jnp.concatenate([query, key, value, gate, out, small], axis=1)


def unpack_small(small, devices):
    rows = small.shape[0] // devices
    by_device = small.reshape(devices, rows, EXTRA)
    down = small[:, :16]
    gain_one = small[:, 16]
    gain_two = small[:, 17]
    bias = by_device[:, : KEYS // devices, 18].reshape(KEYS)
    group = by_device[:, : HEAD_V // devices, 19].reshape(HEAD_V)
    up = small[:, 24:32].reshape(KEYS, 16).T
    return down, gain_one, gain_two, bias, group, up


def pack_small_grads(down, gain_one, gain_two, bias, group, up, devices):
    rows = gain_one.shape[0] // devices

    def column(vector):
        parts = vector.reshape(devices, -1)
        parts = jnp.pad(parts, ((0, 0), (0, rows - parts.shape[1])))
        return parts.reshape(devices * rows, 1)

    pieces = [
        down,
        gain_one[:, None],
        gain_two[:, None],
        column(bias),
        column(group),
        jnp.zeros((rows * devices, 4), jnp.float32),
        up.T.reshape(rows * devices, 8),
        jnp.zeros((rows * devices, EXTRA - 32), jnp.float32),
    ]
    return jnp.concatenate(pieces, axis=1)


def reduce_to_owner(total, names, sizes):
    rows = total.shape[0]
    width = total.shape[1]
    devices = int(np.prod(sizes))
    if "core" in names:
        at = names.index("core")
        before = int(np.prod(sizes[:at], initial=1))
        after = rows // before // sizes[at]
        shaped = total.reshape(before, sizes[at], after, width)
        core = lax.axis_index("core")
        kept = lax.dynamic_index_in_dim(shaped, core, 1, False)
        given = lax.dynamic_index_in_dim(shaped, 1 - core, 1, False)
        taken = lax.ppermute(given, "core", [(0, 1), (1, 0)])
        total = (kept + taken).reshape(rows // sizes[at], width)
    rest = tuple(n for n in names if n != "core")
    return lax.psum_scatter(total, rest, scatter_dimension=0, tiled=True)


def local(
    names,
    sizes,
    seq,
    tokens,
    prefix_len,
    norm1_gain,
    query_weight,
    key_weight,
    value_weight,
    gate_weight,
    decay_down,
    decay_up,
    decay_bias,
    group_gain,
    out_weight,
    norm2_gain,
    ffn_gate,
    ffn_up,
    ffn_down,
    out_grad,
):
    devices = int(np.prod(sizes))
    mixer_full = lax.all_gather(
        pack_mixer(
            norm1_gain,
            norm2_gain,
            query_weight,
            key_weight,
            value_weight,
            gate_weight,
            decay_down,
            decay_up,
            decay_bias,
            group_gain,
            out_weight,
        ),
        names,
        axis=0,
        tiled=True,
    )
    ffn_full = lax.all_gather(
        jnp.concatenate([ffn_gate, ffn_up, ffn_down.T], axis=1), names, axis=0, tiled=True
    )
    weight_q = mixer_full[:, :512]
    weight_k = mixer_full[:, 512:1024]
    weight_v = mixer_full[:, 1024:2048]
    weight_g = mixer_full[:, 2048:3072]
    weight_o = mixer_full[:, 3072:4096]
    weight_down, gain_one, gain_two, bias_full, gain_group, weight_up = unpack_small(
        mixer_full[:, 4096:], devices
    )
    weight_gate = ffn_full[:, :FF]
    weight_upper = ffn_full[:, FF : 2 * FF]
    weight_lower = ffn_full[:, 2 * FF :].T
    seq_count, tok_count, feature_count = tokens.shape
    resid_in = tokens.astype(jnp.float32)
    scale_one = rms_scale(resid_in)
    unit_one = resid_in * scale_one
    normed = (unit_one * gain_one.astype(jnp.float32)).astype(jnp.bfloat16)
    queries = project(normed, weight_q).astype(jnp.bfloat16)
    key_matrix = project(normed, weight_k).astype(jnp.bfloat16)
    value_matrix = project(normed, weight_v).astype(jnp.bfloat16)
    gate_out = project(normed, weight_g)
    lowrank = project(normed, weight_down).astype(jnp.bfloat16)
    logits = project(lowrank, weight_up) + bias_full.astype(jnp.float32)
    decays = jax.nn.log_sigmoid(logits) / 16.0
    query_heads = queries.astype(jnp.float32).reshape(seq_count, tok_count, HEADS, HEAD_K)
    key_heads = key_matrix.astype(jnp.float32).reshape(seq_count, tok_count, HEADS, HEAD_K)
    value_heads = value_matrix.astype(jnp.float32).reshape(seq_count, tok_count, HEADS, HEAD_V)
    decay_heads = decays.reshape(seq_count, tok_count, HEADS, HEAD_K)
    seg_start = lax.axis_index(seq) * tok_count
    places = seg_start + jnp.arange(tok_count)
    in_prefix = (places[None, :] < prefix_len[:, None]).astype(jnp.float32)[:, :, None, None]
    end_local = prefix_len - 1 - seg_start
    is_owner = (end_local >= 0) & (end_local < tok_count)
    local_out, pull_states = jax.vjp(local_states, key_heads, value_heads, decay_heads)
    total_dev, state_dev, starts, cumulative_decay, running_totals = local_out
    incoming = chain_forward(total_dev, state_dev, seq)
    outputs_of = partial(local_outputs, end_local=end_local, is_owner=is_owner)
    (causal, partial_state), pull_outputs = jax.vjp(
        outputs_of,
        query_heads,
        key_heads,
        value_heads,
        incoming,
        starts,
        cumulative_decay,
        running_totals,
    )
    prefix_carry_state = lax.psum(partial_state.astype(jnp.bfloat16), seq).astype(jnp.float32)
    prefix_output = precise_summation("sthk,shkv->sthv", query_heads, prefix_carry_state)
    mixed_heads = in_prefix * prefix_output + (1.0 - in_prefix) * causal
    scale_group = rms_scale(mixed_heads)
    unit_group = mixed_heads * scale_group
    normed_group = unit_group * gain_group.astype(jnp.float32)
    swish_gate = jax.nn.silu(gate_out).reshape(seq_count, tok_count, HEADS, HEAD_V)
    gated_rows = (
        (normed_group * swish_gate).reshape(seq_count, tok_count, VALS).astype(jnp.bfloat16)
    )
    branch = project(gated_rows, weight_o)
    resid_mid = resid_in + branch
    scale_two = rms_scale(resid_mid)
    unit_two = resid_mid * scale_two
    normed_two = (unit_two * gain_two.astype(jnp.float32)).astype(jnp.bfloat16)
    gate_part = project(normed_two, weight_gate)
    up_part = project(normed_two, weight_upper)
    gate_act = jax.nn.silu(gate_part)
    hidden = (gate_act * up_part).astype(jnp.bfloat16)
    ffn_out = project(hidden, weight_lower)
    layer_out = (resid_mid + ffn_out).astype(jnp.bfloat16)
    grad_out = out_grad.astype(jnp.float32)
    grad_hidden = back_project(out_grad, weight_lower)
    lower_grad = weight_grad(out_grad, hidden)
    grad_gate = (grad_hidden * up_part * silu_slope(gate_part)).astype(jnp.bfloat16)
    grad_up = (grad_hidden * gate_act).astype(jnp.bfloat16)
    gate_w_grad = weight_grad(normed_two, grad_gate)
    up_w_grad = weight_grad(normed_two, grad_up)
    grad_normed_two = back_project(grad_gate, weight_gate) + back_project(grad_up, weight_upper)
    gain_two_grad = jnp.sum(grad_normed_two * unit_two, axis=(0, 1))
    grad_mid = grad_out + rms_back(
        grad_normed_two * gain_two.astype(jnp.float32), unit_two, scale_two
    )
    ffn_mine = reduce_to_owner(
        jnp.concatenate([gate_w_grad, up_w_grad, lower_grad], axis=1).astype(jnp.bfloat16),
        names,
        sizes,
    ).astype(jnp.float32)
    grad_branch = grad_mid.astype(jnp.bfloat16)
    out_w_grad = weight_grad(gated_rows, grad_branch)
    grad_gated = back_project(grad_branch, weight_o).reshape(seq_count, tok_count, HEADS, HEAD_V)
    grad_normed_group = grad_gated * swish_gate
    grad_swish = (grad_gated * normed_group).reshape(seq_count, tok_count, VALS)
    grad_gate_out = (grad_swish * silu_slope(gate_out)).astype(jnp.bfloat16)
    group_grad = jnp.sum(grad_normed_group * unit_group, axis=(0, 1, 2))
    grad_mixed = rms_back(
        grad_normed_group * gain_group.astype(jnp.float32), unit_group, scale_group
    )
    grad_prefix = grad_mixed * in_prefix
    grad_causal = grad_mixed - grad_prefix
    grad_query_pre = precise_summation("sthv,shkv->sthk", grad_prefix, prefix_carry_state)
    prefix_term = precise_summation("sthk,sthv->shkv", query_heads, grad_prefix)
    grad_state = lax.psum(prefix_term.astype(jnp.bfloat16), seq).astype(jnp.float32)
    grad_q_local, grad_k_local, grad_v_local, grad_in, grad_starts, grad_cum, grad_tot = (
        pull_outputs((grad_causal, grad_state))
    )
    grad_end = chain_backward(total_dev, grad_in, seq)
    grad_total = jnp.sum(incoming * grad_end, axis=-1) * jnp.exp(total_dev)
    grad_k_chain, grad_v_chain, grad_decay = pull_states(
        (grad_total, grad_end, grad_starts, grad_cum, grad_tot)
    )
    grad_q = (
        (grad_query_pre + grad_q_local).reshape(seq_count, tok_count, KEYS).astype(jnp.bfloat16)
    )
    grad_k = (grad_k_local + grad_k_chain).reshape(seq_count, tok_count, KEYS).astype(jnp.bfloat16)
    grad_v = (grad_v_local + grad_v_chain).reshape(seq_count, tok_count, VALS).astype(jnp.bfloat16)
    grad_logits = (
        grad_decay.reshape(seq_count, tok_count, KEYS) * jax.nn.sigmoid(-logits) / 16.0
    ).astype(jnp.bfloat16)
    bias_grad = jnp.sum(grad_logits.astype(jnp.float32), axis=(0, 1))
    up_rank_grad = weight_grad(lowrank, grad_logits)
    grad_lowrank = back_project(grad_logits, weight_up).astype(jnp.bfloat16)
    down_rank_grad = weight_grad(normed, grad_lowrank)
    grad_normed = (
        back_project(grad_q, weight_q)
        + back_project(grad_k, weight_k)
        + back_project(grad_v, weight_v)
        + back_project(grad_gate_out, weight_g)
        + back_project(grad_lowrank, weight_down)
    )
    gain_one_grad = jnp.sum(grad_normed * unit_one, axis=(0, 1))
    tokens_grad = grad_mid + rms_back(
        grad_normed * gain_one.astype(jnp.float32), unit_one, scale_one
    )
    small_grads = pack_small_grads(
        down_rank_grad, gain_one_grad, gain_two_grad, bias_grad, group_grad, up_rank_grad, devices
    )
    mine = reduce_to_owner(
        jnp.concatenate(
            [
                weight_grad(normed, grad_q),
                weight_grad(normed, grad_k),
                weight_grad(normed, grad_v),
                weight_grad(normed, grad_gate_out),
                out_w_grad,
                small_grads,
            ],
            axis=1,
        ).astype(jnp.bfloat16),
        names,
        sizes,
    ).astype(jnp.float32)
    small = mine[:, 4096:]
    rows = mine.shape[0]
    return (
        layer_out,
        tokens_grad,
        small[:, 16],
        mine[:, :512],
        mine[:, 512:1024],
        mine[:, 1024:2048],
        mine[:, 2048:3072],
        small[:, :16],
        small[:, 24:32].reshape(KEYS // devices, 16).T,
        small[: KEYS // devices, 18],
        small[: HEAD_V // devices, 19],
        mine[:, 3072:4096],
        small[:, 17],
        ffn_mine[:, :FF],
        ffn_mine[:, FF : 2 * FF],
        ffn_mine[:, 2 * FF :].T,
    )


def solution(mesh):
    names, sizes = physical_axes(mesh)
    cut = next(
        i for i in range(len(sizes) + 1) if np.prod(sizes[:i], initial=1) == mesh.shape["dp"]
    )
    dp, seq = names[:cut], names[cut:]
    split = Mesh(mesh.devices.reshape(sizes), names)
    return jax.shard_map(
        partial(local, names, sizes, seq),
        mesh=split,
        in_specs=(
            P(dp, seq, None),
            P(dp),
            P(names),
            P(names, None),
            P(names, None),
            P(names, None),
            P(names, None),
            P(names, None),
            P(None, names),
            P(names),
            P(names),
            P(names, None),
            P(names),
            P(names, None),
            P(names, None),
            P(None, names),
            P(dp, seq, None),
        ),
        out_specs=(
            P(dp, seq, None),
            P(dp, seq, None),
            P(names),
            P(names, None),
            P(names, None),
            P(names, None),
            P(names, None),
            P(names, None),
            P(None, names),
            P(names),
            P(names),
            P(names, None),
            P(names),
            P(names, None),
            P(names, None),
            P(None, names),
        ),
        check_vma=False,
    )
```

```python
from functools import partial

import jax
import jax.numpy as jnp
import numpy as np
from jax import lax
from jax.experimental import pallas as pl
from jax.experimental.pallas import tpu as pltpu
from jax.sharding import Mesh
from jax.sharding import PartitionSpec as P

KEYS = 512
VALS = 1024
HEADS = 4
SPAN = 64
HEAD_K = 128
HEAD_V = 256
FF = 2816


norm_eps = 1e-05


def project(inputs, weight):
    return jnp.einsum("std,de->ste", inputs, weight, preferred_element_type=jnp.float32)


def back_project(gradient, weight):
    return jnp.einsum("ste,de->std", gradient, weight, preferred_element_type=jnp.float32)


def weight_grad(inputs, gradient):
    return jnp.einsum("std,ste->de", inputs, gradient, preferred_element_type=jnp.float32)


def rms_scale(values):
    return lax.rsqrt(jnp.mean(values * values, axis=-1, keepdims=True) + norm_eps)


def rms_back(grad_unit, unit_rows, scale_rows):
    return scale_rows * (
        grad_unit - unit_rows * jnp.mean(grad_unit * unit_rows, axis=-1, keepdims=True)
    )


def silu_slope(values):
    logistic = jax.nn.sigmoid(values)
    return logistic * (1.0 + values * (1.0 - logistic))


CHUNK = 128
MESH = pl.DeviceIdType.MESH


def nn(a, b):
    return lax.dot_general(a, b, (((1,), (0,)), ((), ())), preferred_element_type=jnp.float32)


def nt(a, b):
    return lax.dot_general(a, b, (((1,), (1,)), ((), ())), preferred_element_type=jnp.float32)


def tn(a, b):
    return lax.dot_general(a, b, (((0,), (0,)), ((), ())), preferred_element_type=jnp.float32)


def low(values):
    return values.astype(jnp.bfloat16)


def wide(values):
    return values.astype(jnp.float32)


def three_way(ones, values):
    first = low(values)
    left = values - wide(first)
    second = low(left)
    third = low(left - wide(second))
    return nn(ones, first) + nn(ones, second) + nn(ones, third)


def iota(shape, dim):
    return lax.broadcasted_iota(jnp.int32, shape, dim)


def place_on(axes):
    place = 0
    for name, size in axes:
        place = place * size + lax.axis_index(name)
    return place


def device_at(axes, place):
    where = {}
    for name, size in reversed(axes):
        where[name] = lax.rem(place, size)
        place = lax.div(place, size)
    return where


def line_length(axes):
    return int(np.prod([size for _, size in axes]))


def greet(axes, place, count):
    barrier = pltpu.get_barrier_semaphore()

    @pl.when(place > 0)
    def _():
        pl.semaphore_signal(
            barrier, inc=1, device_id=device_at(axes, place - 1), device_id_type=MESH
        )

    @pl.when(place < count - 1)
    def _():
        pl.semaphore_signal(
            barrier, inc=1, device_id=device_at(axes, place + 1), device_id_type=MESH
        )

    @pl.when(jnp.logical_or(place == 0, place == count - 1))
    def _():
        pl.semaphore_wait(barrier, 1)

    @pl.when(jnp.logical_and(place > 0, place < count - 1))
    def _():
        pl.semaphore_wait(barrier, 2)


def send(source, target, send_sem, recv_sem, axes, place):
    return pltpu.make_async_remote_copy(
        src_ref=source,
        dst_ref=target,
        send_sem=send_sem,
        recv_sem=recv_sem,
        device_id=device_at(axes, place),
        device_id_type=MESH,
    )


def row_places(count):
    return iota((count, HEAD_K), 0)


def prefix_weights(cum, end_local, count):
    rows = row_places(count)
    owner = jnp.logical_and(end_local >= 0, end_local < count)
    end_cum = jnp.sum(jnp.where(rows == end_local, cum, 0.0), axis=0, keepdims=True)
    keep = jnp.logical_and(rows <= end_local, rows <= jnp.where(owner, count, -1))
    weights = jnp.where(keep, jnp.exp(jnp.where(keep, end_cum - cum, 0.0)), 0.0)
    return weights, jnp.exp(end_cum) * jnp.where(owner, 1.0, 0.0)


def chunk_parts(cum, chunk):
    begin = chunk * CHUNK
    piece = cum[begin : begin + CHUNK]
    if chunk:
        piece = piece - cum[begin - 1 : begin]
    return piece, piece[CHUNK - 1 :], piece[CHUNK // 2 - 1 : CHUNK // 2]


def forward_kernel(
    axes,
    prefix_ref,
    q_ref,
    k_ref,
    v_ref,
    decay_ref,
    mixed_ref,
    cum_ref,
    state_ref,
    prefix_state_ref,
    kv_ref,
    part_ref,
    edge_ref,
    right_out,
    right_in,
    left_out,
    left_in,
    right_sent,
    right_got,
    left_sent,
    left_got,
):
    count = line_length(axes)
    place = place_on(axes)
    seqs = prefix_ref.shape[0]
    toks = q_ref.shape[0] // seqs
    chunks = toks // CHUNK
    greet(axes, place, count)
    lower = low(jnp.where(iota((CHUNK, CHUNK), 0) >= iota((CHUNK, CHUNK), 1), 1.0, 0.0))
    causal = iota((CHUNK, CHUNK), 0) >= iota((CHUNK, CHUNK), 1)

    def to_right(i):
        return send(right_out.at[i], right_in.at[i], right_sent.at[i], right_got.at[i], axes, place + 1)

    def to_left(i):
        return send(left_out.at[i], left_in.at[i], left_sent.at[i], left_got.at[i], axes, place - 1)

    def states_of(seq, carry):
        rows = pl.ds(pl.multiple_of(seq * toks, toks), toks)
        end_local = prefix_ref[seq] - 1 - place * toks
        for head in range(HEADS):
            i = seq * HEADS + head
            keys = slice(head * HEAD_K, (head + 1) * HEAD_K)
            vals = slice(head * HEAD_V, (head + 1) * HEAD_V)
            before = jnp.zeros((1, HEAD_K), jnp.float32)
            key = wide(k_ref[rows, keys])
            value = v_ref[rows, vals]
            decay = decay_ref[rows, keys]
            pieces = []
            local = jnp.zeros((HEAD_V, HEAD_K), jnp.float32)
            for chunk in range(chunks):
                at = slice(chunk * CHUNK, (chunk + 1) * CHUNK)
                piece = three_way(lower, decay[at])
                total = piece[CHUNK - 1 :]
                share = tn(value[at], low(key[at] * jnp.exp(total - piece)))
                kv_ref[i, chunk] = share
                local = jnp.exp(total) * local + share
                pieces.append(piece + before)
                before = before + total
            cum = jnp.concatenate(pieces, axis=0)
            cum_ref[rows, keys] = cum
            weights, edge = prefix_weights(cum, end_local, toks)
            part_ref[i] = tn(value, low(key * weights))
            edge_ref[i] = jnp.broadcast_to(edge, (8, HEAD_K))

            @pl.when(place == 0)
            def _():
                right_out[i] = low(local)
                if count > 1:
                    to_right(i).start()

        return carry

    lax.fori_loop(0, seqs, states_of, 0)

    def outputs_of(seq, carry):
        rows = pl.ds(pl.multiple_of(seq * toks, toks), toks)
        for head in range(HEADS):
            i = seq * HEADS + head
            keys = slice(head * HEAD_K, (head + 1) * HEAD_K)
            vals = slice(head * HEAD_V, (head + 1) * HEAD_V)
            cum = cum_ref[rows, keys]
            query = wide(q_ref[rows, keys])
            key = wide(k_ref[rows, keys])
            value = v_ref[rows, vals]
            scores = []
            for chunk in range(chunks):
                at = slice(chunk * CHUNK, (chunk + 1) * CHUNK)
                piece, total, middle = chunk_parts(cum, chunk)
                raw = nt(
                    low(query[at] * jnp.exp(piece - middle)), low(key[at] * jnp.exp(middle - piece))
                )
                scores.append(low(jnp.where(causal, raw, 0.0)))

            @pl.when(place == 0)
            def _():
                right_in[i] = jnp.zeros((HEAD_V, HEAD_K), jnp.bfloat16)

            @pl.when(place > 0)
            def _():
                send(right_out.at[i], right_in.at[i], right_sent.at[i], right_got.at[i], axes, place - 1).wait_recv()

            state = wide(right_in[i])
            part = part_ref[i] + edge_ref[i][:1] * state
            part_ref[i] = part
            for chunk in range(chunks):
                at = slice(chunk * CHUNK, (chunk + 1) * CHUNK)
                piece, total, middle = chunk_parts(cum, chunk)
                narrow = low(state)
                state_ref[i, chunk] = narrow
                output = nn(scores[chunk], value[at]) + nt(
                    low(query[at] * jnp.exp(piece)), narrow
                )
                mixed_ref[pl.ds(seq * toks + chunk * CHUNK, CHUNK), vals] = output
                state = jnp.exp(total) * state + kv_ref[i, chunk]
            state_ref[i, chunks] = low(state)

            @pl.when(jnp.logical_and(place > 0, place < count - 1))
            def _():
                right_out[i] = low(state)
                to_right(i).start()

            if count > 1:

                @pl.when(place == count - 1)
                def _():
                    left_out[i] = low(part)
                    to_left(i).start()

        return carry

    lax.fori_loop(0, seqs, outputs_of, 0)

    def prefix_of(seq, carry):
        rows = pl.ds(pl.multiple_of(seq * toks, toks), toks)
        end_local = prefix_ref[seq] - 1 - place * toks
        inside = iota((toks, HEAD_V), 0) <= end_local
        for head in range(HEADS):
            i = seq * HEADS + head
            keys = slice(head * HEAD_K, (head + 1) * HEAD_K)
            vals = slice(head * HEAD_V, (head + 1) * HEAD_V)

            @pl.when(place < count - 1)
            def _():
                send(left_out.at[i], left_in.at[i], left_sent.at[i], left_got.at[i], axes, place + 1).wait_recv()

            @pl.when(place == count - 1)
            def _():
                left_in[i] = jnp.zeros((HEAD_V, HEAD_K), jnp.bfloat16)

            whole = low(part_ref[i] + wide(left_in[i]))

            @pl.when(jnp.logical_and(place > 0, place < count - 1))
            def _():
                left_out[i] = whole
                to_left(i).start()

            prefix_state_ref[i] = whole
            mixed_ref[rows, vals] = jnp.where(
                inside, nt(q_ref[rows, keys], whole), mixed_ref[rows, vals]
            )
        return carry

    lax.fori_loop(0, seqs, prefix_of, 0)

    def finish(i, carry):
        @pl.when(place < count - 1)
        def _():
            to_right(i).wait_send()

        @pl.when(place > 0)
        def _():
            to_left(i).wait_send()

        return carry

    lax.fori_loop(0, seqs * HEADS, finish, 0)


def backward_kernel(
    axes,
    prefix_ref,
    q_ref,
    k_ref,
    v_ref,
    cum_ref,
    state_ref,
    prefix_state_ref,
    grad_ref,
    dq_ref,
    dk_ref,
    dv_ref,
    ddecay_ref,
    local_ref,
    acc_ref,
    dk_part,
    dv_part,
    dcum_part,
    right_out,
    right_in,
    left_out,
    left_in,
    right_sent,
    right_got,
    left_sent,
    left_got,
):
    count = line_length(axes)
    place = place_on(axes)
    seqs = prefix_ref.shape[0]
    toks = q_ref.shape[0] // seqs
    chunks = toks // CHUNK
    greet(axes, place, count)
    causal = iota((CHUNK, CHUNK), 0) >= iota((CHUNK, CHUNK), 1)
    upper = low(jnp.where(iota((toks, toks), 0) <= iota((toks, toks), 1), 1.0, 0.0))

    def to_right(i):
        return send(right_out.at[i], right_in.at[i], right_sent.at[i], right_got.at[i], axes, place + 1)

    def to_left(i):
        return send(left_out.at[i], left_in.at[i], left_sent.at[i], left_got.at[i], axes, place - 1)

    def shares_of(seq, carry):
        rows = pl.ds(pl.multiple_of(seq * toks, toks), toks)
        end_local = prefix_ref[seq] - 1 - place * toks
        inside = iota((toks, HEAD_V), 0) <= end_local
        for head in range(HEADS):
            i = seq * HEADS + head
            keys = slice(head * HEAD_K, (head + 1) * HEAD_K)
            vals = slice(head * HEAD_V, (head + 1) * HEAD_V)
            cum = cum_ref[rows, keys]
            query = q_ref[rows, keys]
            grad = grad_ref[rows, vals]
            share = tn(low(jnp.where(inside, grad, 0.0)), query)
            acc_ref[i] = share

            @pl.when(place == 0)
            def _():
                right_out[i] = low(share)
                if count > 1:
                    to_right(i).start()

            later = low(jnp.where(inside, 0.0, grad))
            for chunk in range(chunks):
                at = slice(chunk * CHUNK, (chunk + 1) * CHUNK)
                piece, total, middle = chunk_parts(cum, chunk)
                local_ref[i, chunk] = tn(later[at], low(wide(query[at]) * jnp.exp(piece)))
        return carry

    lax.fori_loop(0, seqs, shares_of, 0)

    def local_of(seq, carry):
        rows = pl.ds(pl.multiple_of(seq * toks, toks), toks)
        end_local = prefix_ref[seq] - 1 - place * toks
        inside = iota((toks, HEAD_V), 0) <= end_local
        inside_keys = iota((toks, HEAD_K), 0) <= end_local
        at_end = iota((toks, HEAD_K), 0) == end_local
        for head in range(HEADS):
            i = seq * HEADS + head
            keys = slice(head * HEAD_K, (head + 1) * HEAD_K)
            vals = slice(head * HEAD_V, (head + 1) * HEAD_V)
            cum = cum_ref[rows, keys]
            query = wide(q_ref[rows, keys])
            key = wide(k_ref[rows, keys])
            value = v_ref[rows, vals]
            grad = grad_ref[rows, vals]
            later = low(jnp.where(inside, 0.0, grad))
            weights, edge = prefix_weights(cum, end_local, toks)
            prefix_state = prefix_state_ref[i]

            @pl.when(place == 0)
            def _():
                right_in[i] = jnp.zeros((HEAD_V, HEAD_K), jnp.bfloat16)

            @pl.when(place > 0)
            def _():
                send(right_out.at[i], right_in.at[i], right_sent.at[i], right_got.at[i], axes, place - 1).wait_recv()

            acc = acc_ref[i] + wide(right_in[i])
            narrow_acc = low(acc)

            @pl.when(jnp.logical_and(place > 0, place < count - 1))
            def _():
                right_out[i] = narrow_acc
                to_right(i).start()

            local = jnp.zeros((HEAD_V, HEAD_K), jnp.float32)
            starts = []
            for chunk in reversed(range(chunks)):
                piece, total, middle = chunk_parts(cum, chunk)
                starts.append(local)
                local = jnp.exp(total) * local + local_ref[i, chunk]
            starts = starts[::-1]
            local = local + edge * acc
            acc_ref[i] = local
            if count > 1:

                @pl.when(place == count - 1)
                def _():
                    left_out[i] = low(local)
                    to_left(i).start()

            weighted = low(key * weights)
            dk_all = weights * nn(value, narrow_acc)
            dv_all = nt(weighted, narrow_acc)
            dq_all = nn(low(jnp.where(inside, grad, 0.0)), prefix_state)
            dqs, dks, dvs, dcs = [], [], [], []
            for chunk in range(chunks):
                at = slice(chunk * CHUNK, (chunk + 1) * CHUNK)
                piece, total, middle = chunk_parts(cum, chunk)
                rise = jnp.exp(piece - middle)
                fall = jnp.exp(middle - piece)
                q_in = low(query[at] * rise)
                k_in = low(key[at] * fall)
                scores = low(jnp.where(causal, nt(q_in, k_in), 0.0))
                d_scores = low(jnp.where(causal, nt(later[at], value[at]), 0.0))
                dq_in = nn(d_scores, k_in)
                dk_in = tn(d_scores, q_in)
                dq_state = jnp.exp(piece) * nn(later[at], state_ref[i, chunk])
                to_end = jnp.exp(total - piece)
                after = low(starts[chunk])
                dk_state = to_end * nn(value[at], after) + dk_all[at]
                dv = tn(scores, later[at]) + dv_all[at]
                if chunk < chunks - 1:
                    dv = dv + nt(low(key[at] * to_end), after)
                dqs.append(rise * dq_in + dq_state + dq_all[at])
                dks.append(fall * dk_in + dk_state)
                dvs.append(dv)
                dcs.append(
                    wide(q_in) * dq_in
                    - wide(k_in) * dk_in
                    + query[at] * dq_state
                    - key[at] * dk_state
                )
            dq_ref[rows, keys] = low(jnp.concatenate(dqs, axis=0))
            dk_part[rows, keys] = jnp.concatenate(dks, axis=0)
            dv_part[rows, vals] = jnp.concatenate(dvs, axis=0)
            turn = jnp.sum(wide(narrow_acc) * wide(prefix_state), axis=0, keepdims=True)
            dcum_part[rows, keys] = jnp.concatenate(dcs, axis=0) + jnp.where(at_end, turn, 0.0)
        return carry

    lax.fori_loop(0, seqs, local_of, 0)

    def rest_of(seq, carry):
        rows = pl.ds(pl.multiple_of(seq * toks, toks), toks)
        for head in range(HEADS):
            i = seq * HEADS + head
            keys = slice(head * HEAD_K, (head + 1) * HEAD_K)
            vals = slice(head * HEAD_V, (head + 1) * HEAD_V)
            cum = cum_ref[rows, keys]
            key = wide(k_ref[rows, keys])
            value = v_ref[rows, vals]

            @pl.when(place < count - 1)
            def _():
                send(left_out.at[i], left_in.at[i], left_sent.at[i], left_got.at[i], axes, place + 1).wait_recv()

            @pl.when(place == count - 1)
            def _():
                left_in[i] = jnp.zeros((HEAD_V, HEAD_K), jnp.bfloat16)

            after = left_in[i]
            last = cum[toks - 1 :]

            @pl.when(jnp.logical_and(place > 0, place < count - 1))
            def _():
                left_out[i] = low(jnp.exp(last) * wide(after) + acc_ref[i])
                to_left(i).start()

            to_end = jnp.exp(last - cum)
            dk_more = to_end * nn(value, after)
            dk_ref[rows, keys] = low(dk_part[rows, keys] + dk_more)
            dv_ref[rows, vals] = low(dv_part[rows, vals] + nt(low(key * to_end), after))
            carry_row = jnp.sum(wide(after) * wide(state_ref[i, chunks]), axis=0, keepdims=True)
            dcum = dcum_part[rows, keys] - key * dk_more
            ddecay_ref[rows, keys] = three_way(upper, dcum) + carry_row
        return carry

    lax.fori_loop(0, seqs, rest_of, 0)

    def finish(i, carry):
        @pl.when(place < count - 1)
        def _():
            to_right(i).wait_send()

        @pl.when(place > 0)
        def _():
            to_left(i).wait_send()

        return carry

    lax.fori_loop(0, seqs * HEADS, finish, 0)


def line_scratch(pieces):
    block = pltpu.VMEM((pieces, HEAD_V, HEAD_K), jnp.bfloat16)
    return [block] * 4 + [pltpu.SemaphoreType.DMA((pieces,))] * 4


def whole_specs(count):
    return [pl.BlockSpec(memory_space=pltpu.VMEM)] * count


def mix_forward(axes, prefix_len, queries, keys, values, decays):
    tokens = queries.shape[0]
    seqs = prefix_len.shape[0]
    pieces = seqs * HEADS
    chunks = tokens // seqs // CHUNK
    state = (pieces, HEAD_V, HEAD_K)
    return pl.pallas_call(
        partial(forward_kernel, axes),
        out_shape=(
            jax.ShapeDtypeStruct((tokens, VALS), jnp.float32),
            jax.ShapeDtypeStruct((tokens, KEYS), jnp.float32),
            jax.ShapeDtypeStruct((pieces, chunks + 1, HEAD_V, HEAD_K), jnp.bfloat16),
            jax.ShapeDtypeStruct(state, jnp.bfloat16),
        ),
        in_specs=[pl.BlockSpec(memory_space=pltpu.SMEM)] + whole_specs(4),
        out_specs=tuple(whole_specs(4)),
        scratch_shapes=[
            pltpu.VMEM((pieces, chunks, HEAD_V, HEAD_K), jnp.float32),
            pltpu.VMEM(state, jnp.float32),
            pltpu.VMEM((pieces, 8, HEAD_K), jnp.float32),
            *line_scratch(pieces),
        ],
        compiler_params=pltpu.CompilerParams(
            collective_id=1, has_side_effects=True, vmem_limit_bytes=50 * 2**20
        ),
        name="mix_forward",
    )(prefix_len, queries, keys, values, decays)


def mix_backward(axes, prefix_len, queries, keys, values, cum, states, prefix_state, grad_mixed):
    tokens = queries.shape[0]
    seqs = prefix_len.shape[0]
    pieces = seqs * HEADS
    chunks = tokens // seqs // CHUNK
    state = (pieces, HEAD_V, HEAD_K)
    return pl.pallas_call(
        partial(backward_kernel, axes),
        out_shape=(
            jax.ShapeDtypeStruct((tokens, KEYS), jnp.bfloat16),
            jax.ShapeDtypeStruct((tokens, KEYS), jnp.bfloat16),
            jax.ShapeDtypeStruct((tokens, VALS), jnp.bfloat16),
            jax.ShapeDtypeStruct((tokens, KEYS), jnp.float32),
        ),
        in_specs=[pl.BlockSpec(memory_space=pltpu.SMEM)] + whole_specs(7),
        out_specs=tuple(whole_specs(4)),
        scratch_shapes=[
            pltpu.VMEM((pieces, chunks, HEAD_V, HEAD_K), jnp.float32),
            pltpu.VMEM(state, jnp.float32),
            pltpu.VMEM((tokens, KEYS), jnp.float32),
            pltpu.VMEM((tokens, VALS), jnp.float32),
            pltpu.VMEM((tokens, KEYS), jnp.float32),
            *line_scratch(pieces),
        ],
        compiler_params=pltpu.CompilerParams(
            collective_id=2, has_side_effects=True, vmem_limit_bytes=56 * 2**20
        ),
        name="mix_backward",
    )(prefix_len, queries, keys, values, cum, states, prefix_state, grad_mixed)


EXTRA = 128


def physical_axes(mesh):
    shape = mesh.devices.shape
    names = []
    sizes = []
    for axis, extent in enumerate(shape):
        line = np.moveaxis(mesh.devices, axis, 0).reshape(extent, -1)[:, 0]
        places = [tuple(d.coords) + (d.core_on_chip,) for d in line]
        parts = []
        for dim, label in enumerate(("x", "y", "z", "core")):
            values = [p[dim] for p in places]
            if len(set(values)) > 1:
                step = next(i for i in range(extent) if values[i] != values[0])
                parts.append((step, label, len(set(values))))
        for step, label, size in sorted(parts, reverse=True):
            names.append(label)
            sizes.append(size)
    return tuple(names), tuple(sizes)


def pack_mixer(norm1_gain, norm2_gain, query, key, value, gate, down, up, bias, group, out):
    rows = query.shape[0]
    small = jnp.zeros((rows, EXTRA), query.dtype)
    small = small.at[:, :16].set(down)
    small = small.at[:, 16].set(norm1_gain)
    small = small.at[:, 17].set(norm2_gain)
    small = small.at[: bias.shape[0], 18].set(bias)
    small = small.at[: group.shape[0], 19].set(group)
    small = small.at[:, 24:32].set(up.T.reshape(rows, 8))
    return jnp.concatenate([query, key, value, gate, out, small], axis=1)


def unpack_small(small, devices):
    rows = small.shape[0] // devices
    by_device = small.reshape(devices, rows, EXTRA)
    down = small[:, :16]
    gain_one = small[:, 16]
    gain_two = small[:, 17]
    bias = by_device[:, : KEYS // devices, 18].reshape(KEYS)
    group = by_device[:, : HEAD_V // devices, 19].reshape(HEAD_V)
    up = small[:, 24:32].reshape(KEYS, 16).T
    return down, gain_one, gain_two, bias, group, up


def pack_small_grads(down, gain_one, gain_two, bias, group, up, devices):
    rows = gain_one.shape[0] // devices

    def column(vector):
        parts = vector.reshape(devices, -1)
        parts = jnp.pad(parts, ((0, 0), (0, rows - parts.shape[1])))
        return parts.reshape(devices * rows, 1)

    pieces = [
        down,
        gain_one[:, None],
        gain_two[:, None],
        column(bias),
        column(group),
        jnp.zeros((rows * devices, 4), jnp.float32),
        up.T.reshape(rows * devices, 8),
        jnp.zeros((rows * devices, EXTRA - 32), jnp.float32),
    ]
    return jnp.concatenate(pieces, axis=1)


def reduce_to_owner(total, names, sizes):
    rows = total.shape[0]
    width = total.shape[1]
    devices = int(np.prod(sizes))
    if "core" in names:
        at = names.index("core")
        before = int(np.prod(sizes[:at], initial=1))
        after = rows // before // sizes[at]
        shaped = total.reshape(before, sizes[at], after, width)
        core = lax.axis_index("core")
        kept = lax.dynamic_index_in_dim(shaped, core, 1, False)
        given = lax.dynamic_index_in_dim(shaped, 1 - core, 1, False)
        taken = lax.ppermute(given, "core", [(0, 1), (1, 0)])
        total = (kept + taken).reshape(rows // sizes[at], width)
    rest = tuple(n for n in names if n != "core")
    return lax.psum_scatter(total, rest, scatter_dimension=0, tiled=True)


def local(
    names,
    sizes,
    seq_axes,
    tokens,
    prefix_len,
    norm1_gain,
    query_weight,
    key_weight,
    value_weight,
    gate_weight,
    decay_down,
    decay_up,
    decay_bias,
    group_gain,
    out_weight,
    norm2_gain,
    ffn_gate,
    ffn_up,
    ffn_down,
    out_grad,
):
    devices = int(np.prod(sizes))
    mixer_full = lax.all_gather(
        pack_mixer(
            norm1_gain,
            norm2_gain,
            query_weight,
            key_weight,
            value_weight,
            gate_weight,
            decay_down,
            decay_up,
            decay_bias,
            group_gain,
            out_weight,
        ),
        names,
        axis=0,
        tiled=True,
    )
    ffn_full = lax.all_gather(
        jnp.concatenate([ffn_gate, ffn_up, ffn_down.T], axis=1), names, axis=0, tiled=True
    )
    weight_q = mixer_full[:, :512]
    weight_k = mixer_full[:, 512:1024]
    weight_v = mixer_full[:, 1024:2048]
    weight_g = mixer_full[:, 2048:3072]
    weight_o = mixer_full[:, 3072:4096]
    weight_down, gain_one, gain_two, bias_full, gain_group, weight_up = unpack_small(
        mixer_full[:, 4096:], devices
    )
    weight_gate = ffn_full[:, :FF]
    weight_upper = ffn_full[:, FF : 2 * FF]
    weight_lower = ffn_full[:, 2 * FF :].T
    seq_count, tok_count, feature_count = tokens.shape
    resid_in = tokens.astype(jnp.float32)
    scale_one = rms_scale(resid_in)
    unit_one = resid_in * scale_one
    normed = (unit_one * gain_one.astype(jnp.float32)).astype(jnp.bfloat16)
    queries = project(normed, weight_q).astype(jnp.bfloat16)
    key_matrix = project(normed, weight_k).astype(jnp.bfloat16)
    value_matrix = project(normed, weight_v).astype(jnp.bfloat16)
    gate_out = project(normed, weight_g)
    lowrank = project(normed, weight_down).astype(jnp.bfloat16)
    logits = project(lowrank, weight_up) + bias_full.astype(jnp.float32)
    decays = jax.nn.log_sigmoid(logits) / 16.0
    rows = seq_count * tok_count
    flat_q = queries.reshape(rows, KEYS)
    flat_k = key_matrix.reshape(rows, KEYS)
    flat_v = value_matrix.reshape(rows, VALS)
    mixed, cum, states, prefix_state = mix_forward(
        seq_axes, prefix_len, flat_q, flat_k, flat_v, decays.reshape(rows, KEYS)
    )
    mixed_heads = mixed.reshape(seq_count, tok_count, HEADS, HEAD_V)
    scale_group = rms_scale(mixed_heads)
    unit_group = mixed_heads * scale_group
    normed_group = unit_group * gain_group.astype(jnp.float32)
    swish_gate = jax.nn.silu(gate_out).reshape(seq_count, tok_count, HEADS, HEAD_V)
    gated_rows = (
        (normed_group * swish_gate).reshape(seq_count, tok_count, VALS).astype(jnp.bfloat16)
    )
    branch = project(gated_rows, weight_o)
    resid_mid = resid_in + branch
    scale_two = rms_scale(resid_mid)
    unit_two = resid_mid * scale_two
    normed_two = (unit_two * gain_two.astype(jnp.float32)).astype(jnp.bfloat16)
    gate_part = project(normed_two, weight_gate)
    up_part = project(normed_two, weight_upper)
    gate_act = jax.nn.silu(gate_part)
    hidden = (gate_act * up_part).astype(jnp.bfloat16)
    ffn_out = project(hidden, weight_lower)
    layer_out = (resid_mid + ffn_out).astype(jnp.bfloat16)
    grad_out = out_grad.astype(jnp.float32)
    grad_hidden = back_project(out_grad, weight_lower)
    lower_grad = weight_grad(out_grad, hidden)
    grad_gate = (grad_hidden * up_part * silu_slope(gate_part)).astype(jnp.bfloat16)
    grad_up = (grad_hidden * gate_act).astype(jnp.bfloat16)
    gate_w_grad = weight_grad(normed_two, grad_gate)
    up_w_grad = weight_grad(normed_two, grad_up)
    grad_normed_two = back_project(grad_gate, weight_gate) + back_project(grad_up, weight_upper)
    gain_two_grad = jnp.sum(grad_normed_two * unit_two, axis=(0, 1))
    grad_mid = grad_out + rms_back(
        grad_normed_two * gain_two.astype(jnp.float32), unit_two, scale_two
    )
    ffn_mine = reduce_to_owner(
        jnp.concatenate([gate_w_grad, up_w_grad, lower_grad], axis=1).astype(jnp.bfloat16),
        names,
        sizes,
    ).astype(jnp.float32)
    grad_branch = grad_mid.astype(jnp.bfloat16)
    out_w_grad = weight_grad(gated_rows, grad_branch)
    grad_gated = back_project(grad_branch, weight_o).reshape(seq_count, tok_count, HEADS, HEAD_V)
    grad_normed_group = grad_gated * swish_gate
    grad_swish = (grad_gated * normed_group).reshape(seq_count, tok_count, VALS)
    grad_gate_out = (grad_swish * silu_slope(gate_out)).astype(jnp.bfloat16)
    group_grad = jnp.sum(grad_normed_group * unit_group, axis=(0, 1, 2))
    grad_mixed = rms_back(
        grad_normed_group * gain_group.astype(jnp.float32), unit_group, scale_group
    )
    grad_q, grad_k, grad_v, grad_decay = mix_backward(
        seq_axes,
        prefix_len,
        flat_q,
        flat_k,
        flat_v,
        cum,
        states,
        prefix_state,
        grad_mixed.reshape(rows, VALS),
    )
    grad_q = grad_q.reshape(seq_count, tok_count, KEYS)
    grad_k = grad_k.reshape(seq_count, tok_count, KEYS)
    grad_v = grad_v.reshape(seq_count, tok_count, VALS)
    grad_logits = (
        grad_decay.reshape(seq_count, tok_count, KEYS) * jax.nn.sigmoid(-logits) / 16.0
    ).astype(jnp.bfloat16)
    bias_grad = jnp.sum(grad_logits.astype(jnp.float32), axis=(0, 1))
    up_rank_grad = weight_grad(lowrank, grad_logits)
    grad_lowrank = back_project(grad_logits, weight_up).astype(jnp.bfloat16)
    down_rank_grad = weight_grad(normed, grad_lowrank)
    grad_normed = (
        back_project(grad_q, weight_q)
        + back_project(grad_k, weight_k)
        + back_project(grad_v, weight_v)
        + back_project(grad_gate_out, weight_g)
        + back_project(grad_lowrank, weight_down)
    )
    gain_one_grad = jnp.sum(grad_normed * unit_one, axis=(0, 1))
    tokens_grad = grad_mid + rms_back(
        grad_normed * gain_one.astype(jnp.float32), unit_one, scale_one
    )
    small_grads = pack_small_grads(
        down_rank_grad, gain_one_grad, gain_two_grad, bias_grad, group_grad, up_rank_grad, devices
    )
    mine = reduce_to_owner(
        jnp.concatenate(
            [
                weight_grad(normed, grad_q),
                weight_grad(normed, grad_k),
                weight_grad(normed, grad_v),
                weight_grad(normed, grad_gate_out),
                out_w_grad,
                small_grads,
            ],
            axis=1,
        ).astype(jnp.bfloat16),
        names,
        sizes,
    ).astype(jnp.float32)
    small = mine[:, 4096:]
    return (
        layer_out,
        tokens_grad,
        small[:, 16],
        mine[:, :512],
        mine[:, 512:1024],
        mine[:, 1024:2048],
        mine[:, 2048:3072],
        small[:, :16],
        small[:, 24:32].reshape(KEYS // devices, 16).T,
        small[: KEYS // devices, 18],
        small[: HEAD_V // devices, 19],
        mine[:, 3072:4096],
        small[:, 17],
        ffn_mine[:, :FF],
        ffn_mine[:, FF : 2 * FF],
        ffn_mine[:, 2 * FF :].T,
    )


def solution(mesh):
    names, sizes = physical_axes(mesh)
    cut = next(
        i for i in range(len(sizes) + 1) if np.prod(sizes[:i], initial=1) == mesh.shape["dp"]
    )
    dp, seq = names[:cut], names[cut:]
    split = Mesh(mesh.devices.reshape(sizes), names)
    return jax.shard_map(
        partial(local, names, sizes, tuple(zip(seq, sizes[cut:]))),
        mesh=split,
        in_specs=(
            P(dp, seq, None),
            P(dp),
            P(names),
            P(names, None),
            P(names, None),
            P(names, None),
            P(names, None),
            P(names, None),
            P(None, names),
            P(names),
            P(names),
            P(names, None),
            P(names),
            P(names, None),
            P(names, None),
            P(None, names),
            P(dp, seq, None),
        ),
        out_specs=(
            P(dp, seq, None),
            P(dp, seq, None),
            P(names),
            P(names, None),
            P(names, None),
            P(names, None),
            P(names, None),
            P(names, None),
            P(None, names),
            P(names),
            P(names),
            P(names, None),
            P(names),
            P(names, None),
            P(names, None),
            P(None, names),
        ),
        check_vma=False,
    )
```

```python
from functools import partial

import jax
import jax.numpy as jnp
import numpy as np
from jax import lax
from jax.experimental import pallas as pl
from jax.experimental.pallas import tpu as pltpu
from jax.sharding import Mesh
from jax.sharding import PartitionSpec as P

KEYS = 512
VALS = 1024
HEADS = 4
SPAN = 64
HEAD_K = 128
HEAD_V = 256
FF = 2816


norm_eps = 1e-05


def project(inputs, weight):
    return jnp.einsum("std,de->ste", inputs, weight, preferred_element_type=jnp.float32)


def back_project(gradient, weight):
    return jnp.einsum("ste,de->std", gradient, weight, preferred_element_type=jnp.float32)


def weight_grad(inputs, gradient):
    return jnp.einsum("std,ste->de", inputs, gradient, preferred_element_type=jnp.float32)


def rms_scale(values):
    return lax.rsqrt(jnp.mean(values * values, axis=-1, keepdims=True) + norm_eps)


def rms_back(grad_unit, unit_rows, scale_rows):
    return scale_rows * (
        grad_unit - unit_rows * jnp.mean(grad_unit * unit_rows, axis=-1, keepdims=True)
    )


def silu_slope(values):
    logistic = jax.nn.sigmoid(values)
    return logistic * (1.0 + values * (1.0 - logistic))


CHUNK = 128
MESH = pl.DeviceIdType.MESH


def nn(a, b):
    return lax.dot_general(a, b, (((1,), (0,)), ((), ())), preferred_element_type=jnp.float32)


def nt(a, b):
    return lax.dot_general(a, b, (((1,), (1,)), ((), ())), preferred_element_type=jnp.float32)


def tn(a, b):
    return lax.dot_general(a, b, (((0,), (0,)), ((), ())), preferred_element_type=jnp.float32)


def low(values):
    return values.astype(jnp.bfloat16)


def wide(values):
    return values.astype(jnp.float32)


def three_way(ones, values):
    first = low(values)
    left = values - wide(first)
    second = low(left)
    third = low(left - wide(second))
    return nn(ones, first) + nn(ones, second) + nn(ones, third)


def iota(shape, dim):
    return lax.broadcasted_iota(jnp.int32, shape, dim)


def place_on(axes):
    place = 0
    for name, size in axes:
        place = place * size + lax.axis_index(name)
    return place


def device_at(axes, place):
    where = {}
    for name, size in reversed(axes):
        where[name] = lax.rem(place, size)
        place = lax.div(place, size)
    return where


def line_length(axes):
    return int(np.prod([size for _, size in axes]))


def greet(axes, place, count):
    barrier = pltpu.get_barrier_semaphore()

    @pl.when(place > 0)
    def _():
        pl.semaphore_signal(
            barrier, inc=1, device_id=device_at(axes, place - 1), device_id_type=MESH
        )

    @pl.when(place < count - 1)
    def _():
        pl.semaphore_signal(
            barrier, inc=1, device_id=device_at(axes, place + 1), device_id_type=MESH
        )

    @pl.when(jnp.logical_or(place == 0, place == count - 1))
    def _():
        pl.semaphore_wait(barrier, 1)

    @pl.when(jnp.logical_and(place > 0, place < count - 1))
    def _():
        pl.semaphore_wait(barrier, 2)


def send(source, target, send_sem, recv_sem, axes, place):
    return pltpu.make_async_remote_copy(
        src_ref=source,
        dst_ref=target,
        send_sem=send_sem,
        recv_sem=recv_sem,
        device_id=device_at(axes, place),
        device_id_type=MESH,
    )


def row_places(count):
    return iota((count, HEAD_K), 0)


def prefix_weights(cum, end_local, count):
    rows = row_places(count)
    owner = jnp.logical_and(end_local >= 0, end_local < count)
    end_cum = jnp.sum(jnp.where(rows == end_local, cum, 0.0), axis=0, keepdims=True)
    keep = jnp.logical_and(rows <= end_local, rows <= jnp.where(owner, count, -1))
    weights = jnp.where(keep, jnp.exp(jnp.where(keep, end_cum - cum, 0.0)), 0.0)
    return weights, jnp.exp(end_cum) * jnp.where(owner, 1.0, 0.0)


def chunk_parts(cum, chunk):
    begin = chunk * CHUNK
    piece = cum[begin : begin + CHUNK]
    if chunk:
        piece = piece - cum[begin - 1 : begin]
    return piece, piece[CHUNK - 1 :], piece[CHUNK // 2 - 1 : CHUNK // 2]


def forward_kernel(
    axes,
    prefix_ref,
    q_ref,
    k_ref,
    v_ref,
    decay_ref,
    mixed_ref,
    cum_ref,
    state_ref,
    prefix_state_ref,
    kv_ref,
    part_ref,
    edge_ref,
    right_out,
    right_in,
    left_out,
    left_in,
    right_sent,
    right_got,
    left_sent,
    left_got,
):
    count = line_length(axes)
    place = place_on(axes)
    seqs = prefix_ref.shape[0]
    toks = q_ref.shape[0] // seqs
    chunks = toks // CHUNK
    greet(axes, place, count)
    lower = low(jnp.where(iota((CHUNK, CHUNK), 0) >= iota((CHUNK, CHUNK), 1), 1.0, 0.0))
    causal = iota((CHUNK, CHUNK), 0) >= iota((CHUNK, CHUNK), 1)

    def to_right(i):
        return send(right_out.at[i], right_in.at[i], right_sent.at[i], right_got.at[i], axes, place + 1)

    def to_left(i):
        return send(left_out.at[i], left_in.at[i], left_sent.at[i], left_got.at[i], axes, place - 1)

    def states_of(seq, carry):
        rows = pl.ds(pl.multiple_of(seq * toks, toks), toks)
        end_local = prefix_ref[seq] - 1 - place * toks
        for head in range(HEADS):
            i = seq * HEADS + head
            keys = slice(head * HEAD_K, (head + 1) * HEAD_K)
            vals = slice(head * HEAD_V, (head + 1) * HEAD_V)
            before = jnp.zeros((1, HEAD_K), jnp.float32)
            key = wide(k_ref[rows, keys])
            value = v_ref[rows, vals]
            decay = decay_ref[rows, keys]
            pieces = []
            local = jnp.zeros((HEAD_V, HEAD_K), jnp.float32)
            for chunk in range(chunks):
                at = slice(chunk * CHUNK, (chunk + 1) * CHUNK)
                piece = three_way(lower, decay[at])
                total = piece[CHUNK - 1 :]
                share = tn(value[at], low(key[at] * jnp.exp(total - piece)))
                kv_ref[i, chunk] = share
                local = jnp.exp(total) * local + share
                pieces.append(piece + before)
                before = before + total
            cum = jnp.concatenate(pieces, axis=0)
            cum_ref[rows, keys] = cum
            weights, edge = prefix_weights(cum, end_local, toks)
            part_ref[i] = tn(value, low(key * weights))
            edge_ref[i] = jnp.broadcast_to(edge, (8, HEAD_K))

            @pl.when(place == 0)
            def _():
                right_out[i] = low(local)
                if count > 1:
                    to_right(i).start()

        return carry

    lax.fori_loop(0, seqs, states_of, 0)

    def outputs_of(seq, carry):
        rows = pl.ds(pl.multiple_of(seq * toks, toks), toks)
        for head in range(HEADS):
            i = seq * HEADS + head
            keys = slice(head * HEAD_K, (head + 1) * HEAD_K)
            vals = slice(head * HEAD_V, (head + 1) * HEAD_V)
            cum = cum_ref[rows, keys]
            query = wide(q_ref[rows, keys])
            key = wide(k_ref[rows, keys])
            value = v_ref[rows, vals]
            scores = []
            for chunk in range(chunks):
                at = slice(chunk * CHUNK, (chunk + 1) * CHUNK)
                piece, total, middle = chunk_parts(cum, chunk)
                raw = nt(
                    low(query[at] * jnp.exp(piece - middle)), low(key[at] * jnp.exp(middle - piece))
                )
                scores.append(low(jnp.where(causal, raw, 0.0)))

            @pl.when(place == 0)
            def _():
                right_in[i] = jnp.zeros((HEAD_V, HEAD_K), jnp.bfloat16)

            @pl.when(place > 0)
            def _():
                send(right_out.at[i], right_in.at[i], right_sent.at[i], right_got.at[i], axes, place - 1).wait_recv()

            state = wide(right_in[i])
            part = part_ref[i] + edge_ref[i][:1] * state
            part_ref[i] = part
            for chunk in range(chunks):
                at = slice(chunk * CHUNK, (chunk + 1) * CHUNK)
                piece, total, middle = chunk_parts(cum, chunk)
                narrow = low(state)
                state_ref[i, chunk] = narrow
                output = nn(scores[chunk], value[at]) + nt(
                    low(query[at] * jnp.exp(piece)), narrow
                )
                mixed_ref[pl.ds(seq * toks + chunk * CHUNK, CHUNK), vals] = output
                state = jnp.exp(total) * state + kv_ref[i, chunk]
            state_ref[i, chunks] = low(state)

            @pl.when(jnp.logical_and(place > 0, place < count - 1))
            def _():
                right_out[i] = low(state)
                to_right(i).start()

            if count > 1:

                @pl.when(place == count - 1)
                def _():
                    left_out[i] = low(part)
                    to_left(i).start()

        return carry

    lax.fori_loop(0, seqs, outputs_of, 0)

    def prefix_of(seq, carry):
        rows = pl.ds(pl.multiple_of(seq * toks, toks), toks)
        end_local = prefix_ref[seq] - 1 - place * toks
        inside = iota((toks, HEAD_V), 0) <= end_local
        for head in range(HEADS):
            i = seq * HEADS + head
            keys = slice(head * HEAD_K, (head + 1) * HEAD_K)
            vals = slice(head * HEAD_V, (head + 1) * HEAD_V)

            @pl.when(place < count - 1)
            def _():
                send(left_out.at[i], left_in.at[i], left_sent.at[i], left_got.at[i], axes, place + 1).wait_recv()

            @pl.when(place == count - 1)
            def _():
                left_in[i] = jnp.zeros((HEAD_V, HEAD_K), jnp.bfloat16)

            whole = low(part_ref[i] + wide(left_in[i]))

            @pl.when(jnp.logical_and(place > 0, place < count - 1))
            def _():
                left_out[i] = whole
                to_left(i).start()

            prefix_state_ref[i] = whole
            mixed_ref[rows, vals] = jnp.where(
                inside, nt(q_ref[rows, keys], whole), mixed_ref[rows, vals]
            )
        return carry

    lax.fori_loop(0, seqs, prefix_of, 0)

    def finish(i, carry):
        @pl.when(place < count - 1)
        def _():
            to_right(i).wait_send()

        @pl.when(place > 0)
        def _():
            to_left(i).wait_send()

        return carry

    lax.fori_loop(0, seqs * HEADS, finish, 0)


def backward_kernel(
    axes,
    prefix_ref,
    q_ref,
    k_ref,
    v_ref,
    cum_ref,
    state_ref,
    prefix_state_ref,
    grad_ref,
    dqkv_ref,
    ddecay_ref,
    local_ref,
    acc_ref,
    dk_part,
    dv_part,
    dcum_part,
    right_out,
    right_in,
    left_out,
    left_in,
    right_sent,
    right_got,
    left_sent,
    left_got,
):
    count = line_length(axes)
    place = place_on(axes)
    seqs = prefix_ref.shape[0]
    toks = q_ref.shape[0] // seqs
    chunks = toks // CHUNK
    greet(axes, place, count)
    causal = iota((CHUNK, CHUNK), 0) >= iota((CHUNK, CHUNK), 1)
    upper = low(jnp.where(iota((toks, toks), 0) <= iota((toks, toks), 1), 1.0, 0.0))

    def to_right(i):
        return send(right_out.at[i], right_in.at[i], right_sent.at[i], right_got.at[i], axes, place + 1)

    def to_left(i):
        return send(left_out.at[i], left_in.at[i], left_sent.at[i], left_got.at[i], axes, place - 1)

    def shares_of(seq, carry):
        rows = pl.ds(pl.multiple_of(seq * toks, toks), toks)
        end_local = prefix_ref[seq] - 1 - place * toks
        inside = iota((toks, HEAD_V), 0) <= end_local
        for head in range(HEADS):
            i = seq * HEADS + head
            keys = slice(head * HEAD_K, (head + 1) * HEAD_K)
            vals = slice(head * HEAD_V, (head + 1) * HEAD_V)
            cum = cum_ref[rows, keys]
            query = q_ref[rows, keys]
            grad = grad_ref[rows, vals]
            share = tn(low(jnp.where(inside, grad, 0.0)), query)
            acc_ref[i] = share

            @pl.when(place == 0)
            def _():
                right_out[i] = low(share)
                if count > 1:
                    to_right(i).start()

            later = low(jnp.where(inside, 0.0, grad))
            for chunk in range(chunks):
                at = slice(chunk * CHUNK, (chunk + 1) * CHUNK)
                piece, total, middle = chunk_parts(cum, chunk)
                local_ref[i, chunk] = tn(later[at], low(wide(query[at]) * jnp.exp(piece)))
        return carry

    lax.fori_loop(0, seqs, shares_of, 0)

    def local_of(seq, carry):
        rows = pl.ds(pl.multiple_of(seq * toks, toks), toks)
        end_local = prefix_ref[seq] - 1 - place * toks
        inside = iota((toks, HEAD_V), 0) <= end_local
        inside_keys = iota((toks, HEAD_K), 0) <= end_local
        at_end = iota((toks, HEAD_K), 0) == end_local
        for head in range(HEADS):
            i = seq * HEADS + head
            keys = slice(head * HEAD_K, (head + 1) * HEAD_K)
            vals = slice(head * HEAD_V, (head + 1) * HEAD_V)
            cum = cum_ref[rows, keys]
            query = wide(q_ref[rows, keys])
            key = wide(k_ref[rows, keys])
            value = v_ref[rows, vals]
            grad = grad_ref[rows, vals]
            later = low(jnp.where(inside, 0.0, grad))
            weights, edge = prefix_weights(cum, end_local, toks)
            prefix_state = prefix_state_ref[i]

            @pl.when(place == 0)
            def _():
                right_in[i] = jnp.zeros((HEAD_V, HEAD_K), jnp.bfloat16)

            @pl.when(place > 0)
            def _():
                send(right_out.at[i], right_in.at[i], right_sent.at[i], right_got.at[i], axes, place - 1).wait_recv()

            acc = acc_ref[i] + wide(right_in[i])
            narrow_acc = low(acc)

            @pl.when(jnp.logical_and(place > 0, place < count - 1))
            def _():
                right_out[i] = narrow_acc
                to_right(i).start()

            local = jnp.zeros((HEAD_V, HEAD_K), jnp.float32)
            starts = []
            for chunk in reversed(range(chunks)):
                piece, total, middle = chunk_parts(cum, chunk)
                starts.append(local)
                local = jnp.exp(total) * local + local_ref[i, chunk]
            starts = starts[::-1]
            local = local + edge * acc
            acc_ref[i] = local
            if count > 1:

                @pl.when(place == count - 1)
                def _():
                    left_out[i] = low(local)
                    to_left(i).start()

            weighted = low(key * weights)
            dk_all = weights * nn(value, narrow_acc)
            dv_all = nt(weighted, narrow_acc)
            dq_all = nn(low(jnp.where(inside, grad, 0.0)), prefix_state)
            dqs, dks, dvs, dcs = [], [], [], []
            for chunk in range(chunks):
                at = slice(chunk * CHUNK, (chunk + 1) * CHUNK)
                piece, total, middle = chunk_parts(cum, chunk)
                rise = jnp.exp(piece - middle)
                fall = jnp.exp(middle - piece)
                q_in = low(query[at] * rise)
                k_in = low(key[at] * fall)
                scores = low(jnp.where(causal, nt(q_in, k_in), 0.0))
                d_scores = low(jnp.where(causal, nt(later[at], value[at]), 0.0))
                dq_in = nn(d_scores, k_in)
                dk_in = tn(d_scores, q_in)
                dq_state = jnp.exp(piece) * nn(later[at], state_ref[i, chunk])
                to_end = jnp.exp(total - piece)
                after = low(starts[chunk])
                dk_state = to_end * nn(value[at], after) + dk_all[at]
                dv = tn(scores, later[at]) + dv_all[at]
                if chunk < chunks - 1:
                    dv = dv + nt(low(key[at] * to_end), after)
                dqs.append(rise * dq_in + dq_state + dq_all[at])
                dks.append(fall * dk_in + dk_state)
                dvs.append(dv)
                dcs.append(
                    wide(q_in) * dq_in
                    - wide(k_in) * dk_in
                    + query[at] * dq_state
                    - key[at] * dk_state
                )
            dqkv_ref[rows, keys] = low(jnp.concatenate(dqs, axis=0))
            dk_part[rows, keys] = jnp.concatenate(dks, axis=0)
            dv_part[rows, vals] = jnp.concatenate(dvs, axis=0)
            turn = jnp.sum(wide(narrow_acc) * wide(prefix_state), axis=0, keepdims=True)
            dcum_part[rows, keys] = jnp.concatenate(dcs, axis=0) + jnp.where(at_end, turn, 0.0)
        return carry

    lax.fori_loop(0, seqs, local_of, 0)

    def rest_of(seq, carry):
        rows = pl.ds(pl.multiple_of(seq * toks, toks), toks)
        for head in range(HEADS):
            i = seq * HEADS + head
            keys = slice(head * HEAD_K, (head + 1) * HEAD_K)
            vals = slice(head * HEAD_V, (head + 1) * HEAD_V)
            cum = cum_ref[rows, keys]
            key = wide(k_ref[rows, keys])
            value = v_ref[rows, vals]

            @pl.when(place < count - 1)
            def _():
                send(left_out.at[i], left_in.at[i], left_sent.at[i], left_got.at[i], axes, place + 1).wait_recv()

            @pl.when(place == count - 1)
            def _():
                left_in[i] = jnp.zeros((HEAD_V, HEAD_K), jnp.bfloat16)

            after = left_in[i]
            last = cum[toks - 1 :]

            @pl.when(jnp.logical_and(place > 0, place < count - 1))
            def _():
                left_out[i] = low(jnp.exp(last) * wide(after) + acc_ref[i])
                to_left(i).start()

            to_end = jnp.exp(last - cum)
            dk_more = to_end * nn(value, after)
            dqkv_ref[rows, slice(KEYS + keys.start, KEYS + keys.stop)] = low(
                dk_part[rows, keys] + dk_more
            )
            dqkv_ref[rows, slice(2 * KEYS + vals.start, 2 * KEYS + vals.stop)] = low(
                dv_part[rows, vals] + nt(low(key * to_end), after)
            )
            carry_row = jnp.sum(wide(after) * wide(state_ref[i, chunks]), axis=0, keepdims=True)
            dcum = dcum_part[rows, keys] - key * dk_more
            ddecay_ref[rows, keys] = three_way(upper, dcum) + carry_row
        return carry

    lax.fori_loop(0, seqs, rest_of, 0)

    def finish(i, carry):
        @pl.when(place < count - 1)
        def _():
            to_right(i).wait_send()

        @pl.when(place > 0)
        def _():
            to_left(i).wait_send()

        return carry

    lax.fori_loop(0, seqs * HEADS, finish, 0)


def line_scratch(pieces):
    block = pltpu.VMEM((pieces, HEAD_V, HEAD_K), jnp.bfloat16)
    return [block] * 4 + [pltpu.SemaphoreType.DMA((pieces,))] * 4


def whole_specs(count):
    return [pl.BlockSpec(memory_space=pltpu.VMEM)] * count


def mix_forward(axes, prefix_len, queries, keys, values, decays):
    tokens = queries.shape[0]
    seqs = prefix_len.shape[0]
    pieces = seqs * HEADS
    chunks = tokens // seqs // CHUNK
    state = (pieces, HEAD_V, HEAD_K)
    return pl.pallas_call(
        partial(forward_kernel, axes),
        out_shape=(
            jax.ShapeDtypeStruct((tokens, VALS), jnp.float32),
            jax.ShapeDtypeStruct((tokens, KEYS), jnp.float32),
            jax.ShapeDtypeStruct((pieces, chunks + 1, HEAD_V, HEAD_K), jnp.bfloat16),
            jax.ShapeDtypeStruct(state, jnp.bfloat16),
        ),
        in_specs=[pl.BlockSpec(memory_space=pltpu.SMEM)] + whole_specs(4),
        out_specs=tuple(whole_specs(4)),
        scratch_shapes=[
            pltpu.VMEM((pieces, chunks, HEAD_V, HEAD_K), jnp.float32),
            pltpu.VMEM(state, jnp.float32),
            pltpu.VMEM((pieces, 8, HEAD_K), jnp.float32),
            *line_scratch(pieces),
        ],
        compiler_params=pltpu.CompilerParams(
            collective_id=1, has_side_effects=True, vmem_limit_bytes=50 * 2**20
        ),
        cost_estimate=pl.CostEstimate(
            flops=60_000_000_000, bytes_accessed=220_000_000, transcendentals=0
        ),
        name="mix_forward",
    )(prefix_len, queries, keys, values, decays)


def mix_backward(axes, prefix_len, queries, keys, values, cum, states, prefix_state, grad_mixed):
    tokens = queries.shape[0]
    seqs = prefix_len.shape[0]
    pieces = seqs * HEADS
    chunks = tokens // seqs // CHUNK
    state = (pieces, HEAD_V, HEAD_K)
    return pl.pallas_call(
        partial(backward_kernel, axes),
        out_shape=(
            jax.ShapeDtypeStruct((tokens, 2 * KEYS + VALS), jnp.bfloat16),
            jax.ShapeDtypeStruct((tokens, KEYS), jnp.float32),
        ),
        in_specs=[pl.BlockSpec(memory_space=pltpu.SMEM)] + whole_specs(7),
        out_specs=tuple(whole_specs(2)),
        scratch_shapes=[
            pltpu.VMEM((pieces, chunks, HEAD_V, HEAD_K), jnp.float32),
            pltpu.VMEM(state, jnp.float32),
            pltpu.VMEM((tokens, KEYS), jnp.float32),
            pltpu.VMEM((tokens, VALS), jnp.float32),
            pltpu.VMEM((tokens, KEYS), jnp.float32),
            *line_scratch(pieces),
        ],
        compiler_params=pltpu.CompilerParams(
            collective_id=2, has_side_effects=True, vmem_limit_bytes=56 * 2**20
        ),
        cost_estimate=pl.CostEstimate(
            flops=60_000_000_000, bytes_accessed=220_000_000, transcendentals=0
        ),
        name="mix_backward",
    )(prefix_len, queries, keys, values, cum, states, prefix_state, grad_mixed)


EXTRA = 128


def physical_axes(mesh):
    shape = mesh.devices.shape
    names = []
    sizes = []
    for axis, extent in enumerate(shape):
        line = np.moveaxis(mesh.devices, axis, 0).reshape(extent, -1)[:, 0]
        places = [tuple(d.coords) + (d.core_on_chip,) for d in line]
        parts = []
        for dim, label in enumerate(("x", "y", "z", "core")):
            values = [p[dim] for p in places]
            if len(set(values)) > 1:
                step = next(i for i in range(extent) if values[i] != values[0])
                parts.append((step, label, len(set(values))))
        for step, label, size in sorted(parts, reverse=True):
            names.append(label)
            sizes.append(size)
    return tuple(names), tuple(sizes)


def pack_mixer(norm1_gain, norm2_gain, query, key, value, gate, down, up, bias, group, out):
    rows = query.shape[0]
    small = jnp.zeros((rows, EXTRA), query.dtype)
    small = small.at[:, :16].set(down)
    small = small.at[:, 16].set(norm1_gain)
    small = small.at[:, 17].set(norm2_gain)
    small = small.at[: bias.shape[0], 18].set(bias)
    small = small.at[: group.shape[0], 19].set(group)
    small = small.at[:, 24:32].set(up.T.reshape(rows, 8))
    return jnp.concatenate([query, key, value, gate, out, small], axis=1)


def unpack_small(small, devices):
    rows = small.shape[0] // devices
    by_device = small.reshape(devices, rows, EXTRA)
    down = small[:, :16]
    gain_one = small[:, 16]
    gain_two = small[:, 17]
    bias = by_device[:, : KEYS // devices, 18].reshape(KEYS)
    group = by_device[:, : HEAD_V // devices, 19].reshape(HEAD_V)
    up = small[:, 24:32].reshape(KEYS, 16).T
    return down, gain_one, gain_two, bias, group, up


def pack_small_grads(down, gain_one, gain_two, bias, group, up, devices):
    rows = gain_one.shape[0] // devices

    def column(vector):
        parts = vector.reshape(devices, -1)
        parts = jnp.pad(parts, ((0, 0), (0, rows - parts.shape[1])))
        return parts.reshape(devices * rows, 1)

    pieces = [
        down,
        gain_one[:, None],
        gain_two[:, None],
        column(bias),
        column(group),
        jnp.zeros((rows * devices, 4), jnp.float32),
        up.T.reshape(rows * devices, 8),
        jnp.zeros((rows * devices, EXTRA - 32), jnp.float32),
    ]
    return jnp.concatenate(pieces, axis=1)


def core_halves(rows, names, sizes):
    width = rows.shape[1]
    at = names.index("core")
    before = int(np.prod(sizes[:at], initial=1))
    after = width // before // sizes[at]
    core = lax.axis_index("core")

    def half(which):
        return jnp.concatenate(
            [
                lax.dynamic_slice_in_dim(rows, (2 * i + which) * after, after, 1)
                for i in range(before)
            ],
            axis=1,
        )

    return half(core), half(1 - core)


def swap_cores(values):
    return lax.ppermute(values, "core", [(0, 1), (1, 0)])


def pair_sum(halves, gradient):
    mine, other = halves
    taken = swap_cores(flat_grad(other, gradient).astype(jnp.bfloat16))
    return (flat_grad(mine, gradient) + taken.astype(jnp.float32)).astype(jnp.bfloat16)


def flat_grad(inputs, gradient):
    return jnp.einsum("td,te->de", inputs, gradient, preferred_element_type=jnp.float32)


def by_chip(values, names, sizes):
    chips = tuple(size for name, size in zip(names, sizes) if name != "core")
    return values.reshape(*chips, -1, values.shape[-1])


def pass_along(values, left, name):
    at = left.index(name)
    size = values.shape[at]
    own = lax.axis_index(name)
    arrived = []
    for shift in range(1, size):
        given = lax.dynamic_index_in_dim(values, lax.rem(own + shift, size), at, False)
        arrived.append(
            lax.ppermute(given, name, [(i, (i + shift) % size) for i in range(size)])
        )
    return arrived


def take_in(values, arrived, left, name):
    at = left.index(name)
    total = lax.dynamic_index_in_dim(values, lax.axis_index(name), at, False).astype(jnp.float32)
    for term in arrived:
        total = total + term.astype(jnp.float32)
    return total, [other for other in left if other != name]


def reduce_kernel(plan, *refs):
    inputs, jobs, sizes, slots = plan
    count = len(jobs)
    in_refs = refs[:inputs]
    outputs = max(job[4] for job in jobs) + 1
    out_refs = refs[inputs : inputs + outputs]
    scratch = refs[inputs + outputs :]
    send_sem, recv_sem = scratch[-2:]
    scratch = list(scratch[:-2])

    reached = sorted({name for job in jobs for name in job[3]})
    barrier = pltpu.get_barrier_semaphore()
    peers = 0
    for name in reached:
        for shift in range(1, sizes[name]):
            peer = lax.rem(lax.axis_index(name) + shift, sizes[name])
            pl.semaphore_signal(barrier, inc=1, device_id={name: peer}, device_id_type=MESH)
            peers += 1
    pl.semaphore_wait(barrier, peers)

    class Job:
        pass

    work = []
    slot = 0
    for which, columns, axes, order, out, out_columns in jobs:
        job = Job()
        job.left = list(axes)
        job.order = order
        job.out = out_refs[out]
        job.out_columns = slice(*out_columns)
        job.source = in_refs[which]
        job.columns = slice(*columns)
        job.got = [scratch.pop(0) for _ in order]
        job.kept = [scratch.pop(0) for _ in order[:-1]]
        job.slots = []
        for name in order:
            job.slots.append(slot)
            slot += sizes[name] - 1
        work.append(job)

    def part(job, index):
        at = job.left.index(job.order[job.step])
        lead = [slice(None)] * len(job.left)
        lead[at] = index
        return job.source.at[(*lead, slice(None), job.columns)]

    def copies(job):
        name = job.order[job.step]
        own = lax.axis_index(name)
        for shift in range(1, sizes[name]):
            peer = lax.rem(own + shift, sizes[name])
            at = job.slots[job.step] + shift - 1
            yield pltpu.make_async_remote_copy(
                src_ref=part(job, peer),
                dst_ref=job.got[job.step].at[shift - 1],
                send_sem=send_sem.at[at],
                recv_sem=recv_sem.at[at],
                device_id={name: peer},
                device_id_type=MESH,
            )

    def start(job):
        for copy in copies(job):
            copy.start()

    def add(job):
        name = job.order[job.step]
        at = job.left.index(name)
        own = lax.axis_index(name)
        rest = [n for n in job.left if n != name]
        last = job.step == len(job.order) - 1
        total = int(np.prod([sizes[n] for n in rest], initial=1))
        got = job.got[job.step]
        for copy in copies(job):
            copy.wait()
        source, columns, step = job.source, job.columns, job.step

        def one(i, carry):
            index = []
            for n in reversed(rest):
                index.insert(0, lax.rem(i, sizes[n]))
                i = lax.div(i, sizes[n])
            lead = list(index)
            lead.insert(at, own)
            value = source[(*lead, slice(None), columns)].astype(jnp.float32)
            for shift in range(1, sizes[name]):
                value = value + got[(shift - 1, *index)].astype(jnp.float32)
            if last:
                job.out[:, job.out_columns] = value
            else:
                job.kept[step][tuple(index)] = value.astype(jnp.bfloat16)
            return carry

        if total == 1:
            one(jnp.int32(0), 0)
        else:
            lax.fori_loop(0, total, one, 0)
        job.left = rest
        if not last:
            job.source = job.kept[step]
            job.columns = slice(None)
            job.step += 1
            start(job)

    for job in work:
        job.step = 0
        start(job)
    for step in range(max(len(job.order) for job in work)):
        for job in work:
            if len(job.order) > step:
                add(job)


def reduce_rest(arrays, jobs, sizes, rows, widths, collective):
    scratch = []
    slots = 0
    for which, (begin, end), axes, order, out, out_columns in jobs:
        left = list(axes)
        kept = []
        got = []
        for name in order:
            left.remove(name)
            shape = tuple(sizes[n] for n in left)
            got.append(pltpu.VMEM((sizes[name] - 1, *shape, rows, end - begin), jnp.bfloat16))
            kept.append(pltpu.VMEM((*shape, rows, end - begin), jnp.bfloat16))
            slots += sizes[name] - 1
        scratch += got + kept[:-1]
    scratch += [pltpu.SemaphoreType.DMA((slots,))] * 2
    return pl.pallas_call(
        partial(reduce_kernel, (len(arrays), jobs, sizes, slots)),
        out_shape=tuple(jax.ShapeDtypeStruct((rows, width), jnp.float32) for width in widths),
        in_specs=whole_specs(len(arrays)),
        out_specs=tuple(whole_specs(len(widths))),
        scratch_shapes=scratch,
        compiler_params=pltpu.CompilerParams(
            collective_id=collective, has_side_effects=True, vmem_limit_bytes=40 * 2**20
        ),
        name="reduce_rest",
    )(*arrays)


def chip_orders(names):
    first, second, last = [name for name in names if name != "core"]
    return (first, second, last), (second, last, first), (last, first, second)


def local(
    names,
    sizes,
    seq_axes,
    tokens,
    prefix_len,
    norm1_gain,
    query_weight,
    key_weight,
    value_weight,
    gate_weight,
    decay_down,
    decay_up,
    decay_bias,
    group_gain,
    out_weight,
    norm2_gain,
    ffn_gate,
    ffn_up,
    ffn_down,
    out_grad,
):
    devices = int(np.prod(sizes))
    mixer_full = lax.all_gather(
        pack_mixer(
            norm1_gain,
            norm2_gain,
            query_weight,
            key_weight,
            value_weight,
            gate_weight,
            decay_down,
            decay_up,
            decay_bias,
            group_gain,
            out_weight,
        ),
        names,
        axis=0,
        tiled=True,
    )
    ffn_full = lax.all_gather(
        jnp.concatenate([ffn_gate, ffn_up, ffn_down.T], axis=1), names, axis=0, tiled=True
    )
    weight_q = mixer_full[:, :512]
    weight_k = mixer_full[:, 512:1024]
    weight_v = mixer_full[:, 1024:2048]
    weight_g = mixer_full[:, 2048:3072]
    weight_o = mixer_full[:, 3072:4096]
    weight_down, gain_one, gain_two, bias_full, gain_group, weight_up = unpack_small(
        mixer_full[:, 4096:], devices
    )
    weight_gate = ffn_full[:, :FF]
    weight_upper = ffn_full[:, FF : 2 * FF]
    weight_lower = ffn_full[:, 2 * FF :].T
    seq_count, tok_count, feature_count = tokens.shape
    resid_in = tokens.astype(jnp.float32)
    scale_one = rms_scale(resid_in)
    unit_one = resid_in * scale_one
    normed = (unit_one * gain_one.astype(jnp.float32)).astype(jnp.bfloat16)
    queries = project(normed, weight_q).astype(jnp.bfloat16)
    key_matrix = project(normed, weight_k).astype(jnp.bfloat16)
    value_matrix = project(normed, weight_v).astype(jnp.bfloat16)
    gate_out = project(normed, weight_g)
    lowrank = project(normed, weight_down).astype(jnp.bfloat16)
    logits = project(lowrank, weight_up) + bias_full.astype(jnp.float32)
    decays = jax.nn.log_sigmoid(logits) / 16.0
    rows = seq_count * tok_count
    flat_q = queries.reshape(rows, KEYS)
    flat_k = key_matrix.reshape(rows, KEYS)
    flat_v = value_matrix.reshape(rows, VALS)
    mixed, cum, states, prefix_state = mix_forward(
        seq_axes, prefix_len, flat_q, flat_k, flat_v, decays.reshape(rows, KEYS)
    )
    mixed_heads = mixed.reshape(seq_count, tok_count, HEADS, HEAD_V)
    scale_group = rms_scale(mixed_heads)
    unit_group = mixed_heads * scale_group
    normed_group = unit_group * gain_group.astype(jnp.float32)
    swish_gate = jax.nn.silu(gate_out).reshape(seq_count, tok_count, HEADS, HEAD_V)
    gated_rows = (
        (normed_group * swish_gate).reshape(seq_count, tok_count, VALS).astype(jnp.bfloat16)
    )
    branch = project(gated_rows, weight_o)
    resid_mid = resid_in + branch
    scale_two = rms_scale(resid_mid)
    unit_two = resid_mid * scale_two
    normed_two = (unit_two * gain_two.astype(jnp.float32)).astype(jnp.bfloat16)
    gate_part = project(normed_two, weight_gate)
    up_part = project(normed_two, weight_upper)
    gate_act = jax.nn.silu(gate_part)
    hidden = (gate_act * up_part).astype(jnp.bfloat16)
    ffn_out = project(hidden, weight_lower)
    layer_out = (resid_mid + ffn_out).astype(jnp.bfloat16)
    grad_out = out_grad.astype(jnp.float32)
    grad_hidden = back_project(out_grad, weight_lower)
    grad_gate = (grad_hidden * up_part * silu_slope(gate_part)).astype(jnp.bfloat16)
    grad_up = (grad_hidden * gate_act).astype(jnp.bfloat16)
    grad_normed_two = back_project(grad_gate, weight_gate) + back_project(grad_up, weight_upper)
    gain_two_grad = jnp.sum(grad_normed_two * unit_two, axis=(0, 1))
    grad_mid = grad_out + rms_back(
        grad_normed_two * gain_two.astype(jnp.float32), unit_two, scale_two
    )
    grad_branch = grad_mid.astype(jnp.bfloat16)
    normed_halves = core_halves(normed.reshape(rows, -1), names, sizes)
    two_halves = core_halves(normed_two.reshape(rows, -1), names, sizes)
    gate_sum = pair_sum(two_halves, grad_gate.reshape(rows, FF))
    up_sum = pair_sum(two_halves, grad_up.reshape(rows, FF))
    down_sum = pair_sum(
        core_halves(out_grad.reshape(rows, -1), names, sizes), hidden.reshape(rows, FF)
    )
    out_sum = pair_sum(
        core_halves(gated_rows.reshape(rows, -1), names, sizes), grad_branch.reshape(rows, -1)
    )
    grad_gated = back_project(grad_branch, weight_o).reshape(seq_count, tok_count, HEADS, HEAD_V)
    grad_normed_group = grad_gated * swish_gate
    grad_swish = (grad_gated * normed_group).reshape(seq_count, tok_count, VALS)
    grad_gate_out = (grad_swish * silu_slope(gate_out)).astype(jnp.bfloat16)
    group_grad = jnp.sum(grad_normed_group * unit_group, axis=(0, 1, 2))
    grad_mixed = rms_back(
        grad_normed_group * gain_group.astype(jnp.float32), unit_group, scale_group
    )
    gate_out_sum = pair_sum(normed_halves, grad_gate_out.reshape(rows, VALS))
    groups = (
        jnp.concatenate([gate_sum, out_sum, down_sum[:, 2048:2432]], axis=1),
        jnp.concatenate([up_sum, gate_out_sum, down_sum[:, 2432:]], axis=1),
        down_sum[:, :2048],
    )
    groups, grad_mixed = lax.optimization_barrier((groups, grad_mixed))
    chips = [name for name in names if name != "core"]
    orders = chip_orders(names)
    lefts = [chips] * 3
    groups = [by_chip(group, names, sizes) for group in groups]
    arrived = [pass_along(g, left, order[0]) for g, left, order in zip(groups, lefts, orders)]
    grad_qkv, grad_decay = mix_backward(
        seq_axes,
        prefix_len,
        flat_q,
        flat_k,
        flat_v,
        cum,
        states,
        prefix_state,
        grad_mixed.reshape(rows, VALS),
    )
    arrived, grad_qkv, grad_decay = lax.optimization_barrier((arrived, grad_qkv, grad_decay))

    def next_axis(groups, arrived, lefts, step):
        taken = [
            take_in(g, more, left, order[step])
            for g, more, left, order in zip(groups, arrived, lefts, orders)
        ]
        lefts = [left for _, left in taken]
        if step == 2:
            return [total for total, _ in taken], None, lefts
        groups = [total.astype(jnp.bfloat16) for total, _ in taken]
        arrived = [
            pass_along(g, left, order[step + 1]) for g, left, order in zip(groups, lefts, orders)
        ]
        return groups, arrived, lefts

    groups, arrived, lefts = next_axis(groups, arrived, lefts, 0)
    grad_logits = (
        grad_decay.reshape(seq_count, tok_count, KEYS) * jax.nn.sigmoid(-logits) / 16.0
    ).astype(jnp.bfloat16)
    bias_grad = jnp.sum(grad_logits.astype(jnp.float32), axis=(0, 1))
    up_rank_grad = weight_grad(lowrank, grad_logits)
    grad_lowrank = back_project(grad_logits, weight_up).astype(jnp.bfloat16)
    down_rank_grad = weight_grad(normed, grad_lowrank)
    grad_normed = (
        back_project(grad_qkv.reshape(seq_count, tok_count, -1), mixer_full[:, :2048])
        + back_project(grad_gate_out, weight_g)
        + back_project(grad_lowrank, weight_down)
    )
    gain_one_grad = jnp.sum(grad_normed * unit_one, axis=(0, 1))
    tokens_grad = grad_mid + rms_back(
        grad_normed * gain_one.astype(jnp.float32), unit_one, scale_one
    )
    small_grads = pack_small_grads(
        down_rank_grad, gain_one_grad, gain_two_grad, bias_grad, group_grad, up_rank_grad, devices
    )
    late = flat_grad(normed.reshape(rows, -1), grad_qkv).astype(jnp.bfloat16)
    small_grads = small_grads.astype(jnp.bfloat16)
    arrived, late, small_grads, tokens_grad = lax.optimization_barrier(
        (arrived, late, small_grads, tokens_grad)
    )
    groups = [
        take_in(g, more, left, order[1])[0].astype(jnp.bfloat16)
        for g, more, left, order in zip(groups, arrived, lefts, orders)
    ]
    own_rows = feature_count // devices
    late = late.reshape(*sizes, own_rows, -1)
    small_grads = small_grads.reshape(*sizes, own_rows, -1)
    size_of = dict(zip(names, sizes))
    jobs = [
        (which, columns, names, ("core", *order), which, columns)
        for which, columns, order in (
            (3, (0, 896), orders[0]),
            (3, (896, 1792), orders[1]),
            (3, (1792, 2048), orders[2]),
            (4, (0, EXTRA), orders[2]),
        )
    ] + [
        (i, (0, groups[i].shape[-1]), (order[2],), (order[2],), i, (0, groups[i].shape[-1]))
        for i, order in enumerate(orders)
    ]
    first_group, second_group, third_group, mine, small = reduce_rest(
        (*groups, late, small_grads), jobs, size_of, own_rows, (4224, 4224, 2048, 2048, EXTRA), 3
    )
    return (
        layer_out,
        tokens_grad,
        small[:, 16],
        mine[:, :512],
        mine[:, 512:1024],
        mine[:, 1024:2048],
        second_group[:, FF : FF + VALS],
        small[:, :16],
        small[:, 24:32].reshape(KEYS // devices, 16).T,
        small[: KEYS // devices, 18],
        small[: HEAD_V // devices, 19],
        first_group[:, FF : FF + VALS],
        small[:, 17],
        first_group[:, :FF],
        second_group[:, :FF],
        jnp.concatenate(
            [third_group, first_group[:, FF + VALS :], second_group[:, FF + VALS :]], axis=1
        ).T,
    )


def solution(mesh):
    names, sizes = physical_axes(mesh)
    cut = next(
        i for i in range(len(sizes) + 1) if np.prod(sizes[:i], initial=1) == mesh.shape["dp"]
    )
    dp, seq = names[:cut], names[cut:]
    split = Mesh(mesh.devices.reshape(sizes), names)
    return jax.shard_map(
        partial(local, names, sizes, tuple(zip(seq, sizes[cut:]))),
        mesh=split,
        in_specs=(
            P(dp, seq, None),
            P(dp),
            P(names),
            P(names, None),
            P(names, None),
            P(names, None),
            P(names, None),
            P(names, None),
            P(None, names),
            P(names),
            P(names),
            P(names, None),
            P(names),
            P(names, None),
            P(names, None),
            P(None, names),
            P(dp, seq, None),
        ),
        out_specs=(
            P(dp, seq, None),
            P(dp, seq, None),
            P(names),
            P(names, None),
            P(names, None),
            P(names, None),
            P(names, None),
            P(names, None),
            P(None, names),
            P(names),
            P(names),
            P(names, None),
            P(names),
            P(names, None),
            P(names, None),
            P(None, names),
        ),
        check_vma=False,
    )
```

```python
from functools import partial

import jax
import jax.numpy as jnp
import numpy as np
from jax import lax
from jax.experimental import pallas as pl
from jax.experimental.pallas import tpu as pltpu
from jax.sharding import Mesh
from jax.sharding import PartitionSpec as P

KEYS = 512
VALS = 1024
HEADS = 4
SPAN = 64
HEAD_K = 128
HEAD_V = 256
FF = 2816


norm_eps = 1e-05


def project(inputs, weight):
    return jnp.einsum("td,de->te", inputs, weight, preferred_element_type=jnp.float32)


def back_project(gradient, weight):
    return jnp.einsum("te,de->td", gradient, weight, preferred_element_type=jnp.float32)


def rms_scale(values):
    return lax.rsqrt(jnp.mean(values * values, axis=-1, keepdims=True) + norm_eps)


def rms_back(grad_unit, unit_rows, scale_rows):
    return scale_rows * (
        grad_unit - unit_rows * jnp.mean(grad_unit * unit_rows, axis=-1, keepdims=True)
    )


def silu_slope(values):
    logistic = jax.nn.sigmoid(values)
    return logistic * (1.0 + values * (1.0 - logistic))


CHUNK = 128
MESH = pl.DeviceIdType.MESH


def nn(a, b):
    return lax.dot_general(a, b, (((1,), (0,)), ((), ())), preferred_element_type=jnp.float32)


def nt(a, b):
    return lax.dot_general(a, b, (((1,), (1,)), ((), ())), preferred_element_type=jnp.float32)


def tn(a, b):
    return lax.dot_general(a, b, (((0,), (0,)), ((), ())), preferred_element_type=jnp.float32)


def low(values):
    return values.astype(jnp.bfloat16)


def wide(values):
    return values.astype(jnp.float32)


def three_way(ones, values):
    first = low(values)
    left = values - wide(first)
    second = low(left)
    third = low(left - wide(second))
    return nn(ones, first) + nn(ones, second) + nn(ones, third)


def iota(shape, dim):
    return lax.broadcasted_iota(jnp.int32, shape, dim)


def place_on(axes):
    place = 0
    for name, size in axes:
        place = place * size + lax.axis_index(name)
    return place


def device_at(axes, place):
    where = {}
    for name, size in reversed(axes):
        where[name] = lax.rem(place, size)
        place = lax.div(place, size)
    return where


def line_length(axes):
    return int(np.prod([size for _, size in axes]))


def greet(axes, place, count, extra=0):
    barrier = pltpu.get_barrier_semaphore()

    @pl.when(place > 0)
    def _():
        pl.semaphore_signal(
            barrier, inc=1, device_id=device_at(axes, place - 1), device_id_type=MESH
        )

    @pl.when(place < count - 1)
    def _():
        pl.semaphore_signal(
            barrier, inc=1, device_id=device_at(axes, place + 1), device_id_type=MESH
        )

    @pl.when(jnp.logical_or(place == 0, place == count - 1))
    def _():
        pl.semaphore_wait(barrier, 1 + extra)

    @pl.when(jnp.logical_and(place > 0, place < count - 1))
    def _():
        pl.semaphore_wait(barrier, 2 + extra)


def send(source, target, send_sem, recv_sem, axes, place):
    return pltpu.make_async_remote_copy(
        src_ref=source,
        dst_ref=target,
        send_sem=send_sem,
        recv_sem=recv_sem,
        device_id=device_at(axes, place),
        device_id_type=MESH,
    )


class Gather:
    def __init__(self, names, sizes, pieces, local_sem, send_sem, recv_sem, pair_send, pair_recv):
        self.names = names
        self.sizes = dict(zip(names, sizes))
        self.pieces = pieces
        self.sems = local_sem, send_sem, recv_sem, pair_send, pair_recv
        self.steps = len(pieces[0][4])

    def region(self, piece, known, at):
        lead = []
        for name in self.names:
            if name in known:
                lead.append(slice(None))
            elif name in at:
                lead.append(at[name])
            else:
                lead.append(lax.axis_index(name))
        _, whole, _, columns, _ = piece
        return whole.at[(*lead, slice(None), slice(*columns))]

    def local(self, i):
        shard, _, columns, _, _ = self.pieces[i]
        return pltpu.make_async_copy(
            shard.at[:, slice(*columns)], self.region(self.pieces[i], (), {}), self.sems[0].at[i]
        )

    def copies(self, i, step):
        piece = self.pieces[i]
        order = piece[4]
        name = order[step]
        own = lax.axis_index(name)
        base = (i * self.steps + step) * 3
        for shift in range(1, self.sizes[name]):
            peer = lax.rem(own + shift, self.sizes[name])
            here = self.region(piece, order[:step], {})
            yield pltpu.make_async_remote_copy(
                src_ref=here,
                dst_ref=here,
                send_sem=self.sems[1].at[base + shift - 1],
                recv_sem=self.sems[2].at[base + shift - 1],
                device_id={name: peer},
                device_id_type=MESH,
            )

    def pair(self, i, step, shift):
        piece = self.pieces[i]
        order = piece[4]
        if step < 0:
            here = self.region(piece, (), {})
            at = 0
        else:
            name = order[step]
            source = lax.rem(lax.axis_index(name) + self.sizes[name] - shift, self.sizes[name])
            here = self.region(piece, order[:step], {name: source})
            at = 1 + step * 3 + shift - 1
        at += i * (1 + 3 * self.steps)
        return pltpu.make_async_remote_copy(
            src_ref=here,
            dst_ref=here,
            send_sem=self.sems[3].at[at],
            recv_sem=self.sems[4].at[at],
            device_id={"core": 1 - lax.axis_index("core")},
            device_id_type=MESH,
        )

    def begin(self):
        for i in range(len(self.pieces)):
            self.local(i).start()
        for i in range(len(self.pieces)):
            self.local(i).wait()
            for copy in self.copies(i, 0):
                copy.start()
            self.pair(i, -1, 0).start()

    def advance(self, step):
        for i, piece in enumerate(self.pieces):
            for copy in self.copies(i, step):
                copy.wait_recv()
            if step < self.steps - 1:
                for copy in self.copies(i, step + 1):
                    copy.start()
            for shift in range(1, self.sizes[piece[4][step]]):
                self.pair(i, step, shift).start()

    def end(self):
        for i, piece in enumerate(self.pieces):
            for step in range(self.steps):
                for copy in self.copies(i, step):
                    copy.wait_send()
                for shift in range(1, self.sizes[piece[4][step]]):
                    self.pair(i, step, shift).wait()
            self.pair(i, -1, 0).wait()

    @staticmethod
    def scratch(count):
        return [
            pltpu.SemaphoreType.DMA((count,)),
            pltpu.SemaphoreType.DMA((count * 9,)),
            pltpu.SemaphoreType.DMA((count * 9,)),
            pltpu.SemaphoreType.DMA((count * 10,)),
            pltpu.SemaphoreType.DMA((count * 10,)),
        ]


def signal_axes(names, sizes):
    barrier = pltpu.get_barrier_semaphore()
    peers = 0
    for name, size in zip(names, sizes):
        for shift in range(1, size):
            peer = lax.rem(lax.axis_index(name) + shift, size)
            pl.semaphore_signal(barrier, inc=1, device_id={name: peer}, device_id_type=MESH)
            peers += 1
    return peers


def gather_kernel(plan, *refs):
    names, sizes, inputs, outputs, pieces = plan
    wholes = refs[inputs : inputs + outputs]
    peers = signal_axes(names, sizes)
    pl.semaphore_wait(pltpu.get_barrier_semaphore(), peers)
    gather = Gather(
        names,
        sizes,
        [(refs[i], wholes[o], cols, to, order) for i, o, cols, to, order in pieces],
        *refs[inputs + outputs :],
    )
    gather.begin()
    for step in range(gather.steps):
        gather.advance(step)
    gather.end()


def gather_first(names, sizes, shards, widths, pieces):
    rows = shards[0].shape[0]
    anywhere = pl.BlockSpec(memory_space=pl.ANY)
    return pl.pallas_call(
        partial(gather_kernel, (names, sizes, len(shards), len(widths), pieces)),
        out_shape=tuple(
            jax.ShapeDtypeStruct((*sizes, rows, width), jnp.bfloat16) for width in widths
        ),
        in_specs=[anywhere] * len(shards),
        out_specs=(anywhere,) * len(widths),
        scratch_shapes=Gather.scratch(len(pieces)),
        compiler_params=pltpu.CompilerParams(collective_id=4, has_side_effects=True),
        name="gather_first",
    )(*shards)


def row_places(count):
    return iota((count, HEAD_K), 0)


def prefix_weights(cum, end_local, count):
    rows = row_places(count)
    owner = jnp.logical_and(end_local >= 0, end_local < count)
    end_cum = jnp.sum(jnp.where(rows == end_local, cum, 0.0), axis=0, keepdims=True)
    keep = jnp.logical_and(rows <= end_local, rows <= jnp.where(owner, count, -1))
    weights = jnp.where(keep, jnp.exp(jnp.where(keep, end_cum - cum, 0.0)), 0.0)
    return weights, jnp.exp(end_cum) * jnp.where(owner, 1.0, 0.0)


def chunk_parts(cum, chunk):
    begin = chunk * CHUNK
    piece = cum[begin : begin + CHUNK]
    if chunk:
        piece = piece - cum[begin - 1 : begin]
    return piece, piece[CHUNK - 1 :], piece[CHUNK // 2 - 1 : CHUNK // 2]


def query_columns(head):
    return slice(head * HEAD_K, (head + 1) * HEAD_K)


def key_columns(head):
    return slice(KEYS + head * HEAD_K, KEYS + (head + 1) * HEAD_K)


def value_columns(head):
    return slice(2 * KEYS + head * HEAD_V, 2 * KEYS + (head + 1) * HEAD_V)


def gate_columns(head):
    begin = 2 * KEYS + VALS + head * HEAD_V
    return slice(begin, begin + HEAD_V)


def forward_kernel(plan, *refs):
    axes = plan
    prefix_ref, proj_ref, decay_ref, gain_ref = refs[:4]
    gated_ref, unit_ref, scale_ref, cum_ref, state_ref, prefix_state_ref = refs[4:10]
    mixed_ref, kv_ref, part_ref, edge_ref, *line = refs[10:]
    right_out, right_in, left_out, left_in, right_sent, right_got, left_sent, left_got = line
    count = line_length(axes)
    place = place_on(axes)
    seqs = prefix_ref.shape[0]
    toks = proj_ref.shape[0] // seqs
    chunks = toks // CHUNK
    greet(axes, place, count)
    lower = low(jnp.where(iota((CHUNK, CHUNK), 0) >= iota((CHUNK, CHUNK), 1), 1.0, 0.0))
    causal = iota((CHUNK, CHUNK), 0) >= iota((CHUNK, CHUNK), 1)

    def to_right(i):
        return send(right_out.at[i], right_in.at[i], right_sent.at[i], right_got.at[i], axes, place + 1)

    def to_left(i):
        return send(left_out.at[i], left_in.at[i], left_sent.at[i], left_got.at[i], axes, place - 1)

    def states_of(seq, carry):
        rows = pl.ds(pl.multiple_of(seq * toks, toks), toks)
        end_local = prefix_ref[seq] - 1 - place * toks
        for head in range(HEADS):
            i = seq * HEADS + head
            keys = slice(head * HEAD_K, (head + 1) * HEAD_K)
            vals = slice(head * HEAD_V, (head + 1) * HEAD_V)
            before = jnp.zeros((1, HEAD_K), jnp.float32)
            key = wide(proj_ref[rows, key_columns(head)])
            value = proj_ref[rows, value_columns(head)]
            decay = decay_ref[rows, keys]
            pieces = []
            local = jnp.zeros((HEAD_V, HEAD_K), jnp.float32)
            for chunk in range(chunks):
                at = slice(chunk * CHUNK, (chunk + 1) * CHUNK)
                piece = three_way(lower, decay[at])
                total = piece[CHUNK - 1 :]
                share = tn(value[at], low(key[at] * jnp.exp(total - piece)))
                kv_ref[i, chunk] = share
                local = jnp.exp(total) * local + share
                pieces.append(piece + before)
                before = before + total
            cum = jnp.concatenate(pieces, axis=0)
            cum_ref[rows, keys] = cum
            weights, edge = prefix_weights(cum, end_local, toks)
            part_ref[i] = tn(value, low(key * weights))
            edge_ref[i] = jnp.broadcast_to(edge, (8, HEAD_K))

            @pl.when(place == 0)
            def _():
                right_out[i] = low(local)
                if count > 1:
                    to_right(i).start()

        return carry

    lax.fori_loop(0, seqs, states_of, 0)

    def outputs_of(seq, carry):
        rows = pl.ds(pl.multiple_of(seq * toks, toks), toks)
        for head in range(HEADS):
            i = seq * HEADS + head
            keys = slice(head * HEAD_K, (head + 1) * HEAD_K)
            vals = slice(head * HEAD_V, (head + 1) * HEAD_V)
            cum = cum_ref[rows, keys]
            query = wide(proj_ref[rows, query_columns(head)])
            key = wide(proj_ref[rows, key_columns(head)])
            value = proj_ref[rows, value_columns(head)]
            scores = []
            for chunk in range(chunks):
                at = slice(chunk * CHUNK, (chunk + 1) * CHUNK)
                piece, total, middle = chunk_parts(cum, chunk)
                raw = nt(
                    low(query[at] * jnp.exp(piece - middle)), low(key[at] * jnp.exp(middle - piece))
                )
                scores.append(low(jnp.where(causal, raw, 0.0)))

            @pl.when(place == 0)
            def _():
                right_in[i] = jnp.zeros((HEAD_V, HEAD_K), jnp.bfloat16)

            @pl.when(place > 0)
            def _():
                send(right_out.at[i], right_in.at[i], right_sent.at[i], right_got.at[i], axes, place - 1).wait_recv()

            state = wide(right_in[i])
            part = part_ref[i] + edge_ref[i][:1] * state
            part_ref[i] = part
            for chunk in range(chunks):
                at = slice(chunk * CHUNK, (chunk + 1) * CHUNK)
                piece, total, middle = chunk_parts(cum, chunk)
                narrow = low(state)
                state_ref[i, chunk] = narrow
                output = nn(scores[chunk], value[at]) + nt(
                    low(query[at] * jnp.exp(piece)), narrow
                )
                mixed_ref[pl.ds(seq * toks + chunk * CHUNK, CHUNK), vals] = output
                state = jnp.exp(total) * state + kv_ref[i, chunk]
            state_ref[i, chunks] = low(state)

            @pl.when(jnp.logical_and(place > 0, place < count - 1))
            def _():
                right_out[i] = low(state)
                to_right(i).start()

            if count > 1:

                @pl.when(place == count - 1)
                def _():
                    left_out[i] = low(part)
                    to_left(i).start()

        return carry

    lax.fori_loop(0, seqs, outputs_of, 0)

    def prefix_of(seq, carry):
        rows = pl.ds(pl.multiple_of(seq * toks, toks), toks)
        end_local = prefix_ref[seq] - 1 - place * toks
        inside = iota((toks, HEAD_V), 0) <= end_local
        for head in range(HEADS):
            i = seq * HEADS + head
            keys = slice(head * HEAD_K, (head + 1) * HEAD_K)
            vals = slice(head * HEAD_V, (head + 1) * HEAD_V)

            @pl.when(place < count - 1)
            def _():
                send(left_out.at[i], left_in.at[i], left_sent.at[i], left_got.at[i], axes, place + 1).wait_recv()

            @pl.when(place == count - 1)
            def _():
                left_in[i] = jnp.zeros((HEAD_V, HEAD_K), jnp.bfloat16)

            whole = low(part_ref[i] + wide(left_in[i]))

            @pl.when(jnp.logical_and(place > 0, place < count - 1))
            def _():
                left_out[i] = whole
                to_left(i).start()

            prefix_state_ref[i] = whole
            mixed = jnp.where(
                inside, nt(proj_ref[rows, query_columns(head)], whole), mixed_ref[rows, vals]
            )
            scale = lax.rsqrt(jnp.mean(mixed * mixed, axis=1, keepdims=True) + norm_eps)
            unit = mixed * scale
            gate = wide(proj_ref[rows, gate_columns(head)])
            gated_ref[rows, vals] = low(unit * gain_ref[:1] * (gate / (1.0 + jnp.exp(-gate))))
            unit_ref[rows, vals] = low(unit)
            scale_ref[rows, slice(head, head + 1)] = scale
        return carry

    lax.fori_loop(0, seqs, prefix_of, 0)

    def finish(i, carry):
        @pl.when(place < count - 1)
        def _():
            to_right(i).wait_send()

        @pl.when(place > 0)
        def _():
            to_left(i).wait_send()

        return carry

    lax.fori_loop(0, seqs * HEADS, finish, 0)


def backward_kernel(
    axes,
    prefix_ref,
    proj_ref,
    cum_ref,
    state_ref,
    prefix_state_ref,
    gated_grad_ref,
    unit_ref,
    scale_ref,
    gain_ref,
    dproj_ref,
    ddecay_ref,
    gain_grad_ref,
    grad_ref,
    local_ref,
    acc_ref,
    dk_part,
    dv_part,
    dcum_part,
    right_out,
    right_in,
    left_out,
    left_in,
    right_sent,
    right_got,
    left_sent,
    left_got,
):
    count = line_length(axes)
    place = place_on(axes)
    seqs = prefix_ref.shape[0]
    toks = proj_ref.shape[0] // seqs
    chunks = toks // CHUNK
    greet(axes, place, count)
    causal = iota((CHUNK, CHUNK), 0) >= iota((CHUNK, CHUNK), 1)
    upper = low(jnp.where(iota((toks, toks), 0) <= iota((toks, toks), 1), 1.0, 0.0))

    def to_right(i):
        return send(right_out.at[i], right_in.at[i], right_sent.at[i], right_got.at[i], axes, place + 1)

    def to_left(i):
        return send(left_out.at[i], left_in.at[i], left_sent.at[i], left_got.at[i], axes, place - 1)

    def shares_of(seq, carry):
        rows = pl.ds(pl.multiple_of(seq * toks, toks), toks)
        end_local = prefix_ref[seq] - 1 - place * toks
        inside = iota((toks, HEAD_V), 0) <= end_local
        for head in range(HEADS):
            i = seq * HEADS + head
            keys = slice(head * HEAD_K, (head + 1) * HEAD_K)
            vals = slice(head * HEAD_V, (head + 1) * HEAD_V)
            cum = cum_ref[rows, keys]
            query = proj_ref[rows, query_columns(head)]
            gate = wide(proj_ref[rows, gate_columns(head)])
            logistic = 1.0 / (1.0 + jnp.exp(-gate))
            unit = wide(unit_ref[rows, vals])
            gain = gain_ref[:1]
            gated_grad = wide(gated_grad_ref[rows, vals])
            through = gated_grad * unit
            active = gate * logistic
            dproj_ref[rows, gate_columns(head)] = low(
                through * gain * (logistic + active * (1.0 - logistic))
            )
            gain_grad_ref[:1] += jnp.sum(through * active, axis=0, keepdims=True)
            weighted = gated_grad * active * gain
            grad = scale_ref[rows, slice(head, head + 1)] * (
                weighted - unit * jnp.mean(weighted * unit, axis=1, keepdims=True)
            )
            grad_ref[rows, vals] = low(grad)
            share = tn(low(jnp.where(inside, grad, 0.0)), query)
            acc_ref[i] = share

            @pl.when(place == 0)
            def _():
                right_out[i] = low(share)
                if count > 1:
                    to_right(i).start()

            later = low(jnp.where(inside, 0.0, grad))
            for chunk in range(chunks):
                at = slice(chunk * CHUNK, (chunk + 1) * CHUNK)
                piece, total, middle = chunk_parts(cum, chunk)
                local_ref[i, chunk] = tn(later[at], low(wide(query[at]) * jnp.exp(piece)))
        return carry

    gain_grad_ref[...] = jnp.zeros_like(gain_grad_ref)
    lax.fori_loop(0, seqs, shares_of, 0)

    def local_of(seq, carry):
        rows = pl.ds(pl.multiple_of(seq * toks, toks), toks)
        end_local = prefix_ref[seq] - 1 - place * toks
        inside = iota((toks, HEAD_V), 0) <= end_local
        inside_keys = iota((toks, HEAD_K), 0) <= end_local
        at_end = iota((toks, HEAD_K), 0) == end_local
        for head in range(HEADS):
            i = seq * HEADS + head
            keys = slice(head * HEAD_K, (head + 1) * HEAD_K)
            vals = slice(head * HEAD_V, (head + 1) * HEAD_V)
            cum = cum_ref[rows, keys]
            query = wide(proj_ref[rows, query_columns(head)])
            key = wide(proj_ref[rows, key_columns(head)])
            value = proj_ref[rows, value_columns(head)]
            grad = wide(grad_ref[rows, vals])
            later = low(jnp.where(inside, 0.0, grad))
            weights, edge = prefix_weights(cum, end_local, toks)
            prefix_state = prefix_state_ref[i]

            @pl.when(place == 0)
            def _():
                right_in[i] = jnp.zeros((HEAD_V, HEAD_K), jnp.bfloat16)

            @pl.when(place > 0)
            def _():
                send(right_out.at[i], right_in.at[i], right_sent.at[i], right_got.at[i], axes, place - 1).wait_recv()

            acc = acc_ref[i] + wide(right_in[i])
            narrow_acc = low(acc)

            @pl.when(jnp.logical_and(place > 0, place < count - 1))
            def _():
                right_out[i] = narrow_acc
                to_right(i).start()

            local = jnp.zeros((HEAD_V, HEAD_K), jnp.float32)
            starts = []
            for chunk in reversed(range(chunks)):
                piece, total, middle = chunk_parts(cum, chunk)
                starts.append(local)
                local = jnp.exp(total) * local + local_ref[i, chunk]
            starts = starts[::-1]
            local = local + edge * acc
            acc_ref[i] = local
            if count > 1:

                @pl.when(place == count - 1)
                def _():
                    left_out[i] = low(local)
                    to_left(i).start()

            weighted = low(key * weights)
            dk_all = weights * nn(value, narrow_acc)
            dv_all = nt(weighted, narrow_acc)
            dq_all = nn(low(jnp.where(inside, grad, 0.0)), prefix_state)
            dqs, dks, dvs, dcs = [], [], [], []
            for chunk in range(chunks):
                at = slice(chunk * CHUNK, (chunk + 1) * CHUNK)
                piece, total, middle = chunk_parts(cum, chunk)
                rise = jnp.exp(piece - middle)
                fall = jnp.exp(middle - piece)
                q_in = low(query[at] * rise)
                k_in = low(key[at] * fall)
                scores = low(jnp.where(causal, nt(q_in, k_in), 0.0))
                d_scores = low(jnp.where(causal, nt(later[at], value[at]), 0.0))
                dq_in = nn(d_scores, k_in)
                dk_in = tn(d_scores, q_in)
                dq_state = jnp.exp(piece) * nn(later[at], state_ref[i, chunk])
                to_end = jnp.exp(total - piece)
                after = low(starts[chunk])
                dk_state = to_end * nn(value[at], after) + dk_all[at]
                dv = tn(scores, later[at]) + dv_all[at]
                if chunk < chunks - 1:
                    dv = dv + nt(low(key[at] * to_end), after)
                dqs.append(rise * dq_in + dq_state + dq_all[at])
                dks.append(fall * dk_in + dk_state)
                dvs.append(dv)
                dcs.append(
                    wide(q_in) * dq_in
                    - wide(k_in) * dk_in
                    + query[at] * dq_state
                    - key[at] * dk_state
                )
            dproj_ref[rows, query_columns(head)] = low(jnp.concatenate(dqs, axis=0))
            dk_part[rows, keys] = jnp.concatenate(dks, axis=0)
            dv_part[rows, vals] = jnp.concatenate(dvs, axis=0)
            turn = jnp.sum(wide(narrow_acc) * wide(prefix_state), axis=0, keepdims=True)
            dcum_part[rows, keys] = jnp.concatenate(dcs, axis=0) + jnp.where(at_end, turn, 0.0)
        return carry

    lax.fori_loop(0, seqs, local_of, 0)

    def rest_of(seq, carry):
        rows = pl.ds(pl.multiple_of(seq * toks, toks), toks)
        for head in range(HEADS):
            i = seq * HEADS + head
            keys = slice(head * HEAD_K, (head + 1) * HEAD_K)
            vals = slice(head * HEAD_V, (head + 1) * HEAD_V)
            cum = cum_ref[rows, keys]
            key = wide(proj_ref[rows, key_columns(head)])
            value = proj_ref[rows, value_columns(head)]

            @pl.when(place < count - 1)
            def _():
                send(left_out.at[i], left_in.at[i], left_sent.at[i], left_got.at[i], axes, place + 1).wait_recv()

            @pl.when(place == count - 1)
            def _():
                left_in[i] = jnp.zeros((HEAD_V, HEAD_K), jnp.bfloat16)

            after = left_in[i]
            last = cum[toks - 1 :]

            @pl.when(jnp.logical_and(place > 0, place < count - 1))
            def _():
                left_out[i] = low(jnp.exp(last) * wide(after) + acc_ref[i])
                to_left(i).start()

            to_end = jnp.exp(last - cum)
            dk_more = to_end * nn(value, after)
            dproj_ref[rows, key_columns(head)] = low(
                dk_part[rows, keys] + dk_more
            )
            dproj_ref[rows, value_columns(head)] = low(
                dv_part[rows, vals] + nt(low(key * to_end), after)
            )
            carry_row = jnp.sum(wide(after) * wide(state_ref[i, chunks]), axis=0, keepdims=True)
            dcum = dcum_part[rows, keys] - key * dk_more
            ddecay_ref[rows, keys] = three_way(upper, dcum) + carry_row
        return carry

    lax.fori_loop(0, seqs, rest_of, 0)

    def finish(i, carry):
        @pl.when(place < count - 1)
        def _():
            to_right(i).wait_send()

        @pl.when(place > 0)
        def _():
            to_left(i).wait_send()

        return carry

    lax.fori_loop(0, seqs * HEADS, finish, 0)


def line_scratch(pieces):
    block = pltpu.VMEM((pieces, HEAD_V, HEAD_K), jnp.bfloat16)
    return [block] * 4 + [pltpu.SemaphoreType.DMA((pieces,))] * 4


def whole_specs(count):
    return [pl.BlockSpec(memory_space=pltpu.VMEM)] * count


def mix_forward(axes, prefix_len, projected, decays, group_gain):
    tokens = projected.shape[0]
    seqs = prefix_len.shape[0]
    heads = seqs * HEADS
    chunks = tokens // seqs // CHUNK
    state = (heads, HEAD_V, HEAD_K)
    return pl.pallas_call(
        partial(forward_kernel, axes),
        out_shape=(
            jax.ShapeDtypeStruct((tokens, VALS), jnp.bfloat16),
            jax.ShapeDtypeStruct((tokens, VALS), jnp.bfloat16),
            jax.ShapeDtypeStruct((tokens, 128), jnp.float32),
            jax.ShapeDtypeStruct((tokens, KEYS), jnp.float32),
            jax.ShapeDtypeStruct((heads, chunks + 1, HEAD_V, HEAD_K), jnp.bfloat16),
            jax.ShapeDtypeStruct(state, jnp.bfloat16),
        ),
        in_specs=[pl.BlockSpec(memory_space=pltpu.SMEM)] + whole_specs(3),
        out_specs=tuple(whole_specs(6)),
        scratch_shapes=[
            pltpu.VMEM((tokens, VALS), jnp.float32),
            pltpu.VMEM((heads, chunks, HEAD_V, HEAD_K), jnp.float32),
            pltpu.VMEM(state, jnp.float32),
            pltpu.VMEM((heads, 8, HEAD_K), jnp.float32),
            *line_scratch(heads),
        ],
        compiler_params=pltpu.CompilerParams(
            collective_id=1, has_side_effects=True, vmem_limit_bytes=50 * 2**20
        ),
        cost_estimate=pl.CostEstimate(
            flops=60_000_000_000, bytes_accessed=220_000_000, transcendentals=0
        ),
        name="mix_forward",
    )(prefix_len, projected, decays, group_gain)


def mix_backward(
    axes, prefix_len, projected, cum, states, prefix_state, gated_grad, unit, scale, group_gain
):
    tokens = projected.shape[0]
    seqs = prefix_len.shape[0]
    pieces = seqs * HEADS
    chunks = tokens // seqs // CHUNK
    state = (pieces, HEAD_V, HEAD_K)
    return pl.pallas_call(
        partial(backward_kernel, axes),
        out_shape=(
            jax.ShapeDtypeStruct(projected.shape, jnp.bfloat16),
            jax.ShapeDtypeStruct((tokens, KEYS), jnp.float32),
            jax.ShapeDtypeStruct((8, HEAD_V), jnp.float32),
        ),
        in_specs=[pl.BlockSpec(memory_space=pltpu.SMEM)] + whole_specs(8),
        out_specs=tuple(whole_specs(3)),
        scratch_shapes=[
            pltpu.VMEM((tokens, VALS), jnp.bfloat16),
            pltpu.VMEM((pieces, chunks, HEAD_V, HEAD_K), jnp.float32),
            pltpu.VMEM(state, jnp.float32),
            pltpu.VMEM((tokens, KEYS), jnp.float32),
            pltpu.VMEM((tokens, VALS), jnp.float32),
            pltpu.VMEM((tokens, KEYS), jnp.float32),
            *line_scratch(pieces),
        ],
        compiler_params=pltpu.CompilerParams(
            collective_id=2, has_side_effects=True, vmem_limit_bytes=56 * 2**20
        ),
        cost_estimate=pl.CostEstimate(
            flops=60_000_000_000, bytes_accessed=220_000_000, transcendentals=0
        ),
        name="mix_backward",
    )(
        prefix_len,
        projected,
        cum,
        states,
        prefix_state,
        gated_grad,
        unit,
        scale,
        group_gain,
    )


EXTRA = 128


def physical_axes(mesh):
    shape = mesh.devices.shape
    names = []
    sizes = []
    for axis, extent in enumerate(shape):
        line = np.moveaxis(mesh.devices, axis, 0).reshape(extent, -1)[:, 0]
        places = [tuple(d.coords) + (d.core_on_chip,) for d in line]
        parts = []
        for dim, label in enumerate(("x", "y", "z", "core")):
            values = [p[dim] for p in places]
            if len(set(values)) > 1:
                step = next(i for i in range(extent) if values[i] != values[0])
                parts.append((step, label, len(set(values))))
        for step, label, size in sorted(parts, reverse=True):
            names.append(label)
            sizes.append(size)
    return tuple(names), tuple(sizes)


def pack_small(norm1_gain, norm2_gain, down, up, bias, group):
    rows = down.shape[0]

    def column(vector):
        return jnp.pad(vector, (0, rows - vector.shape[0]))[:, None]

    pieces = [
        down,
        column(norm1_gain),
        column(norm2_gain),
        column(bias),
        column(group),
        jnp.zeros((rows, 4), down.dtype),
        up.T.reshape(rows, 8),
        jnp.zeros((rows, EXTRA - 32), down.dtype),
    ]
    return jnp.concatenate(pieces, axis=1)


def unpack_small(small, devices):
    rows = small.shape[0] // devices
    by_device = small.reshape(devices, rows, EXTRA)
    down = small[:, :16]
    gain_one = small[:, 16]
    gain_two = small[:, 17]
    bias = by_device[:, : KEYS // devices, 18].reshape(KEYS)
    group = by_device[:, : HEAD_V // devices, 19].reshape(HEAD_V)
    up = small[:, 24:32].reshape(KEYS, 16).T
    return down, gain_one, gain_two, bias, group, up


def pack_small_grads(down, gain_one, gain_two, bias, group, up, devices):
    rows = gain_one.shape[0] // devices

    def column(vector):
        parts = vector.reshape(devices, -1)
        parts = jnp.pad(parts, ((0, 0), (0, rows - parts.shape[1])))
        return parts.reshape(devices * rows, 1)

    pieces = [
        down,
        gain_one[:, None],
        gain_two[:, None],
        column(bias),
        column(group),
        jnp.zeros((rows * devices, 4), jnp.float32),
        up.T.reshape(rows * devices, 8),
        jnp.zeros((rows * devices, EXTRA - 32), jnp.float32),
    ]
    return jnp.concatenate(pieces, axis=1)


def core_halves(rows, names, sizes):
    width = rows.shape[1]
    at = names.index("core")
    before = int(np.prod(sizes[:at], initial=1))
    after = width // before // sizes[at]
    core = lax.axis_index("core")

    def half(which):
        return jnp.concatenate(
            [
                lax.dynamic_slice_in_dim(rows, (2 * i + which) * after, after, 1)
                for i in range(before)
            ],
            axis=1,
        )

    return half(core), half(1 - core)


def swap_cores(values):
    return lax.ppermute(values, "core", [(0, 1), (1, 0)])


def pair_sum(halves, gradient):
    mine, other = halves
    taken = swap_cores(flat_grad(other, gradient).astype(jnp.bfloat16))
    return (flat_grad(mine, gradient) + taken.astype(jnp.float32)).astype(jnp.bfloat16)


def flat_grad(inputs, gradient):
    return jnp.einsum("td,te->de", inputs, gradient, preferred_element_type=jnp.float32)


def by_chip(values, names, sizes):
    chips = tuple(size for name, size in zip(names, sizes) if name != "core")
    return values.reshape(*chips, -1, values.shape[-1])


def pass_along(values, left, name):
    at = left.index(name)
    size = values.shape[at]
    own = lax.axis_index(name)
    arrived = []
    for shift in range(1, size):
        given = lax.dynamic_index_in_dim(values, lax.rem(own + shift, size), at, False)
        arrived.append(
            lax.ppermute(given, name, [(i, (i + shift) % size) for i in range(size)])
        )
    return arrived


def take_in(values, arrived, left, name):
    at = left.index(name)
    total = lax.dynamic_index_in_dim(values, lax.axis_index(name), at, False).astype(jnp.float32)
    for term in arrived:
        total = total + term.astype(jnp.float32)
    return total, [other for other in left if other != name]


def reduce_kernel(plan, *refs):
    inputs, jobs, sizes, slots = plan
    count = len(jobs)
    in_refs = refs[:inputs]
    outputs = max(job[4] for job in jobs) + 1
    out_refs = refs[inputs : inputs + outputs]
    scratch = refs[inputs + outputs :]
    send_sem, recv_sem = scratch[-2:]
    scratch = list(scratch[:-2])

    reached = sorted({name for job in jobs for name in job[3]})
    barrier = pltpu.get_barrier_semaphore()
    peers = 0
    for name in reached:
        for shift in range(1, sizes[name]):
            peer = lax.rem(lax.axis_index(name) + shift, sizes[name])
            pl.semaphore_signal(barrier, inc=1, device_id={name: peer}, device_id_type=MESH)
            peers += 1
    pl.semaphore_wait(barrier, peers)

    class Job:
        pass

    work = []
    slot = 0
    for which, columns, axes, order, out, out_columns in jobs:
        job = Job()
        job.left = list(axes)
        job.order = order
        job.out = out_refs[out]
        job.out_columns = slice(*out_columns)
        job.source = in_refs[which]
        job.columns = slice(*columns)
        job.got = [scratch.pop(0) for _ in order]
        job.kept = [scratch.pop(0) for _ in order[:-1]]
        job.slots = []
        for name in order:
            job.slots.append(slot)
            slot += sizes[name] - 1
        work.append(job)

    def part(job, index):
        at = job.left.index(job.order[job.step])
        lead = [slice(None)] * len(job.left)
        lead[at] = index
        return job.source.at[(*lead, slice(None), job.columns)]

    def copies(job):
        name = job.order[job.step]
        own = lax.axis_index(name)
        for shift in range(1, sizes[name]):
            peer = lax.rem(own + shift, sizes[name])
            at = job.slots[job.step] + shift - 1
            yield pltpu.make_async_remote_copy(
                src_ref=part(job, peer),
                dst_ref=job.got[job.step].at[shift - 1],
                send_sem=send_sem.at[at],
                recv_sem=recv_sem.at[at],
                device_id={name: peer},
                device_id_type=MESH,
            )

    def start(job):
        for copy in copies(job):
            copy.start()

    def add(job):
        name = job.order[job.step]
        at = job.left.index(name)
        own = lax.axis_index(name)
        rest = [n for n in job.left if n != name]
        last = job.step == len(job.order) - 1
        total = int(np.prod([sizes[n] for n in rest], initial=1))
        got = job.got[job.step]
        for copy in copies(job):
            copy.wait()
        source, columns, step = job.source, job.columns, job.step

        def one(i, carry):
            index = []
            for n in reversed(rest):
                index.insert(0, lax.rem(i, sizes[n]))
                i = lax.div(i, sizes[n])
            lead = list(index)
            lead.insert(at, own)
            value = source[(*lead, slice(None), columns)].astype(jnp.float32)
            for shift in range(1, sizes[name]):
                value = value + got[(shift - 1, *index)].astype(jnp.float32)
            if last:
                job.out[:, job.out_columns] = value
            else:
                job.kept[step][tuple(index)] = value.astype(jnp.bfloat16)
            return carry

        if total == 1:
            one(jnp.int32(0), 0)
        else:
            lax.fori_loop(0, total, one, 0)
        job.left = rest
        if not last:
            job.source = job.kept[step]
            job.columns = slice(None)
            job.step += 1
            start(job)

    for job in work:
        job.step = 0
        start(job)
    for step in range(max(len(job.order) for job in work)):
        for job in work:
            if len(job.order) > step:
                add(job)


def reduce_rest(arrays, jobs, sizes, rows, widths, collective):
    scratch = []
    slots = 0
    for which, (begin, end), axes, order, out, out_columns in jobs:
        left = list(axes)
        kept = []
        got = []
        for name in order:
            left.remove(name)
            shape = tuple(sizes[n] for n in left)
            got.append(pltpu.VMEM((sizes[name] - 1, *shape, rows, end - begin), jnp.bfloat16))
            kept.append(pltpu.VMEM((*shape, rows, end - begin), jnp.bfloat16))
            slots += sizes[name] - 1
        scratch += got + kept[:-1]
    scratch += [pltpu.SemaphoreType.DMA((slots,))] * 2
    return pl.pallas_call(
        partial(reduce_kernel, (len(arrays), jobs, sizes, slots)),
        out_shape=tuple(jax.ShapeDtypeStruct((rows, width), jnp.float32) for width in widths),
        in_specs=whole_specs(len(arrays)),
        out_specs=tuple(whole_specs(len(widths))),
        scratch_shapes=scratch,
        compiler_params=pltpu.CompilerParams(
            collective_id=collective, has_side_effects=True, vmem_limit_bytes=40 * 2**20
        ),
        name="reduce_rest",
    )(*arrays)


def chip_orders(names):
    first, second, last = [name for name in names if name != "core"]
    return (first, second, last), (second, last, first), (last, first, second)


def two_orders(names):
    first, second, last = [name for name in names if name != "core"]
    return (first, second, last), (second, last, first)


def last_orders(names):
    first, second, last = [name for name in names if name != "core"]
    return (first, second, last), (second, first, last)


def local(
    names,
    sizes,
    seq_axes,
    tokens,
    prefix_len,
    norm1_gain,
    query_weight,
    key_weight,
    value_weight,
    gate_weight,
    decay_down,
    decay_up,
    decay_bias,
    group_gain,
    out_weight,
    norm2_gain,
    ffn_gate,
    ffn_up,
    ffn_down,
    out_grad,
):
    devices = int(np.prod(sizes))
    orders = chip_orders(names)
    wide_order, long_order, late_order = (order[::-1] for order in orders)
    small_shard = pack_small(norm1_gain, norm2_gain, decay_down, decay_up, decay_bias, group_gain)
    first, small_full = gather_first(
        names,
        sizes,
        (query_weight, key_weight, value_weight, gate_weight, small_shard),
        (3072, EXTRA),
        (
            (3, 0, (0, 1024), (2048, 3072), wide_order),
            (4, 1, (0, EXTRA), (0, EXTRA), wide_order),
            (0, 0, (0, 128), (0, 128), wide_order),
            (2, 0, (0, 1024), (1024, 2048), long_order),
            (0, 0, (128, 384), (128, 384), long_order),
            (1, 0, (0, 512), (512, 1024), late_order),
            (0, 0, (384, 512), (384, 512), late_order),
        ),
    )
    ffn_shard = jnp.concatenate([ffn_gate, ffn_up, ffn_down.T, out_weight], axis=1)
    ffn_full = lax.all_gather(ffn_shard, names, axis=0, tiled=True)
    weight_gate = ffn_full[:, :FF]
    weight_upper = ffn_full[:, FF : 2 * FF]
    weight_lower = ffn_full[:, 2 * FF : 3 * FF].T
    weight_o = ffn_full[:, 3 * FF :]
    mixer_full = first.reshape(-1, 3072)
    small_full = small_full.reshape(-1, EXTRA)
    weight_down, gain_one, gain_two, bias_full, gain_group, weight_up = unpack_small(
        small_full, devices
    )
    seq_count, tok_count, feature_count = tokens.shape
    rows = seq_count * tok_count
    resid_in = tokens.reshape(rows, feature_count).astype(jnp.float32)
    scale_one = rms_scale(resid_in)
    unit_one = resid_in * scale_one
    normed = (unit_one * gain_one.astype(jnp.float32)).astype(jnp.bfloat16)
    projected = project(normed, mixer_full).astype(jnp.bfloat16)
    lowrank = project(normed, weight_down).astype(jnp.bfloat16)
    logits = project(lowrank, weight_up) + bias_full.astype(jnp.float32)
    decays = jax.nn.log_sigmoid(logits) / 16.0
    wide_gain = jnp.broadcast_to(gain_group.astype(jnp.float32)[None], (8, HEAD_V))
    gated_rows, unit_group, scale_group, cum, states, prefix_state = mix_forward(
        seq_axes, prefix_len, projected, decays, wide_gain
    )
    resid_mid = resid_in + project(gated_rows, weight_o)
    scale_two = rms_scale(resid_mid)
    unit_two = resid_mid * scale_two
    normed_two = (unit_two * gain_two.astype(jnp.float32)).astype(jnp.bfloat16)
    gate_part = project(normed_two, weight_gate)
    up_part = project(normed_two, weight_upper)
    gate_act = jax.nn.silu(gate_part)
    hidden = (gate_act * up_part).astype(jnp.bfloat16)
    ffn_out = project(hidden, weight_lower)
    layer_out = (resid_mid + ffn_out).astype(jnp.bfloat16)
    out_grad = out_grad.reshape(rows, feature_count)
    grad_out = out_grad.astype(jnp.float32)
    grad_hidden = back_project(out_grad, weight_lower)
    grad_gate = (grad_hidden * up_part * silu_slope(gate_part)).astype(jnp.bfloat16)
    grad_up = (grad_hidden * gate_act).astype(jnp.bfloat16)
    grad_normed_two = back_project(grad_gate, weight_gate) + back_project(grad_up, weight_upper)
    gain_two_grad = jnp.sum(grad_normed_two * unit_two, axis=0)
    grad_mid = grad_out + rms_back(
        grad_normed_two * gain_two.astype(jnp.float32), unit_two, scale_two
    )
    grad_branch = grad_mid.astype(jnp.bfloat16)
    gated_grad = back_project(grad_branch, weight_o).astype(jnp.bfloat16)
    two_halves = core_halves(normed_two, names, sizes)
    gate_sum = pair_sum(two_halves, grad_gate)
    up_sum = pair_sum(two_halves, grad_up)
    down_sum = pair_sum(core_halves(out_grad, names, sizes), hidden)
    out_sum = pair_sum(core_halves(gated_rows, names, sizes), grad_branch)
    groups = (
        jnp.concatenate([gate_sum, out_sum, down_sum[:, :896]], axis=1),
        jnp.concatenate([up_sum, down_sum[:, 896:]], axis=1),
    )
    groups, gated_grad = lax.optimization_barrier((groups, gated_grad))
    chips = [name for name in names if name != "core"]
    orders = two_orders(names)
    lefts = [chips] * 2
    groups = [by_chip(group, names, sizes) for group in groups]
    arrived = [pass_along(g, left, order[0]) for g, left, order in zip(groups, lefts, orders)]
    grad_projected, grad_decay, group_grad = mix_backward(
        seq_axes,
        prefix_len,
        projected,
        cum,
        states,
        prefix_state,
        gated_grad,
        unit_group,
        scale_group,
        wide_gain,
    )
    arrived, grad_projected, grad_decay = lax.optimization_barrier(
        (arrived, grad_projected, grad_decay)
    )
    taken = [
        take_in(g, more, left, order[0])
        for g, more, left, order in zip(groups, arrived, lefts, orders)
    ]
    groups = [total.astype(jnp.bfloat16) for total, _ in taken]
    lefts = [left for _, left in taken]
    arrived = [pass_along(g, left, order[1]) for g, left, order in zip(groups, lefts, orders)]
    late = flat_grad(normed, grad_projected).astype(jnp.bfloat16)
    grad_logits = (grad_decay * jax.nn.sigmoid(-logits) / 16.0).astype(jnp.bfloat16)
    bias_grad = jnp.sum(grad_logits.astype(jnp.float32), axis=0)
    up_rank_grad = flat_grad(lowrank, grad_logits)
    grad_lowrank = back_project(grad_logits, weight_up).astype(jnp.bfloat16)
    down_rank_grad = flat_grad(normed, grad_lowrank)
    grad_normed = back_project(grad_projected, mixer_full) + back_project(
        grad_lowrank, weight_down
    )
    gain_one_grad = jnp.sum(grad_normed * unit_one, axis=0)
    tokens_grad = grad_mid + rms_back(
        grad_normed * gain_one.astype(jnp.float32), unit_one, scale_one
    )
    small_grads = pack_small_grads(
        down_rank_grad,
        gain_one_grad,
        gain_two_grad,
        bias_grad,
        group_grad[0],
        up_rank_grad,
        devices,
    ).astype(jnp.bfloat16)
    arrived, late, small_grads, tokens_grad = lax.optimization_barrier(
        (arrived, late, small_grads, tokens_grad)
    )
    groups = [
        take_in(g, more, left, order[1])[0].astype(jnp.bfloat16)
        for g, more, left, order in zip(groups, arrived, lefts, orders)
    ]
    own_rows = feature_count // devices
    late = late.reshape(*sizes, own_rows, -1)
    small_grads = small_grads.reshape(*sizes, own_rows, -1)
    size_of = dict(zip(names, sizes))
    ends = last_orders(names)
    jobs = [
        (which, columns, names, ("core", *order), which, columns)
        for which, columns, order in (
            (2, (0, 1536), ends[0]),
            (2, (1536, 3072), ends[1]),
            (3, (0, EXTRA), ends[0]),
        )
    ] + [
        (i, (0, groups[i].shape[-1]), (order[2],), (order[2],), i, (0, groups[i].shape[-1]))
        for i, order in enumerate(orders)
    ]
    first_group, second_group, mine, small = reduce_rest(
        (*groups, late, small_grads), jobs, size_of, own_rows, (4736, 4736, 3072, EXTRA), 3
    )
    shape = tokens.shape
    return (
        layer_out.reshape(shape),
        tokens_grad.reshape(shape),
        small[:, 16],
        mine[:, :512],
        mine[:, 512:1024],
        mine[:, 1024:2048],
        mine[:, 2048:],
        small[:, :16],
        small[:, 24:32].reshape(KEYS // devices, 16).T,
        small[: KEYS // devices, 18],
        small[: HEAD_V // devices, 19],
        first_group[:, FF : FF + VALS],
        small[:, 17],
        first_group[:, :FF],
        second_group[:, :FF],
        jnp.concatenate([first_group[:, FF + VALS :], second_group[:, FF:]], axis=1).T,
    )


def solution(mesh):
    names, sizes = physical_axes(mesh)
    cut = next(
        i for i in range(len(sizes) + 1) if np.prod(sizes[:i], initial=1) == mesh.shape["dp"]
    )
    dp, seq = names[:cut], names[cut:]
    split = Mesh(mesh.devices.reshape(sizes), names)
    return jax.shard_map(
        partial(local, names, sizes, tuple(zip(seq, sizes[cut:]))),
        mesh=split,
        in_specs=(
            P(dp, seq, None),
            P(dp),
            P(names),
            P(names, None),
            P(names, None),
            P(names, None),
            P(names, None),
            P(names, None),
            P(None, names),
            P(names),
            P(names),
            P(names, None),
            P(names),
            P(names, None),
            P(names, None),
            P(None, names),
            P(dp, seq, None),
        ),
        out_specs=(
            P(dp, seq, None),
            P(dp, seq, None),
            P(names),
            P(names, None),
            P(names, None),
            P(names, None),
            P(names, None),
            P(names, None),
            P(None, names),
            P(names),
            P(names),
            P(names, None),
            P(names),
            P(names, None),
            P(names, None),
            P(None, names),
        ),
        check_vma=False,
    )
```

```python
from functools import partial

import jax
import jax.numpy as jnp
import numpy as np
from jax import lax
from jax.experimental import pallas as pl
from jax.experimental.pallas import tpu as pltpu
from jax.sharding import Mesh
from jax.sharding import PartitionSpec as P

KEYS = 512
VALS = 1024
HEADS = 4
SPAN = 64
HEAD_K = 128
HEAD_V = 256
FF = 2816


norm_eps = 1e-05


def project(inputs, weight):
    return jnp.einsum("td,de->te", inputs, weight, preferred_element_type=jnp.float32)


def back_project(gradient, weight):
    return jnp.einsum("te,de->td", gradient, weight, preferred_element_type=jnp.float32)


def rms_scale(values):
    return lax.rsqrt(jnp.mean(values * values, axis=-1, keepdims=True) + norm_eps)


def rms_back(grad_unit, unit_rows, scale_rows):
    return scale_rows * (
        grad_unit - unit_rows * jnp.mean(grad_unit * unit_rows, axis=-1, keepdims=True)
    )


CHUNK = 128
MESH = pl.DeviceIdType.MESH


def nn(a, b):
    return lax.dot_general(a, b, (((1,), (0,)), ((), ())), preferred_element_type=jnp.float32)


def nt(a, b):
    return lax.dot_general(a, b, (((1,), (1,)), ((), ())), preferred_element_type=jnp.float32)


def tn(a, b):
    return lax.dot_general(a, b, (((0,), (0,)), ((), ())), preferred_element_type=jnp.float32)


def low(values):
    return values.astype(jnp.bfloat16)


def wide(values):
    return values.astype(jnp.float32)


def three_way(ones, values):
    first = low(values)
    left = values - wide(first)
    second = low(left)
    third = low(left - wide(second))
    return nn(ones, first) + nn(ones, second) + nn(ones, third)


def iota(shape, dim):
    return lax.broadcasted_iota(jnp.int32, shape, dim)


def place_on(axes):
    place = 0
    for name, size in axes:
        place = place * size + lax.axis_index(name)
    return place


def device_at(axes, place):
    where = {}
    for name, size in reversed(axes):
        where[name] = lax.rem(place, size)
        place = lax.div(place, size)
    return where


def line_length(axes):
    return int(np.prod([size for _, size in axes]))


def greet(axes, place, count, extra=0):
    barrier = pltpu.get_barrier_semaphore()

    @pl.when(place > 0)
    def _():
        pl.semaphore_signal(
            barrier, inc=1, device_id=device_at(axes, place - 1), device_id_type=MESH
        )

    @pl.when(place < count - 1)
    def _():
        pl.semaphore_signal(
            barrier, inc=1, device_id=device_at(axes, place + 1), device_id_type=MESH
        )

    @pl.when(jnp.logical_or(place == 0, place == count - 1))
    def _():
        pl.semaphore_wait(barrier, 1 + extra)

    @pl.when(jnp.logical_and(place > 0, place < count - 1))
    def _():
        pl.semaphore_wait(barrier, 2 + extra)


def send(source, target, send_sem, recv_sem, axes, place):
    return pltpu.make_async_remote_copy(
        src_ref=source,
        dst_ref=target,
        send_sem=send_sem,
        recv_sem=recv_sem,
        device_id=device_at(axes, place),
        device_id_type=MESH,
    )


class Gather:
    def __init__(self, names, sizes, pieces, local_sem, send_sem, recv_sem, pair_send, pair_recv):
        self.names = names
        self.sizes = dict(zip(names, sizes))
        self.pieces = pieces
        self.sems = local_sem, send_sem, recv_sem, pair_send, pair_recv
        self.steps = len(pieces[0][4])

    def region(self, piece, known, at):
        lead = []
        for name in self.names:
            if name in known:
                lead.append(slice(None))
            elif name in at:
                lead.append(at[name])
            else:
                lead.append(lax.axis_index(name))
        _, whole, _, columns, _ = piece
        return whole.at[(*lead, slice(None), slice(*columns))]

    def local(self, i):
        shard, _, columns, _, _ = self.pieces[i]
        return pltpu.make_async_copy(
            shard.at[:, slice(*columns)], self.region(self.pieces[i], (), {}), self.sems[0].at[i]
        )

    def copies(self, i, step):
        piece = self.pieces[i]
        order = piece[4]
        name = order[step]
        own = lax.axis_index(name)
        base = (i * self.steps + step) * 3
        for shift in range(1, self.sizes[name]):
            peer = lax.rem(own + shift, self.sizes[name])
            here = self.region(piece, order[:step], {})
            yield pltpu.make_async_remote_copy(
                src_ref=here,
                dst_ref=here,
                send_sem=self.sems[1].at[base + shift - 1],
                recv_sem=self.sems[2].at[base + shift - 1],
                device_id={name: peer},
                device_id_type=MESH,
            )

    def pair(self, i, step, shift):
        piece = self.pieces[i]
        order = piece[4]
        if step < 0:
            here = self.region(piece, (), {})
            at = 0
        else:
            name = order[step]
            source = lax.rem(lax.axis_index(name) + self.sizes[name] - shift, self.sizes[name])
            here = self.region(piece, order[:step], {name: source})
            at = 1 + step * 3 + shift - 1
        at += i * (1 + 3 * self.steps)
        return pltpu.make_async_remote_copy(
            src_ref=here,
            dst_ref=here,
            send_sem=self.sems[3].at[at],
            recv_sem=self.sems[4].at[at],
            device_id={"core": 1 - lax.axis_index("core")},
            device_id_type=MESH,
        )

    def begin(self):
        for i in range(len(self.pieces)):
            self.local(i).start()
        for i in range(len(self.pieces)):
            self.local(i).wait()
            for copy in self.copies(i, 0):
                copy.start()
            self.pair(i, -1, 0).start()

    def advance(self, step):
        for i, piece in enumerate(self.pieces):
            for copy in self.copies(i, step):
                copy.wait_recv()
            if step < self.steps - 1:
                for copy in self.copies(i, step + 1):
                    copy.start()
            for shift in range(1, self.sizes[piece[4][step]]):
                self.pair(i, step, shift).start()

    def end(self):
        for i, piece in enumerate(self.pieces):
            for step in range(self.steps):
                for copy in self.copies(i, step):
                    copy.wait_send()
                for shift in range(1, self.sizes[piece[4][step]]):
                    self.pair(i, step, shift).wait()
            self.pair(i, -1, 0).wait()

    @staticmethod
    def scratch(count):
        return [
            pltpu.SemaphoreType.DMA((count,)),
            pltpu.SemaphoreType.DMA((count * 9,)),
            pltpu.SemaphoreType.DMA((count * 9,)),
            pltpu.SemaphoreType.DMA((count * 10,)),
            pltpu.SemaphoreType.DMA((count * 10,)),
        ]


def signal_axes(names, sizes):
    barrier = pltpu.get_barrier_semaphore()
    peers = 0
    for name, size in zip(names, sizes):
        for shift in range(1, size):
            peer = lax.rem(lax.axis_index(name) + shift, size)
            pl.semaphore_signal(barrier, inc=1, device_id={name: peer}, device_id_type=MESH)
            peers += 1
    return peers


def gather_kernel(plan, *refs):
    names, sizes, inputs, outputs, pieces = plan
    wholes = refs[inputs : inputs + outputs]
    peers = signal_axes(names, sizes)
    pl.semaphore_wait(pltpu.get_barrier_semaphore(), peers)
    gather = Gather(
        names,
        sizes,
        [(refs[i], wholes[o], cols, to, order) for i, o, cols, to, order in pieces],
        *refs[inputs + outputs :],
    )
    gather.begin()
    for step in range(gather.steps):
        gather.advance(step)
    gather.end()


def gather_first(names, sizes, shards, widths, pieces):
    rows = shards[0].shape[0]
    anywhere = pl.BlockSpec(memory_space=pl.ANY)
    return pl.pallas_call(
        partial(gather_kernel, (names, sizes, len(shards), len(widths), pieces)),
        out_shape=tuple(
            jax.ShapeDtypeStruct((*sizes, rows, width), jnp.bfloat16) for width in widths
        ),
        in_specs=[anywhere] * len(shards),
        out_specs=(anywhere,) * len(widths),
        scratch_shapes=Gather.scratch(len(pieces)),
        compiler_params=pltpu.CompilerParams(collective_id=4, has_side_effects=True),
        name="gather_first",
    )(*shards)


def row_places(count):
    return iota((count, HEAD_K), 0)


def prefix_weights(cum, end_local, count):
    rows = row_places(count)
    owner = jnp.logical_and(end_local >= 0, end_local < count)
    end_cum = jnp.sum(jnp.where(rows == end_local, cum, 0.0), axis=0, keepdims=True)
    keep = jnp.logical_and(rows <= end_local, rows <= jnp.where(owner, count, -1))
    weights = jnp.where(keep, jnp.exp(jnp.where(keep, end_cum - cum, 0.0)), 0.0)
    return weights, jnp.exp(end_cum) * jnp.where(owner, 1.0, 0.0)


def chunk_parts(cum, chunk):
    begin = chunk * CHUNK
    piece = cum[begin : begin + CHUNK]
    if chunk:
        piece = piece - cum[begin - 1 : begin]
    return piece, piece[CHUNK - 1 :], piece[CHUNK // 2 - 1 : CHUNK // 2]


def query_columns(head):
    return slice(head * HEAD_K, (head + 1) * HEAD_K)


def key_columns(head):
    return slice(KEYS + head * HEAD_K, KEYS + (head + 1) * HEAD_K)


def value_columns(head):
    return slice(2 * KEYS + head * HEAD_V, 2 * KEYS + (head + 1) * HEAD_V)


def gate_columns(head):
    begin = 2 * KEYS + VALS + head * HEAD_V
    return slice(begin, begin + HEAD_V)


def forward_kernel(plan, *refs):
    axes = plan
    prefix_ref, proj_ref, decay_ref, gain_ref = refs[:4]
    gated_ref, unit_ref, scale_ref, cum_ref, state_ref, prefix_state_ref = refs[4:10]
    mixed_ref, kv_ref, part_ref, edge_ref, *line = refs[10:]
    right_out, right_in, left_out, left_in, right_sent, right_got, left_sent, left_got = line
    count = line_length(axes)
    place = place_on(axes)
    seqs = prefix_ref.shape[0]
    toks = proj_ref.shape[0] // seqs
    chunks = toks // CHUNK
    greet(axes, place, count)
    lower = low(jnp.where(iota((CHUNK, CHUNK), 0) >= iota((CHUNK, CHUNK), 1), 1.0, 0.0))
    causal = iota((CHUNK, CHUNK), 0) >= iota((CHUNK, CHUNK), 1)

    def to_right(i):
        return send(right_out.at[i], right_in.at[i], right_sent.at[i], right_got.at[i], axes, place + 1)

    def to_left(i):
        return send(left_out.at[i], left_in.at[i], left_sent.at[i], left_got.at[i], axes, place - 1)

    def states_of(seq, carry):
        rows = pl.ds(pl.multiple_of(seq * toks, toks), toks)
        end_local = prefix_ref[seq] - 1 - place * toks
        for head in range(HEADS):
            i = seq * HEADS + head
            keys = slice(head * HEAD_K, (head + 1) * HEAD_K)
            vals = slice(head * HEAD_V, (head + 1) * HEAD_V)
            before = jnp.zeros((1, HEAD_K), jnp.float32)
            key = wide(proj_ref[rows, key_columns(head)])
            value = proj_ref[rows, value_columns(head)]
            decay = decay_ref[rows, keys]
            pieces = []
            local = jnp.zeros((HEAD_V, HEAD_K), jnp.float32)
            for chunk in range(chunks):
                at = slice(chunk * CHUNK, (chunk + 1) * CHUNK)
                piece = three_way(lower, decay[at])
                total = piece[CHUNK - 1 :]
                share = tn(value[at], low(key[at] * jnp.exp(total - piece)))
                kv_ref[i, chunk] = share
                local = jnp.exp(total) * local + share
                pieces.append(piece + before)
                before = before + total
            cum = jnp.concatenate(pieces, axis=0)
            cum_ref[rows, keys] = cum
            weights, edge = prefix_weights(cum, end_local, toks)
            part_ref[i] = tn(value, low(key * weights))
            edge_ref[i] = jnp.broadcast_to(edge, (8, HEAD_K))

            @pl.when(place == 0)
            def _():
                right_out[i] = low(local)
                if count > 1:
                    to_right(i).start()

        return carry

    lax.fori_loop(0, seqs, states_of, 0)

    def outputs_of(seq, carry):
        rows = pl.ds(pl.multiple_of(seq * toks, toks), toks)
        for head in range(HEADS):
            i = seq * HEADS + head
            keys = slice(head * HEAD_K, (head + 1) * HEAD_K)
            vals = slice(head * HEAD_V, (head + 1) * HEAD_V)
            cum = cum_ref[rows, keys]
            query = wide(proj_ref[rows, query_columns(head)])
            key = wide(proj_ref[rows, key_columns(head)])
            value = proj_ref[rows, value_columns(head)]
            scores = []
            for chunk in range(chunks):
                at = slice(chunk * CHUNK, (chunk + 1) * CHUNK)
                piece, total, middle = chunk_parts(cum, chunk)
                raw = nt(
                    low(query[at] * jnp.exp(piece - middle)), low(key[at] * jnp.exp(middle - piece))
                )
                scores.append(low(jnp.where(causal, raw, 0.0)))

            @pl.when(place == 0)
            def _():
                right_in[i] = jnp.zeros((HEAD_V, HEAD_K), jnp.bfloat16)

            @pl.when(place > 0)
            def _():
                send(right_out.at[i], right_in.at[i], right_sent.at[i], right_got.at[i], axes, place - 1).wait_recv()

            state = wide(right_in[i])
            part = part_ref[i] + edge_ref[i][:1] * state
            part_ref[i] = part
            for chunk in range(chunks):
                at = slice(chunk * CHUNK, (chunk + 1) * CHUNK)
                piece, total, middle = chunk_parts(cum, chunk)
                narrow = low(state)
                state_ref[i, chunk] = narrow
                output = nn(scores[chunk], value[at]) + nt(
                    low(query[at] * jnp.exp(piece)), narrow
                )
                mixed_ref[pl.ds(seq * toks + chunk * CHUNK, CHUNK), vals] = output
                state = jnp.exp(total) * state + kv_ref[i, chunk]
            state_ref[i, chunks] = low(state)

            @pl.when(jnp.logical_and(place > 0, place < count - 1))
            def _():
                right_out[i] = low(state)
                to_right(i).start()

            if count > 1:

                @pl.when(place == count - 1)
                def _():
                    left_out[i] = low(part)
                    to_left(i).start()

        return carry

    lax.fori_loop(0, seqs, outputs_of, 0)

    def prefix_of(seq, carry):
        rows = pl.ds(pl.multiple_of(seq * toks, toks), toks)
        end_local = prefix_ref[seq] - 1 - place * toks
        inside = iota((toks, HEAD_V), 0) <= end_local
        for head in range(HEADS):
            i = seq * HEADS + head
            keys = slice(head * HEAD_K, (head + 1) * HEAD_K)
            vals = slice(head * HEAD_V, (head + 1) * HEAD_V)

            @pl.when(place < count - 1)
            def _():
                send(left_out.at[i], left_in.at[i], left_sent.at[i], left_got.at[i], axes, place + 1).wait_recv()

            @pl.when(place == count - 1)
            def _():
                left_in[i] = jnp.zeros((HEAD_V, HEAD_K), jnp.bfloat16)

            whole = low(part_ref[i] + wide(left_in[i]))

            @pl.when(jnp.logical_and(place > 0, place < count - 1))
            def _():
                left_out[i] = whole
                to_left(i).start()

            prefix_state_ref[i] = whole
            mixed = jnp.where(
                inside, nt(proj_ref[rows, query_columns(head)], whole), mixed_ref[rows, vals]
            )
            scale = lax.rsqrt(jnp.mean(mixed * mixed, axis=1, keepdims=True) + norm_eps)
            unit = mixed * scale
            gate = wide(proj_ref[rows, gate_columns(head)])
            gated_ref[rows, vals] = low(unit * gain_ref[:1] * (gate / (1.0 + jnp.exp(-gate))))
            unit_ref[rows, vals] = low(unit)
            scale_ref[rows, slice(head, head + 1)] = scale
        return carry

    lax.fori_loop(0, seqs, prefix_of, 0)

    def finish(i, carry):
        @pl.when(place < count - 1)
        def _():
            to_right(i).wait_send()

        @pl.when(place > 0)
        def _():
            to_left(i).wait_send()

        return carry

    lax.fori_loop(0, seqs * HEADS, finish, 0)


def backward_kernel(
    axes,
    prefix_ref,
    proj_ref,
    cum_ref,
    state_ref,
    prefix_state_ref,
    gated_grad_ref,
    unit_ref,
    scale_ref,
    gain_ref,
    dproj_ref,
    ddecay_ref,
    gain_grad_ref,
    grad_ref,
    local_ref,
    acc_ref,
    dk_part,
    dv_part,
    dcum_part,
    right_out,
    right_in,
    left_out,
    left_in,
    right_sent,
    right_got,
    left_sent,
    left_got,
):
    count = line_length(axes)
    place = place_on(axes)
    seqs = prefix_ref.shape[0]
    toks = proj_ref.shape[0] // seqs
    chunks = toks // CHUNK
    greet(axes, place, count)
    causal = iota((CHUNK, CHUNK), 0) >= iota((CHUNK, CHUNK), 1)
    upper = low(jnp.where(iota((toks, toks), 0) <= iota((toks, toks), 1), 1.0, 0.0))

    def to_right(i):
        return send(right_out.at[i], right_in.at[i], right_sent.at[i], right_got.at[i], axes, place + 1)

    def to_left(i):
        return send(left_out.at[i], left_in.at[i], left_sent.at[i], left_got.at[i], axes, place - 1)

    def shares_of(seq, carry):
        rows = pl.ds(pl.multiple_of(seq * toks, toks), toks)
        end_local = prefix_ref[seq] - 1 - place * toks
        inside = iota((toks, HEAD_V), 0) <= end_local
        for head in range(HEADS):
            i = seq * HEADS + head
            keys = slice(head * HEAD_K, (head + 1) * HEAD_K)
            vals = slice(head * HEAD_V, (head + 1) * HEAD_V)
            cum = cum_ref[rows, keys]
            query = proj_ref[rows, query_columns(head)]
            gate = wide(proj_ref[rows, gate_columns(head)])
            logistic = 1.0 / (1.0 + jnp.exp(-gate))
            unit = wide(unit_ref[rows, vals])
            gain = gain_ref[:1]
            gated_grad = wide(gated_grad_ref[rows, vals])
            through = gated_grad * unit
            active = gate * logistic
            dproj_ref[rows, gate_columns(head)] = low(
                through * gain * (logistic + active * (1.0 - logistic))
            )
            gain_grad_ref[:1] += jnp.sum(through * active, axis=0, keepdims=True)
            weighted = gated_grad * active * gain
            grad = scale_ref[rows, slice(head, head + 1)] * (
                weighted - unit * jnp.mean(weighted * unit, axis=1, keepdims=True)
            )
            grad_ref[rows, vals] = low(grad)
            share = tn(low(jnp.where(inside, grad, 0.0)), query)
            acc_ref[i] = share

            @pl.when(place == 0)
            def _():
                right_out[i] = low(share)
                if count > 1:
                    to_right(i).start()

            later = low(jnp.where(inside, 0.0, grad))
            for chunk in range(chunks):
                at = slice(chunk * CHUNK, (chunk + 1) * CHUNK)
                piece, total, middle = chunk_parts(cum, chunk)
                local_ref[i, chunk] = tn(later[at], low(wide(query[at]) * jnp.exp(piece)))
        return carry

    gain_grad_ref[...] = jnp.zeros_like(gain_grad_ref)
    lax.fori_loop(0, seqs, shares_of, 0)

    def local_of(seq, carry):
        rows = pl.ds(pl.multiple_of(seq * toks, toks), toks)
        end_local = prefix_ref[seq] - 1 - place * toks
        inside = iota((toks, HEAD_V), 0) <= end_local
        inside_keys = iota((toks, HEAD_K), 0) <= end_local
        at_end = iota((toks, HEAD_K), 0) == end_local
        for head in range(HEADS):
            i = seq * HEADS + head
            keys = slice(head * HEAD_K, (head + 1) * HEAD_K)
            vals = slice(head * HEAD_V, (head + 1) * HEAD_V)
            cum = cum_ref[rows, keys]
            query = wide(proj_ref[rows, query_columns(head)])
            key = wide(proj_ref[rows, key_columns(head)])
            value = proj_ref[rows, value_columns(head)]
            grad = wide(grad_ref[rows, vals])
            later = low(jnp.where(inside, 0.0, grad))
            weights, edge = prefix_weights(cum, end_local, toks)
            prefix_state = prefix_state_ref[i]

            @pl.when(place == 0)
            def _():
                right_in[i] = jnp.zeros((HEAD_V, HEAD_K), jnp.bfloat16)

            @pl.when(place > 0)
            def _():
                send(right_out.at[i], right_in.at[i], right_sent.at[i], right_got.at[i], axes, place - 1).wait_recv()

            acc = acc_ref[i] + wide(right_in[i])
            narrow_acc = low(acc)

            @pl.when(jnp.logical_and(place > 0, place < count - 1))
            def _():
                right_out[i] = narrow_acc
                to_right(i).start()

            local = jnp.zeros((HEAD_V, HEAD_K), jnp.float32)
            starts = []
            for chunk in reversed(range(chunks)):
                piece, total, middle = chunk_parts(cum, chunk)
                starts.append(local)
                local = jnp.exp(total) * local + local_ref[i, chunk]
            starts = starts[::-1]
            local = local + edge * acc
            acc_ref[i] = local
            if count > 1:

                @pl.when(place == count - 1)
                def _():
                    left_out[i] = low(local)
                    to_left(i).start()

            weighted = low(key * weights)
            dk_all = weights * nn(value, narrow_acc)
            dv_all = nt(weighted, narrow_acc)
            dq_all = nn(low(jnp.where(inside, grad, 0.0)), prefix_state)
            dqs, dks, dvs, dcs = [], [], [], []
            for chunk in range(chunks):
                at = slice(chunk * CHUNK, (chunk + 1) * CHUNK)
                piece, total, middle = chunk_parts(cum, chunk)
                rise = jnp.exp(piece - middle)
                fall = jnp.exp(middle - piece)
                q_in = low(query[at] * rise)
                k_in = low(key[at] * fall)
                scores = low(jnp.where(causal, nt(q_in, k_in), 0.0))
                d_scores = low(jnp.where(causal, nt(later[at], value[at]), 0.0))
                dq_in = nn(d_scores, k_in)
                dk_in = tn(d_scores, q_in)
                dq_state = jnp.exp(piece) * nn(later[at], state_ref[i, chunk])
                to_end = jnp.exp(total - piece)
                after = low(starts[chunk])
                dk_state = to_end * nn(value[at], after) + dk_all[at]
                dv = tn(scores, later[at]) + dv_all[at]
                if chunk < chunks - 1:
                    dv = dv + nt(low(key[at] * to_end), after)
                dqs.append(rise * dq_in + dq_state + dq_all[at])
                dks.append(fall * dk_in + dk_state)
                dvs.append(dv)
                dcs.append(
                    wide(q_in) * dq_in
                    - wide(k_in) * dk_in
                    + query[at] * dq_state
                    - key[at] * dk_state
                )
            dproj_ref[rows, query_columns(head)] = low(jnp.concatenate(dqs, axis=0))
            dk_part[rows, keys] = jnp.concatenate(dks, axis=0)
            dv_part[rows, vals] = jnp.concatenate(dvs, axis=0)
            turn = jnp.sum(wide(narrow_acc) * wide(prefix_state), axis=0, keepdims=True)
            dcum_part[rows, keys] = jnp.concatenate(dcs, axis=0) + jnp.where(at_end, turn, 0.0)
        return carry

    lax.fori_loop(0, seqs, local_of, 0)

    def rest_of(seq, carry):
        rows = pl.ds(pl.multiple_of(seq * toks, toks), toks)
        for head in range(HEADS):
            i = seq * HEADS + head
            keys = slice(head * HEAD_K, (head + 1) * HEAD_K)
            vals = slice(head * HEAD_V, (head + 1) * HEAD_V)
            cum = cum_ref[rows, keys]
            key = wide(proj_ref[rows, key_columns(head)])
            value = proj_ref[rows, value_columns(head)]

            @pl.when(place < count - 1)
            def _():
                send(left_out.at[i], left_in.at[i], left_sent.at[i], left_got.at[i], axes, place + 1).wait_recv()

            @pl.when(place == count - 1)
            def _():
                left_in[i] = jnp.zeros((HEAD_V, HEAD_K), jnp.bfloat16)

            after = left_in[i]
            last = cum[toks - 1 :]

            @pl.when(jnp.logical_and(place > 0, place < count - 1))
            def _():
                left_out[i] = low(jnp.exp(last) * wide(after) + acc_ref[i])
                to_left(i).start()

            to_end = jnp.exp(last - cum)
            dk_more = to_end * nn(value, after)
            dproj_ref[rows, key_columns(head)] = low(
                dk_part[rows, keys] + dk_more
            )
            dproj_ref[rows, value_columns(head)] = low(
                dv_part[rows, vals] + nt(low(key * to_end), after)
            )
            carry_row = jnp.sum(wide(after) * wide(state_ref[i, chunks]), axis=0, keepdims=True)
            dcum = dcum_part[rows, keys] - key * dk_more
            ddecay_ref[rows, keys] = three_way(upper, dcum) + carry_row
        return carry

    lax.fori_loop(0, seqs, rest_of, 0)

    def finish(i, carry):
        @pl.when(place < count - 1)
        def _():
            to_right(i).wait_send()

        @pl.when(place > 0)
        def _():
            to_left(i).wait_send()

        return carry

    lax.fori_loop(0, seqs * HEADS, finish, 0)


def line_scratch(pieces):
    block = pltpu.VMEM((pieces, HEAD_V, HEAD_K), jnp.bfloat16)
    return [block] * 4 + [pltpu.SemaphoreType.DMA((pieces,))] * 4


def whole_specs(count):
    return [pl.BlockSpec(memory_space=pltpu.VMEM)] * count


def mix_forward(axes, prefix_len, projected, decays, group_gain):
    tokens = projected.shape[0]
    seqs = prefix_len.shape[0]
    heads = seqs * HEADS
    chunks = tokens // seqs // CHUNK
    state = (heads, HEAD_V, HEAD_K)
    return pl.pallas_call(
        partial(forward_kernel, axes),
        out_shape=(
            jax.ShapeDtypeStruct((tokens, VALS), jnp.bfloat16),
            jax.ShapeDtypeStruct((tokens, VALS), jnp.bfloat16),
            jax.ShapeDtypeStruct((tokens, 128), jnp.float32),
            jax.ShapeDtypeStruct((tokens, KEYS), jnp.float32),
            jax.ShapeDtypeStruct((heads, chunks + 1, HEAD_V, HEAD_K), jnp.bfloat16),
            jax.ShapeDtypeStruct(state, jnp.bfloat16),
        ),
        in_specs=[pl.BlockSpec(memory_space=pltpu.SMEM)] + whole_specs(3),
        out_specs=tuple(whole_specs(6)),
        scratch_shapes=[
            pltpu.VMEM((tokens, VALS), jnp.float32),
            pltpu.VMEM((heads, chunks, HEAD_V, HEAD_K), jnp.float32),
            pltpu.VMEM(state, jnp.float32),
            pltpu.VMEM((heads, 8, HEAD_K), jnp.float32),
            *line_scratch(heads),
        ],
        compiler_params=pltpu.CompilerParams(
            collective_id=1, has_side_effects=True, vmem_limit_bytes=50 * 2**20
        ),
        cost_estimate=pl.CostEstimate(
            flops=60_000_000_000, bytes_accessed=220_000_000, transcendentals=0
        ),
        name="mix_forward",
    )(prefix_len, projected, decays, group_gain)


def mix_backward(
    axes, prefix_len, projected, cum, states, prefix_state, gated_grad, unit, scale, group_gain
):
    tokens = projected.shape[0]
    seqs = prefix_len.shape[0]
    pieces = seqs * HEADS
    chunks = tokens // seqs // CHUNK
    state = (pieces, HEAD_V, HEAD_K)
    return pl.pallas_call(
        partial(backward_kernel, axes),
        out_shape=(
            jax.ShapeDtypeStruct(projected.shape, jnp.bfloat16),
            jax.ShapeDtypeStruct((tokens, KEYS), jnp.float32),
            jax.ShapeDtypeStruct((8, HEAD_V), jnp.float32),
        ),
        in_specs=[pl.BlockSpec(memory_space=pltpu.SMEM)] + whole_specs(8),
        out_specs=tuple(whole_specs(3)),
        scratch_shapes=[
            pltpu.VMEM((tokens, VALS), jnp.bfloat16),
            pltpu.VMEM((pieces, chunks, HEAD_V, HEAD_K), jnp.float32),
            pltpu.VMEM(state, jnp.float32),
            pltpu.VMEM((tokens, KEYS), jnp.float32),
            pltpu.VMEM((tokens, VALS), jnp.float32),
            pltpu.VMEM((tokens, KEYS), jnp.float32),
            *line_scratch(pieces),
        ],
        compiler_params=pltpu.CompilerParams(
            collective_id=2, has_side_effects=True, vmem_limit_bytes=56 * 2**20
        ),
        cost_estimate=pl.CostEstimate(
            flops=60_000_000_000, bytes_accessed=220_000_000, transcendentals=0
        ),
        name="mix_backward",
    )(
        prefix_len,
        projected,
        cum,
        states,
        prefix_state,
        gated_grad,
        unit,
        scale,
        group_gain,
    )


FFN_BLOCK = 256
FFN_ROWS = 512


def ffn_kernel(
    rows_ref,
    grad_ref,
    mine_ref,
    other_ref,
    grad_mine_ref,
    grad_other_ref,
    weight_ref,
    out_ref,
    drows_ref,
    gate_sum_ref,
    up_sum_ref,
    down_sum_ref,
    pair_slots,
    down_slots,
    hidden_ref,
    dpair_ref,
    turned,
    given,
    taken,
    load_sem,
    sent_sem,
    got_sem,
):
    blocks = FF // FFN_BLOCK
    tokens = rows_ref.shape[0]
    other_core = {"core": 1 - lax.axis_index("core")}
    barrier = pltpu.get_barrier_semaphore()
    pl.semaphore_signal(barrier, inc=1, device_id=other_core, device_id_type=MESH)
    pl.semaphore_wait(barrier, 1)
    first, second = slice(0, FFN_BLOCK), slice(FFN_BLOCK, 2 * FFN_BLOCK)

    def load(block, part):
        begin = pl.multiple_of(part * FF + block * FFN_BLOCK, FFN_BLOCK)
        slot = lax.rem(block, 2)
        target = down_slots.at[slot] if part == 2 else pair_slots.at[slot, :, (first, second)[part]]
        return pltpu.make_async_copy(
            weight_ref.at[:, pl.ds(begin, FFN_BLOCK)], target, load_sem.at[slot, part]
        )

    def give(block):
        return pltpu.make_async_remote_copy(
            src_ref=given.at[lax.rem(block, 2)],
            dst_ref=taken.at[block],
            send_sem=sent_sem.at[block],
            recv_sem=got_sem.at[block],
            device_id=other_core,
            device_id_type=MESH,
        )

    def take(block):
        give(block).wait_recv()
        columns = pl.ds(pl.multiple_of(block * FFN_BLOCK, FFN_BLOCK), FFN_BLOCK)
        for part, sum_ref in enumerate((gate_sum_ref, up_sum_ref, down_sum_ref)):
            at = slice(part * FFN_BLOCK, (part + 1) * FFN_BLOCK)
            sum_ref[:, columns] = low(wide(sum_ref[:, columns]) + wide(taken[block, :, at]))

    for part in range(3):
        load(0, part).start()

    def turn(i, carry):
        begin = pl.multiple_of(i * FFN_BLOCK, FFN_BLOCK)
        at = pl.ds(begin, FFN_BLOCK)
        for which, ref in enumerate((mine_ref, other_ref, grad_mine_ref, grad_other_ref)):
            turned[which, :, at] = jnp.transpose(ref[at, :])
        out_ref[at, :] = jnp.zeros((FFN_BLOCK, out_ref.shape[1]), jnp.float32)
        drows_ref[at, :] = jnp.zeros((FFN_BLOCK, out_ref.shape[1]), jnp.float32)
        return carry

    lax.fori_loop(0, tokens // FFN_BLOCK, turn, 0)

    def one(block, carry):
        slot = lax.rem(block, 2)

        @pl.when(block < blocks - 1)
        def _():
            for part in range(3):
                load(block + 1, part).start()

        @pl.when(block > 1)
        def _():
            give(block - 2).wait_send()

        for part in range(3):
            load(block, part).wait()
        columns = pl.ds(pl.multiple_of(block * FFN_BLOCK, FFN_BLOCK), FFN_BLOCK)
        for tile in range(tokens // FFN_ROWS):
            at = slice(tile * FFN_ROWS, (tile + 1) * FFN_ROWS)
            both = nn(rows_ref[at], pair_slots[slot])
            dhidden = nn(grad_ref[at], down_slots[slot])
            gate = both[:, first]
            up = both[:, second]
            logistic = 0.5 * jnp.tanh(0.5 * gate) + 0.5
            active = gate * logistic
            hidden_ref[at] = low(active * up)
            dpair_ref[at, first] = low(dhidden * up * (logistic + active * (1.0 - logistic)))
            dpair_ref[at, second] = low(dhidden * active)
        for tile in range(tokens // FFN_ROWS):
            at = slice(tile * FFN_ROWS, (tile + 1) * FFN_ROWS)
            out_ref[at] += nt(hidden_ref[at], down_slots[slot])
            drows_ref[at] += nt(dpair_ref[at], pair_slots[slot])
        given[slot, :, : 2 * FFN_BLOCK] = low(nn(turned[1], dpair_ref[...]))
        given[slot, :, 2 * FFN_BLOCK :] = low(nn(turned[3], hidden_ref[...]))
        give(block).start()
        pair = nn(turned[0], dpair_ref[...])
        gate_sum_ref[:, columns] = low(pair[:, first])
        up_sum_ref[:, columns] = low(pair[:, second])
        down_sum_ref[:, columns] = low(nn(turned[2], hidden_ref[...]))

        @pl.when(block > 0)
        def _():
            take(block - 1)

        return carry

    lax.fori_loop(0, blocks, one, 0)
    take(blocks - 1)
    give(blocks - 2).wait_send()
    give(blocks - 1).wait_send()


def ffn_both(rows, grad, row_halves, grad_halves, weights):
    tokens, width = rows.shape
    half = width // 2
    blocks = FF // FFN_BLOCK
    share = jax.ShapeDtypeStruct((half, FF), jnp.bfloat16)
    total = jax.ShapeDtypeStruct((tokens, width), jnp.float32)
    return pl.pallas_call(
        ffn_kernel,
        out_shape=(total, total, share, share, share),
        in_specs=whole_specs(6) + [pl.BlockSpec(memory_space=pl.ANY)],
        out_specs=tuple(whole_specs(5)),
        scratch_shapes=[
            pltpu.VMEM((2, width, 2 * FFN_BLOCK), jnp.bfloat16),
            pltpu.VMEM((2, width, FFN_BLOCK), jnp.bfloat16),
            pltpu.VMEM((tokens, FFN_BLOCK), jnp.bfloat16),
            pltpu.VMEM((tokens, 2 * FFN_BLOCK), jnp.bfloat16),
            pltpu.VMEM((4, half, tokens), jnp.bfloat16),
            pltpu.VMEM((2, half, 3 * FFN_BLOCK), jnp.bfloat16),
            pltpu.VMEM((blocks, half, 3 * FFN_BLOCK), jnp.bfloat16),
            pltpu.SemaphoreType.DMA((2, 3)),
            pltpu.SemaphoreType.DMA((blocks,)),
            pltpu.SemaphoreType.DMA((blocks,)),
        ],
        compiler_params=pltpu.CompilerParams(
            collective_id=5, has_side_effects=True, vmem_limit_bytes=58 * 2**20
        ),
        name="ffn_both",
    )(rows, grad, *row_halves, *grad_halves, weights)


EXTRA = 128


def physical_axes(mesh):
    shape = mesh.devices.shape
    names = []
    sizes = []
    for axis, extent in enumerate(shape):
        line = np.moveaxis(mesh.devices, axis, 0).reshape(extent, -1)[:, 0]
        places = [tuple(d.coords) + (d.core_on_chip,) for d in line]
        parts = []
        for dim, label in enumerate(("x", "y", "z", "core")):
            values = [p[dim] for p in places]
            if len(set(values)) > 1:
                step = next(i for i in range(extent) if values[i] != values[0])
                parts.append((step, label, len(set(values))))
        for step, label, size in sorted(parts, reverse=True):
            names.append(label)
            sizes.append(size)
    return tuple(names), tuple(sizes)


def pack_small(norm1_gain, norm2_gain, down, up, bias, group):
    rows = down.shape[0]

    def column(vector):
        return jnp.pad(vector, (0, rows - vector.shape[0]))[:, None]

    pieces = [
        down,
        column(norm1_gain),
        column(norm2_gain),
        column(bias),
        column(group),
        jnp.zeros((rows, 4), down.dtype),
        up.T.reshape(rows, 8),
        jnp.zeros((rows, EXTRA - 32), down.dtype),
    ]
    return jnp.concatenate(pieces, axis=1)


def unpack_small(small, devices):
    rows = small.shape[0] // devices
    by_device = small.reshape(devices, rows, EXTRA)
    down = small[:, :16]
    gain_one = small[:, 16]
    gain_two = small[:, 17]
    bias = by_device[:, : KEYS // devices, 18].reshape(KEYS)
    group = by_device[:, : HEAD_V // devices, 19].reshape(HEAD_V)
    up = small[:, 24:32].reshape(KEYS, 16).T
    return down, gain_one, gain_two, bias, group, up


def pack_small_grads(down, gain_one, gain_two, bias, group, up, devices):
    rows = gain_one.shape[0] // devices

    def column(vector):
        parts = vector.reshape(devices, -1)
        parts = jnp.pad(parts, ((0, 0), (0, rows - parts.shape[1])))
        return parts.reshape(devices * rows, 1)

    pieces = [
        down,
        gain_one[:, None],
        gain_two[:, None],
        column(bias),
        column(group),
        jnp.zeros((rows * devices, 4), jnp.float32),
        up.T.reshape(rows * devices, 8),
        jnp.zeros((rows * devices, EXTRA - 32), jnp.float32),
    ]
    return jnp.concatenate(pieces, axis=1)


def core_halves(rows, names, sizes):
    width = rows.shape[1]
    at = names.index("core")
    before = int(np.prod(sizes[:at], initial=1))
    after = width // before // sizes[at]
    core = lax.axis_index("core")

    def half(which):
        return jnp.concatenate(
            [
                lax.dynamic_slice_in_dim(rows, (2 * i + which) * after, after, 1)
                for i in range(before)
            ],
            axis=1,
        )

    return half(core), half(1 - core)


def swap_cores(values):
    return lax.ppermute(values, "core", [(0, 1), (1, 0)])


def pair_sum(halves, gradient):
    mine, other = halves
    taken = swap_cores(flat_grad(other, gradient).astype(jnp.bfloat16))
    return (flat_grad(mine, gradient) + taken.astype(jnp.float32)).astype(jnp.bfloat16)


def flat_grad(inputs, gradient):
    return jnp.einsum("td,te->de", inputs, gradient, preferred_element_type=jnp.float32)


def by_chip(values, names, sizes):
    chips = tuple(size for name, size in zip(names, sizes) if name != "core")
    return values.reshape(*chips, -1, values.shape[-1])


def pass_along(values, left, name):
    at = left.index(name)
    size = values.shape[at]
    own = lax.axis_index(name)
    arrived = []
    for shift in range(1, size):
        given = lax.dynamic_index_in_dim(values, lax.rem(own + shift, size), at, False)
        arrived.append(
            lax.ppermute(given, name, [(i, (i + shift) % size) for i in range(size)])
        )
    return arrived


def take_in(values, arrived, left, name):
    at = left.index(name)
    total = lax.dynamic_index_in_dim(values, lax.axis_index(name), at, False).astype(jnp.float32)
    for term in arrived:
        total = total + term.astype(jnp.float32)
    return total, [other for other in left if other != name]


def reduce_kernel(plan, *refs):
    inputs, jobs, sizes, slots = plan
    count = len(jobs)
    in_refs = refs[:inputs]
    outputs = max(job[4] for job in jobs) + 1
    out_refs = refs[inputs : inputs + outputs]
    scratch = refs[inputs + outputs :]
    send_sem, recv_sem = scratch[-2:]
    scratch = list(scratch[:-2])

    reached = sorted({name for job in jobs for name in job[3]})
    barrier = pltpu.get_barrier_semaphore()
    peers = 0
    for name in reached:
        for shift in range(1, sizes[name]):
            peer = lax.rem(lax.axis_index(name) + shift, sizes[name])
            pl.semaphore_signal(barrier, inc=1, device_id={name: peer}, device_id_type=MESH)
            peers += 1
    pl.semaphore_wait(barrier, peers)

    class Job:
        pass

    work = []
    slot = 0
    for which, columns, axes, order, out, out_columns in jobs:
        job = Job()
        job.left = list(axes)
        job.order = order
        job.out = out_refs[out]
        job.out_columns = slice(*out_columns)
        job.source = in_refs[which]
        job.columns = slice(*columns)
        job.got = [scratch.pop(0) for _ in order]
        job.kept = [scratch.pop(0) for _ in order[:-1]]
        job.slots = []
        for name in order:
            job.slots.append(slot)
            slot += sizes[name] - 1
        work.append(job)

    def part(job, index):
        at = job.left.index(job.order[job.step])
        lead = [slice(None)] * len(job.left)
        lead[at] = index
        return job.source.at[(*lead, slice(None), job.columns)]

    def copies(job):
        name = job.order[job.step]
        own = lax.axis_index(name)
        for shift in range(1, sizes[name]):
            peer = lax.rem(own + shift, sizes[name])
            at = job.slots[job.step] + shift - 1
            yield pltpu.make_async_remote_copy(
                src_ref=part(job, peer),
                dst_ref=job.got[job.step].at[shift - 1],
                send_sem=send_sem.at[at],
                recv_sem=recv_sem.at[at],
                device_id={name: peer},
                device_id_type=MESH,
            )

    def start(job):
        for copy in copies(job):
            copy.start()

    def add(job):
        name = job.order[job.step]
        at = job.left.index(name)
        own = lax.axis_index(name)
        rest = [n for n in job.left if n != name]
        last = job.step == len(job.order) - 1
        total = int(np.prod([sizes[n] for n in rest], initial=1))
        got = job.got[job.step]
        for copy in copies(job):
            copy.wait()
        source, columns, step = job.source, job.columns, job.step

        def one(i, carry):
            index = []
            for n in reversed(rest):
                index.insert(0, lax.rem(i, sizes[n]))
                i = lax.div(i, sizes[n])
            lead = list(index)
            lead.insert(at, own)
            value = source[(*lead, slice(None), columns)].astype(jnp.float32)
            for shift in range(1, sizes[name]):
                value = value + got[(shift - 1, *index)].astype(jnp.float32)
            if last:
                job.out[:, job.out_columns] = value
            else:
                job.kept[step][tuple(index)] = value.astype(jnp.bfloat16)
            return carry

        if total == 1:
            one(jnp.int32(0), 0)
        else:
            lax.fori_loop(0, total, one, 0)
        job.left = rest
        if not last:
            job.source = job.kept[step]
            job.columns = slice(None)
            job.step += 1
            start(job)

    for job in work:
        job.step = 0
        start(job)
    for step in range(max(len(job.order) for job in work)):
        for job in work:
            if len(job.order) > step:
                add(job)


def reduce_rest(arrays, jobs, sizes, rows, widths, collective):
    scratch = []
    slots = 0
    for which, (begin, end), axes, order, out, out_columns in jobs:
        left = list(axes)
        kept = []
        got = []
        for name in order:
            left.remove(name)
            shape = tuple(sizes[n] for n in left)
            got.append(pltpu.VMEM((sizes[name] - 1, *shape, rows, end - begin), jnp.bfloat16))
            kept.append(pltpu.VMEM((*shape, rows, end - begin), jnp.bfloat16))
            slots += sizes[name] - 1
        scratch += got + kept[:-1]
    scratch += [pltpu.SemaphoreType.DMA((slots,))] * 2
    return pl.pallas_call(
        partial(reduce_kernel, (len(arrays), jobs, sizes, slots)),
        out_shape=tuple(jax.ShapeDtypeStruct((rows, width), jnp.float32) for width in widths),
        in_specs=whole_specs(len(arrays)),
        out_specs=tuple(whole_specs(len(widths))),
        scratch_shapes=scratch,
        compiler_params=pltpu.CompilerParams(
            collective_id=collective, has_side_effects=True, vmem_limit_bytes=40 * 2**20
        ),
        name="reduce_rest",
    )(*arrays)


def chip_orders(names):
    first, second, last = [name for name in names if name != "core"]
    return (first, second, last), (second, last, first), (last, first, second)


def two_orders(names):
    first, second, last = [name for name in names if name != "core"]
    return (first, second, last), (second, last, first)


def last_orders(names):
    first, second, last = [name for name in names if name != "core"]
    return (first, second, last), (second, first, last)


def local(
    names,
    sizes,
    seq_axes,
    tokens,
    prefix_len,
    norm1_gain,
    query_weight,
    key_weight,
    value_weight,
    gate_weight,
    decay_down,
    decay_up,
    decay_bias,
    group_gain,
    out_weight,
    norm2_gain,
    ffn_gate,
    ffn_up,
    ffn_down,
    out_grad,
):
    devices = int(np.prod(sizes))
    orders = chip_orders(names)
    wide_order, long_order, late_order = (order[::-1] for order in orders)
    small_shard = pack_small(norm1_gain, norm2_gain, decay_down, decay_up, decay_bias, group_gain)
    first, small_full = gather_first(
        names,
        sizes,
        (query_weight, key_weight, value_weight, gate_weight, small_shard),
        (3072, EXTRA),
        (
            (3, 0, (0, 1024), (2048, 3072), wide_order),
            (4, 1, (0, EXTRA), (0, EXTRA), wide_order),
            (0, 0, (0, 128), (0, 128), wide_order),
            (2, 0, (0, 1024), (1024, 2048), long_order),
            (0, 0, (128, 384), (128, 384), long_order),
            (1, 0, (0, 512), (512, 1024), late_order),
            (0, 0, (384, 512), (384, 512), late_order),
        ),
    )
    ffn_shard = jnp.concatenate([ffn_gate, ffn_up, ffn_down.T, out_weight], axis=1)
    ffn_full = lax.all_gather(ffn_shard, names, axis=0, tiled=True)
    weight_o = ffn_full[:, 3 * FF :]
    mixer_full = first.reshape(-1, 3072)
    small_full = small_full.reshape(-1, EXTRA)
    weight_down, gain_one, gain_two, bias_full, gain_group, weight_up = unpack_small(
        small_full, devices
    )
    seq_count, tok_count, feature_count = tokens.shape
    rows = seq_count * tok_count
    resid_in = tokens.reshape(rows, feature_count).astype(jnp.float32)
    scale_one = rms_scale(resid_in)
    unit_one = resid_in * scale_one
    normed = (unit_one * gain_one.astype(jnp.float32)).astype(jnp.bfloat16)
    projected = project(normed, mixer_full).astype(jnp.bfloat16)
    lowrank = project(normed, weight_down).astype(jnp.bfloat16)
    logits = project(lowrank, weight_up) + bias_full.astype(jnp.float32)
    decays = jax.nn.log_sigmoid(logits) / 16.0
    wide_gain = jnp.broadcast_to(gain_group.astype(jnp.float32)[None], (8, HEAD_V))
    gated_rows, unit_group, scale_group, cum, states, prefix_state = mix_forward(
        seq_axes, prefix_len, projected, decays, wide_gain
    )
    resid_mid = resid_in + project(gated_rows, weight_o)
    scale_two = rms_scale(resid_mid)
    unit_two = resid_mid * scale_two
    normed_two = (unit_two * gain_two.astype(jnp.float32)).astype(jnp.bfloat16)
    out_grad = out_grad.reshape(rows, feature_count)
    grad_out = out_grad.astype(jnp.float32)
    ffn_out, grad_normed_two, gate_sum, up_sum, down_sum = ffn_both(
        normed_two,
        out_grad,
        core_halves(normed_two, names, sizes),
        core_halves(out_grad, names, sizes),
        ffn_full,
    )
    layer_out = (resid_mid + ffn_out).astype(jnp.bfloat16)
    gain_two_grad = jnp.sum(grad_normed_two * unit_two, axis=0)
    grad_mid = grad_out + rms_back(
        grad_normed_two * gain_two.astype(jnp.float32), unit_two, scale_two
    )
    grad_branch = grad_mid.astype(jnp.bfloat16)
    gated_grad = back_project(grad_branch, weight_o).astype(jnp.bfloat16)
    out_sum = pair_sum(core_halves(gated_rows, names, sizes), grad_branch)
    groups = (
        jnp.concatenate([gate_sum, out_sum, down_sum[:, :896]], axis=1),
        jnp.concatenate([up_sum, down_sum[:, 896:]], axis=1),
    )
    groups, gated_grad = lax.optimization_barrier((groups, gated_grad))
    chips = [name for name in names if name != "core"]
    orders = two_orders(names)
    lefts = [chips] * 2
    groups = [by_chip(group, names, sizes) for group in groups]
    arrived = [pass_along(g, left, order[0]) for g, left, order in zip(groups, lefts, orders)]
    grad_projected, grad_decay, group_grad = mix_backward(
        seq_axes,
        prefix_len,
        projected,
        cum,
        states,
        prefix_state,
        gated_grad,
        unit_group,
        scale_group,
        wide_gain,
    )
    arrived, grad_projected, grad_decay = lax.optimization_barrier(
        (arrived, grad_projected, grad_decay)
    )
    taken = [
        take_in(g, more, left, order[0])
        for g, more, left, order in zip(groups, arrived, lefts, orders)
    ]
    groups = [total.astype(jnp.bfloat16) for total, _ in taken]
    lefts = [left for _, left in taken]
    arrived = [pass_along(g, left, order[1]) for g, left, order in zip(groups, lefts, orders)]
    late = flat_grad(normed, grad_projected).astype(jnp.bfloat16)
    grad_logits = (grad_decay * jax.nn.sigmoid(-logits) / 16.0).astype(jnp.bfloat16)
    bias_grad = jnp.sum(grad_logits.astype(jnp.float32), axis=0)
    up_rank_grad = flat_grad(lowrank, grad_logits)
    grad_lowrank = back_project(grad_logits, weight_up).astype(jnp.bfloat16)
    down_rank_grad = flat_grad(normed, grad_lowrank)
    grad_normed = back_project(grad_projected, mixer_full) + back_project(
        grad_lowrank, weight_down
    )
    gain_one_grad = jnp.sum(grad_normed * unit_one, axis=0)
    tokens_grad = grad_mid + rms_back(
        grad_normed * gain_one.astype(jnp.float32), unit_one, scale_one
    )
    small_grads = pack_small_grads(
        down_rank_grad,
        gain_one_grad,
        gain_two_grad,
        bias_grad,
        group_grad[0],
        up_rank_grad,
        devices,
    ).astype(jnp.bfloat16)
    arrived, late, small_grads, tokens_grad = lax.optimization_barrier(
        (arrived, late, small_grads, tokens_grad)
    )
    groups = [
        take_in(g, more, left, order[1])[0].astype(jnp.bfloat16)
        for g, more, left, order in zip(groups, arrived, lefts, orders)
    ]
    own_rows = feature_count // devices
    late = late.reshape(*sizes, own_rows, -1)
    small_grads = small_grads.reshape(*sizes, own_rows, -1)
    size_of = dict(zip(names, sizes))
    ends = last_orders(names)
    jobs = [
        (which, columns, names, ("core", *order), which, columns)
        for which, columns, order in (
            (2, (0, 1536), ends[0]),
            (2, (1536, 3072), ends[1]),
            (3, (0, EXTRA), ends[0]),
        )
    ] + [
        (i, (0, groups[i].shape[-1]), (order[2],), (order[2],), i, (0, groups[i].shape[-1]))
        for i, order in enumerate(orders)
    ]
    first_group, second_group, mine, small = reduce_rest(
        (*groups, late, small_grads), jobs, size_of, own_rows, (4736, 4736, 3072, EXTRA), 3
    )
    shape = tokens.shape
    return (
        layer_out.reshape(shape),
        tokens_grad.reshape(shape),
        small[:, 16],
        mine[:, :512],
        mine[:, 512:1024],
        mine[:, 1024:2048],
        mine[:, 2048:],
        small[:, :16],
        small[:, 24:32].reshape(KEYS // devices, 16).T,
        small[: KEYS // devices, 18],
        small[: HEAD_V // devices, 19],
        first_group[:, FF : FF + VALS],
        small[:, 17],
        first_group[:, :FF],
        second_group[:, :FF],
        jnp.concatenate([first_group[:, FF + VALS :], second_group[:, FF:]], axis=1).T,
    )


def solution(mesh):
    names, sizes = physical_axes(mesh)
    cut = next(
        i for i in range(len(sizes) + 1) if np.prod(sizes[:i], initial=1) == mesh.shape["dp"]
    )
    dp, seq = names[:cut], names[cut:]
    split = Mesh(mesh.devices.reshape(sizes), names)
    return jax.shard_map(
        partial(local, names, sizes, tuple(zip(seq, sizes[cut:]))),
        mesh=split,
        in_specs=(
            P(dp, seq, None),
            P(dp),
            P(names),
            P(names, None),
            P(names, None),
            P(names, None),
            P(names, None),
            P(names, None),
            P(None, names),
            P(names),
            P(names),
            P(names, None),
            P(names),
            P(names, None),
            P(names, None),
            P(None, names),
            P(dp, seq, None),
        ),
        out_specs=(
            P(dp, seq, None),
            P(dp, seq, None),
            P(names),
            P(names, None),
            P(names, None),
            P(names, None),
            P(names, None),
            P(names, None),
            P(None, names),
            P(names),
            P(names),
            P(names, None),
            P(names),
            P(names, None),
            P(names, None),
            P(None, names),
        ),
        check_vma=False,
    )
```

```python
from functools import partial

import jax
import jax.numpy as jnp
import numpy as np
from jax import lax
from jax.experimental import pallas as pl
from jax.experimental.pallas import tpu as pltpu
from jax.sharding import Mesh
from jax.sharding import PartitionSpec as P

KEYS = 512
VALS = 1024
HEADS = 4
SPAN = 64
HEAD_K = 128
HEAD_V = 256
FF = 2816


norm_eps = 1e-05


def project(inputs, weight):
    return jnp.einsum("td,de->te", inputs, weight, preferred_element_type=jnp.float32)


def back_project(gradient, weight):
    return jnp.einsum("te,de->td", gradient, weight, preferred_element_type=jnp.float32)


def rms_scale(values):
    return lax.rsqrt(jnp.mean(values * values, axis=-1, keepdims=True) + norm_eps)


def rms_back(grad_unit, unit_rows, scale_rows):
    return scale_rows * (
        grad_unit - unit_rows * jnp.mean(grad_unit * unit_rows, axis=-1, keepdims=True)
    )


CHUNK = 128
MESH = pl.DeviceIdType.MESH


def nn(a, b):
    return lax.dot_general(a, b, (((1,), (0,)), ((), ())), preferred_element_type=jnp.float32)


def nt(a, b):
    return lax.dot_general(a, b, (((1,), (1,)), ((), ())), preferred_element_type=jnp.float32)


def tn(a, b):
    return lax.dot_general(a, b, (((0,), (0,)), ((), ())), preferred_element_type=jnp.float32)


def low(values):
    return values.astype(jnp.bfloat16)


def wide(values):
    return values.astype(jnp.float32)


def three_way(ones, values):
    first = low(values)
    left = values - wide(first)
    second = low(left)
    third = low(left - wide(second))
    return nn(ones, first) + nn(ones, second) + nn(ones, third)


def logistic_of(values):
    return 0.5 * jnp.tanh(0.5 * values) + 0.5


def iota(shape, dim):
    return lax.broadcasted_iota(jnp.int32, shape, dim)


def place_on(axes):
    place = 0
    for name, size in axes:
        place = place * size + lax.axis_index(name)
    return place


def device_at(axes, place):
    where = {}
    for name, size in reversed(axes):
        where[name] = lax.rem(place, size)
        place = lax.div(place, size)
    return where


def line_length(axes):
    return int(np.prod([size for _, size in axes]))


def greet(axes, place, count, extra=0):
    barrier = pltpu.get_barrier_semaphore()

    @pl.when(place > 0)
    def _():
        pl.semaphore_signal(
            barrier, inc=1, device_id=device_at(axes, place - 1), device_id_type=MESH
        )

    @pl.when(place < count - 1)
    def _():
        pl.semaphore_signal(
            barrier, inc=1, device_id=device_at(axes, place + 1), device_id_type=MESH
        )

    @pl.when(jnp.logical_or(place == 0, place == count - 1))
    def _():
        pl.semaphore_wait(barrier, 1 + extra)

    @pl.when(jnp.logical_and(place > 0, place < count - 1))
    def _():
        pl.semaphore_wait(barrier, 2 + extra)


def send(source, target, send_sem, recv_sem, axes, place):
    return pltpu.make_async_remote_copy(
        src_ref=source,
        dst_ref=target,
        send_sem=send_sem,
        recv_sem=recv_sem,
        device_id=device_at(axes, place),
        device_id_type=MESH,
    )


class Gather:
    def __init__(self, names, sizes, pieces, local_sem, send_sem, recv_sem, pair_send, pair_recv):
        self.names = names
        self.sizes = dict(zip(names, sizes))
        self.pieces = pieces
        self.sems = local_sem, send_sem, recv_sem, pair_send, pair_recv
        self.steps = len(pieces[0][4])

    def region(self, piece, known, at):
        lead = []
        for name in self.names:
            if name in known:
                lead.append(slice(None))
            elif name in at:
                lead.append(at[name])
            else:
                lead.append(lax.axis_index(name))
        _, whole, _, columns, _ = piece
        return whole.at[(*lead, slice(None), slice(*columns))]

    def local(self, i):
        shard, _, columns, _, _ = self.pieces[i]
        return pltpu.make_async_copy(
            shard.at[:, slice(*columns)], self.region(self.pieces[i], (), {}), self.sems[0].at[i]
        )

    def copies(self, i, step):
        piece = self.pieces[i]
        order = piece[4]
        name = order[step]
        own = lax.axis_index(name)
        base = (i * self.steps + step) * 3
        for shift in range(1, self.sizes[name]):
            peer = lax.rem(own + shift, self.sizes[name])
            here = self.region(piece, order[:step], {})
            yield pltpu.make_async_remote_copy(
                src_ref=here,
                dst_ref=here,
                send_sem=self.sems[1].at[base + shift - 1],
                recv_sem=self.sems[2].at[base + shift - 1],
                device_id={name: peer},
                device_id_type=MESH,
            )

    def pair(self, i, step, shift):
        piece = self.pieces[i]
        order = piece[4]
        if step < 0:
            here = self.region(piece, (), {})
            at = 0
        else:
            name = order[step]
            source = lax.rem(lax.axis_index(name) + self.sizes[name] - shift, self.sizes[name])
            here = self.region(piece, order[:step], {name: source})
            at = 1 + step * 3 + shift - 1
        at += i * (1 + 3 * self.steps)
        return pltpu.make_async_remote_copy(
            src_ref=here,
            dst_ref=here,
            send_sem=self.sems[3].at[at],
            recv_sem=self.sems[4].at[at],
            device_id={"core": 1 - lax.axis_index("core")},
            device_id_type=MESH,
        )

    def begin(self):
        for i in range(len(self.pieces)):
            self.local(i).start()
        for i in range(len(self.pieces)):
            self.local(i).wait()
            for copy in self.copies(i, 0):
                copy.start()
            self.pair(i, -1, 0).start()

    def advance(self, step):
        for i, piece in enumerate(self.pieces):
            for copy in self.copies(i, step):
                copy.wait_recv()
            if step < self.steps - 1:
                for copy in self.copies(i, step + 1):
                    copy.start()
            for shift in range(1, self.sizes[piece[4][step]]):
                self.pair(i, step, shift).start()

    def end(self):
        for i, piece in enumerate(self.pieces):
            for step in range(self.steps):
                for copy in self.copies(i, step):
                    copy.wait_send()
                for shift in range(1, self.sizes[piece[4][step]]):
                    self.pair(i, step, shift).wait()
            self.pair(i, -1, 0).wait()

    @staticmethod
    def scratch(count):
        return [
            pltpu.SemaphoreType.DMA((count,)),
            pltpu.SemaphoreType.DMA((count * 9,)),
            pltpu.SemaphoreType.DMA((count * 9,)),
            pltpu.SemaphoreType.DMA((count * 10,)),
            pltpu.SemaphoreType.DMA((count * 10,)),
        ]


def signal_axes(names, sizes):
    barrier = pltpu.get_barrier_semaphore()
    peers = 0
    for name, size in zip(names, sizes):
        for shift in range(1, size):
            peer = lax.rem(lax.axis_index(name) + shift, size)
            pl.semaphore_signal(barrier, inc=1, device_id={name: peer}, device_id_type=MESH)
            peers += 1
    return peers


def gather_kernel(plan, *refs):
    names, sizes, inputs, outputs, pieces = plan
    wholes = refs[inputs : inputs + outputs]
    peers = signal_axes(names, sizes)
    pl.semaphore_wait(pltpu.get_barrier_semaphore(), peers)
    gather = Gather(
        names,
        sizes,
        [(refs[i], wholes[o], cols, to, order) for i, o, cols, to, order in pieces],
        *refs[inputs + outputs :],
    )
    gather.begin()
    for step in range(gather.steps):
        gather.advance(step)
    gather.end()


def gather_first(names, sizes, shards, widths, pieces):
    rows = shards[0].shape[0]
    anywhere = pl.BlockSpec(memory_space=pl.ANY)
    return pl.pallas_call(
        partial(gather_kernel, (names, sizes, len(shards), len(widths), pieces)),
        out_shape=tuple(
            jax.ShapeDtypeStruct((*sizes, rows, width), jnp.bfloat16) for width in widths
        ),
        in_specs=[anywhere] * len(shards),
        out_specs=(anywhere,) * len(widths),
        scratch_shapes=Gather.scratch(len(pieces)),
        compiler_params=pltpu.CompilerParams(collective_id=4, has_side_effects=True),
        name="gather_first",
    )(*shards)


def row_places(count):
    return iota((count, HEAD_K), 0)


def both_ways(seqs, place, count, go_right, go_left):
    behind = count - 1 - place

    def step(seq, carry):
        for head in range(HEADS):

            @pl.when(seq < seqs)
            def _():
                go_right(seq, head)

            @pl.when(jnp.logical_and(seq >= behind, seq < behind + seqs))
            def _():
                go_left(seq - behind, head)

        return carry

    lax.fori_loop(0, seqs + count - 1, step, 0)


def prefix_weights(cum, end_local, count):
    rows = row_places(count)
    owner = jnp.logical_and(end_local >= 0, end_local < count)
    end_cum = jnp.sum(jnp.where(rows == end_local, cum, 0.0), axis=0, keepdims=True)
    keep = jnp.logical_and(rows <= end_local, rows <= jnp.where(owner, count, -1))
    weights = jnp.where(keep, jnp.exp(jnp.where(keep, end_cum - cum, 0.0)), 0.0)
    return weights, jnp.exp(end_cum) * jnp.where(owner, 1.0, 0.0)


def chunk_parts(cum, chunk):
    begin = chunk * CHUNK
    piece = cum[begin : begin + CHUNK]
    if chunk:
        piece = piece - cum[begin - 1 : begin]
    return piece, piece[CHUNK - 1 :], piece[CHUNK // 2 - 1 : CHUNK // 2]


def query_columns(head):
    return slice(head * HEAD_K, (head + 1) * HEAD_K)


def key_columns(head):
    return slice(KEYS + head * HEAD_K, KEYS + (head + 1) * HEAD_K)


def value_columns(head):
    return slice(2 * KEYS + head * HEAD_V, 2 * KEYS + (head + 1) * HEAD_V)


def gate_columns(head):
    begin = 2 * KEYS + VALS + head * HEAD_V
    return slice(begin, begin + HEAD_V)


def forward_kernel(plan, *refs):
    axes = plan
    prefix_ref, proj_ref, decay_ref, gain_ref = refs[:4]
    gated_ref, unit_ref, scale_ref, cum_ref, state_ref, prefix_state_ref = refs[4:10]
    mixed_ref, kv_ref, part_ref, edge_ref, *line = refs[10:]
    right_out, right_in, left_out, left_in, right_sent, right_got, left_sent, left_got = line
    count = line_length(axes)
    place = place_on(axes)
    seqs = prefix_ref.shape[0]
    toks = proj_ref.shape[0] // seqs
    chunks = toks // CHUNK
    greet(axes, place, count)
    lower = low(jnp.where(iota((CHUNK, CHUNK), 0) >= iota((CHUNK, CHUNK), 1), 1.0, 0.0))
    causal = iota((CHUNK, CHUNK), 0) >= iota((CHUNK, CHUNK), 1)

    def to_right(i):
        return send(right_out.at[i], right_in.at[i], right_sent.at[i], right_got.at[i], axes, place + 1)

    def to_left(i):
        return send(left_out.at[i], left_in.at[i], left_sent.at[i], left_got.at[i], axes, place - 1)

    def states_of(seq, carry):
        rows = pl.ds(pl.multiple_of(seq * toks, toks), toks)
        end_local = prefix_ref[seq] - 1 - place * toks
        locals_ = []
        for head in range(HEADS):
            i = seq * HEADS + head
            keys = query_columns(head)
            before = jnp.zeros((1, HEAD_K), jnp.float32)
            key = wide(proj_ref[rows, key_columns(head)])
            value = proj_ref[rows, value_columns(head)]
            decay = decay_ref[rows, keys]
            pieces = []
            local = jnp.zeros((HEAD_V, HEAD_K), jnp.float32)
            for chunk in range(chunks):
                at = slice(chunk * CHUNK, (chunk + 1) * CHUNK)
                piece = three_way(lower, decay[at])
                total = piece[CHUNK - 1 :]
                share = tn(value[at], low(key[at] * jnp.exp(total - piece)))
                kv_ref[i, chunk] = share
                local = jnp.exp(total) * local + share
                pieces.append(piece + before)
                before = before + total
            cum = jnp.concatenate(pieces, axis=0)
            cum_ref[rows, keys] = cum
            weights, edge = prefix_weights(cum, end_local, toks)
            part_ref[i] = tn(value, low(key * weights))
            edge_ref[i] = jnp.broadcast_to(edge, (8, HEAD_K))
            locals_.append(low(local))

        @pl.when(place == 0)
        def _():
            for head in range(HEADS):
                i = seq * HEADS + head
                right_out[i] = locals_[head]
                if count > 1:
                    to_right(i).start()

        return carry

    lax.fori_loop(0, seqs, states_of, 0)

    def go_right(seq, head):
        rows = pl.ds(pl.multiple_of(seq * toks, toks), toks)
        i = seq * HEADS + head
        vals = slice(head * HEAD_V, (head + 1) * HEAD_V)
        cum = cum_ref[rows, query_columns(head)]

        @pl.when(place == 0)
        def _():
            right_in[i] = jnp.zeros((HEAD_V, HEAD_K), jnp.bfloat16)

        @pl.when(place > 0)
        def _():
            send(
                right_out.at[i], right_in.at[i], right_sent.at[i], right_got.at[i], axes, place - 1
            ).wait_recv()

        state = wide(right_in[i])
        part = part_ref[i] + edge_ref[i][:1] * state
        part_ref[i] = part
        for chunk in range(chunks):
            state_ref[i, chunk] = low(state)
            state = jnp.exp(chunk_parts(cum, chunk)[1]) * state + kv_ref[i, chunk]
        state_ref[i, chunks] = low(state)

        @pl.when(jnp.logical_and(place > 0, place < count - 1))
        def _():
            right_out[i] = low(state)
            to_right(i).start()

        if count > 1:

            @pl.when(place == count - 1)
            def _():
                left_out[i] = low(part)
                to_left(i).start()

        query = wide(proj_ref[rows, query_columns(head)])
        key = wide(proj_ref[rows, key_columns(head)])
        value = proj_ref[rows, value_columns(head)]
        for chunk in range(chunks):
            at = slice(chunk * CHUNK, (chunk + 1) * CHUNK)
            piece, total, middle = chunk_parts(cum, chunk)
            raw = nt(
                low(query[at] * jnp.exp(piece - middle)), low(key[at] * jnp.exp(middle - piece))
            )
            mixed_ref[pl.ds(seq * toks + chunk * CHUNK, CHUNK), vals] = nn(
                low(jnp.where(causal, raw, 0.0)), value[at]
            ) + nt(low(query[at] * jnp.exp(piece)), state_ref[i, chunk])

    def go_left(seq, head):
        rows = pl.ds(pl.multiple_of(seq * toks, toks), toks)
        end_local = prefix_ref[seq] - 1 - place * toks
        inside = iota((toks, HEAD_V), 0) <= end_local
        i = seq * HEADS + head
        vals = slice(head * HEAD_V, (head + 1) * HEAD_V)

        @pl.when(place < count - 1)
        def _():
            send(
                left_out.at[i], left_in.at[i], left_sent.at[i], left_got.at[i], axes, place + 1
            ).wait_recv()

        @pl.when(place == count - 1)
        def _():
            left_in[i] = jnp.zeros((HEAD_V, HEAD_K), jnp.bfloat16)

        whole = low(part_ref[i] + wide(left_in[i]))

        @pl.when(jnp.logical_and(place > 0, place < count - 1))
        def _():
            left_out[i] = whole
            to_left(i).start()

        prefix_state_ref[i] = whole
        mixed = jnp.where(
            inside, nt(proj_ref[rows, query_columns(head)], whole), mixed_ref[rows, vals]
        )
        scale = lax.rsqrt(jnp.mean(mixed * mixed, axis=1, keepdims=True) + norm_eps)
        unit = mixed * scale
        gate = wide(proj_ref[rows, gate_columns(head)])
        gated_ref[rows, vals] = low(unit * gain_ref[:1] * gate * logistic_of(gate))
        unit_ref[rows, vals] = low(unit)
        scale_ref[rows, slice(head, head + 1)] = scale

    both_ways(seqs, place, count, go_right, go_left)

    def finish(i, carry):
        @pl.when(place < count - 1)
        def _():
            to_right(i).wait_send()

        @pl.when(place > 0)
        def _():
            to_left(i).wait_send()

        return carry

    lax.fori_loop(0, seqs * HEADS, finish, 0)


def backward_kernel(
    axes,
    prefix_ref,
    proj_ref,
    cum_ref,
    state_ref,
    prefix_state_ref,
    gated_grad_ref,
    unit_ref,
    scale_ref,
    gain_ref,
    dproj_ref,
    ddecay_ref,
    gain_grad_ref,
    grad_ref,
    local_ref,
    acc_ref,
    dk_part,
    dv_part,
    dcum_part,
    right_out,
    right_in,
    left_out,
    left_in,
    right_sent,
    right_got,
    left_sent,
    left_got,
):
    count = line_length(axes)
    place = place_on(axes)
    seqs = prefix_ref.shape[0]
    toks = proj_ref.shape[0] // seqs
    chunks = toks // CHUNK
    greet(axes, place, count)
    causal = iota((CHUNK, CHUNK), 0) >= iota((CHUNK, CHUNK), 1)
    upper = low(jnp.where(iota((toks, toks), 0) <= iota((toks, toks), 1), 1.0, 0.0))

    def to_right(i):
        return send(right_out.at[i], right_in.at[i], right_sent.at[i], right_got.at[i], axes, place + 1)

    def to_left(i):
        return send(left_out.at[i], left_in.at[i], left_sent.at[i], left_got.at[i], axes, place - 1)

    def shares_of(seq, carry):
        rows = pl.ds(pl.multiple_of(seq * toks, toks), toks)
        end_local = prefix_ref[seq] - 1 - place * toks
        inside = iota((toks, HEAD_V), 0) <= end_local
        shares = []
        gain = gain_ref[:1]
        gain_grad = jnp.zeros((1, HEAD_V), jnp.float32)
        for head in range(HEADS):
            i = seq * HEADS + head
            vals = slice(head * HEAD_V, (head + 1) * HEAD_V)
            cum = cum_ref[rows, query_columns(head)]
            query = proj_ref[rows, query_columns(head)]
            gate = wide(proj_ref[rows, gate_columns(head)])
            logistic = logistic_of(gate)
            unit = wide(unit_ref[rows, vals])
            gated_grad = wide(gated_grad_ref[rows, vals])
            through = gated_grad * unit
            active = gate * logistic
            dproj_ref[rows, gate_columns(head)] = low(
                through * gain * (logistic + active * (1.0 - logistic))
            )
            gain_grad = gain_grad + jnp.sum(through * active, axis=0, keepdims=True)
            weighted = gated_grad * active * gain
            grad = scale_ref[rows, slice(head, head + 1)] * (
                weighted - unit * jnp.mean(weighted * unit, axis=1, keepdims=True)
            )
            grad_ref[rows, vals] = low(grad)
            share = tn(low(jnp.where(inside, grad, 0.0)), query)
            acc_ref[i] = share
            shares.append(low(share))
            later = low(jnp.where(inside, 0.0, grad))
            for chunk in range(chunks):
                at = slice(chunk * CHUNK, (chunk + 1) * CHUNK)
                piece, total, middle = chunk_parts(cum, chunk)
                local_ref[i, chunk] = tn(later[at], low(wide(query[at]) * jnp.exp(piece)))
        gain_grad_ref[:1] += gain_grad

        @pl.when(place == 0)
        def _():
            for head in range(HEADS):
                i = seq * HEADS + head
                right_out[i] = shares[head]
                if count > 1:
                    to_right(i).start()

        return carry

    gain_grad_ref[...] = jnp.zeros_like(gain_grad_ref)
    lax.fori_loop(0, seqs, shares_of, 0)

    def go_right(seq, head):
        rows = pl.ds(pl.multiple_of(seq * toks, toks), toks)
        end_local = prefix_ref[seq] - 1 - place * toks
        inside = iota((toks, HEAD_V), 0) <= end_local
        at_end = iota((toks, HEAD_K), 0) == end_local
        i = seq * HEADS + head
        cum = cum_ref[rows, query_columns(head)]

        @pl.when(place == 0)
        def _():
            right_in[i] = jnp.zeros((HEAD_V, HEAD_K), jnp.bfloat16)

        @pl.when(place > 0)
        def _():
            send(
                right_out.at[i], right_in.at[i], right_sent.at[i], right_got.at[i], axes, place - 1
            ).wait_recv()

        acc = acc_ref[i] + wide(right_in[i])
        narrow_acc = low(acc)

        @pl.when(jnp.logical_and(place > 0, place < count - 1))
        def _():
            right_out[i] = narrow_acc
            to_right(i).start()

        weights, edge = prefix_weights(cum, end_local, toks)
        local = jnp.zeros((HEAD_V, HEAD_K), jnp.float32)
        starts = []
        for chunk in reversed(range(chunks)):
            starts.append(low(local))
            local = jnp.exp(chunk_parts(cum, chunk)[1]) * local + local_ref[i, chunk]
        starts = starts[::-1]
        local = local + edge * acc
        acc_ref[i] = local
        if count > 1:

            @pl.when(place == count - 1)
            def _():
                left_out[i] = low(local)
                to_left(i).start()

        keys = query_columns(head)
        vals = slice(head * HEAD_V, (head + 1) * HEAD_V)
        query = wide(proj_ref[rows, query_columns(head)])
        key = wide(proj_ref[rows, key_columns(head)])
        value = proj_ref[rows, value_columns(head)]
        grad = wide(grad_ref[rows, vals])
        later = low(jnp.where(inside, 0.0, grad))
        prefix_state = prefix_state_ref[i]
        weighted = low(key * weights)
        dk_all = weights * nn(value, narrow_acc)
        dv_all = nt(weighted, narrow_acc)
        dq_all = nn(low(jnp.where(inside, grad, 0.0)), prefix_state)
        dqs, dks, dvs, dcs = [], [], [], []
        for chunk in range(chunks):
            at = slice(chunk * CHUNK, (chunk + 1) * CHUNK)
            piece, total, middle = chunk_parts(cum, chunk)
            rise = jnp.exp(piece - middle)
            fall = jnp.exp(middle - piece)
            q_in = low(query[at] * rise)
            k_in = low(key[at] * fall)
            scores = low(jnp.where(causal, nt(q_in, k_in), 0.0))
            d_scores = low(jnp.where(causal, nt(later[at], value[at]), 0.0))
            dq_in = nn(d_scores, k_in)
            dk_in = tn(d_scores, q_in)
            dq_state = jnp.exp(piece) * nn(later[at], state_ref[i, chunk])
            dk_state = dk_all[at]
            dv = tn(scores, later[at]) + dv_all[at]
            if chunk < chunks - 1:
                to_end = jnp.exp(total - piece)
                dk_state = to_end * nn(value[at], starts[chunk]) + dk_state
                dv = dv + nt(low(key[at] * to_end), starts[chunk])
            dqs.append(rise * dq_in + dq_state + dq_all[at])
            dks.append(fall * dk_in + dk_state)
            dvs.append(dv)
            dcs.append(
                wide(q_in) * dq_in
                - wide(k_in) * dk_in
                + query[at] * dq_state
                - key[at] * dk_state
            )
        dproj_ref[rows, query_columns(head)] = low(jnp.concatenate(dqs, axis=0))
        dk_part[rows, keys] = jnp.concatenate(dks, axis=0)
        dv_part[rows, vals] = jnp.concatenate(dvs, axis=0)
        turn = jnp.sum(wide(narrow_acc) * wide(prefix_state), axis=0, keepdims=True)
        dcum_part[rows, keys] = jnp.concatenate(dcs, axis=0) + jnp.where(at_end, turn, 0.0)

    def go_left(seq, head):
        rows = pl.ds(pl.multiple_of(seq * toks, toks), toks)
        i = seq * HEADS + head
        keys = query_columns(head)
        vals = slice(head * HEAD_V, (head + 1) * HEAD_V)

        @pl.when(place < count - 1)
        def _():
            send(
                left_out.at[i], left_in.at[i], left_sent.at[i], left_got.at[i], axes, place + 1
            ).wait_recv()

        @pl.when(place == count - 1)
        def _():
            left_in[i] = jnp.zeros((HEAD_V, HEAD_K), jnp.bfloat16)

        @pl.when(jnp.logical_and(place > 0, place < count - 1))
        def _():
            last = cum_ref[rows, keys][toks - 1 :]
            left_out[i] = low(jnp.exp(last) * wide(left_in[i]) + acc_ref[i])
            to_left(i).start()

        cum = cum_ref[rows, keys]
        key = wide(proj_ref[rows, key_columns(head)])
        value = proj_ref[rows, value_columns(head)]
        after = left_in[i]
        to_end = jnp.exp(cum[toks - 1 :] - cum)
        dk_more = to_end * nn(value, after)
        dproj_ref[rows, key_columns(head)] = low(dk_part[rows, keys] + dk_more)
        dproj_ref[rows, value_columns(head)] = low(
            dv_part[rows, vals] + nt(low(key * to_end), after)
        )
        carry_row = jnp.sum(wide(after) * wide(state_ref[i, chunks]), axis=0, keepdims=True)
        dcum = dcum_part[rows, keys] - key * dk_more
        ddecay_ref[rows, keys] = three_way(upper, dcum) + carry_row

    both_ways(seqs, place, count, go_right, go_left)

    def finish(i, carry):
        @pl.when(place < count - 1)
        def _():
            to_right(i).wait_send()

        @pl.when(place > 0)
        def _():
            to_left(i).wait_send()

        return carry

    lax.fori_loop(0, seqs * HEADS, finish, 0)


def line_scratch(pieces):
    block = pltpu.VMEM((pieces, HEAD_V, HEAD_K), jnp.bfloat16)
    return [block] * 4 + [pltpu.SemaphoreType.DMA((pieces,))] * 4


def whole_specs(count):
    return [pl.BlockSpec(memory_space=pltpu.VMEM)] * count


def mix_forward(axes, prefix_len, projected, decays, group_gain):
    tokens = projected.shape[0]
    seqs = prefix_len.shape[0]
    heads = seqs * HEADS
    chunks = tokens // seqs // CHUNK
    state = (heads, HEAD_V, HEAD_K)
    return pl.pallas_call(
        partial(forward_kernel, axes),
        out_shape=(
            jax.ShapeDtypeStruct((tokens, VALS), jnp.bfloat16),
            jax.ShapeDtypeStruct((tokens, VALS), jnp.bfloat16),
            jax.ShapeDtypeStruct((tokens, 128), jnp.float32),
            jax.ShapeDtypeStruct((tokens, KEYS), jnp.float32),
            jax.ShapeDtypeStruct((heads, chunks + 1, HEAD_V, HEAD_K), jnp.bfloat16),
            jax.ShapeDtypeStruct(state, jnp.bfloat16),
        ),
        in_specs=[pl.BlockSpec(memory_space=pltpu.SMEM)] + whole_specs(3),
        out_specs=tuple(whole_specs(6)),
        scratch_shapes=[
            pltpu.VMEM((tokens, VALS), jnp.float32),
            pltpu.VMEM((heads, chunks, HEAD_V, HEAD_K), jnp.float32),
            pltpu.VMEM(state, jnp.float32),
            pltpu.VMEM((heads, 8, HEAD_K), jnp.float32),
            *line_scratch(heads),
        ],
        compiler_params=pltpu.CompilerParams(
            collective_id=1, has_side_effects=True, vmem_limit_bytes=50 * 2**20
        ),
        cost_estimate=pl.CostEstimate(
            flops=60_000_000_000, bytes_accessed=220_000_000, transcendentals=0
        ),
        name="mix_forward",
    )(prefix_len, projected, decays, group_gain)


def mix_backward(
    axes, prefix_len, projected, cum, states, prefix_state, gated_grad, unit, scale, group_gain
):
    tokens = projected.shape[0]
    seqs = prefix_len.shape[0]
    pieces = seqs * HEADS
    chunks = tokens // seqs // CHUNK
    state = (pieces, HEAD_V, HEAD_K)
    return pl.pallas_call(
        partial(backward_kernel, axes),
        out_shape=(
            jax.ShapeDtypeStruct(projected.shape, jnp.bfloat16),
            jax.ShapeDtypeStruct((tokens, KEYS), jnp.float32),
            jax.ShapeDtypeStruct((8, HEAD_V), jnp.float32),
        ),
        in_specs=[pl.BlockSpec(memory_space=pltpu.SMEM)] + whole_specs(8),
        out_specs=tuple(whole_specs(3)),
        scratch_shapes=[
            pltpu.VMEM((tokens, VALS), jnp.bfloat16),
            pltpu.VMEM((pieces, chunks, HEAD_V, HEAD_K), jnp.float32),
            pltpu.VMEM(state, jnp.float32),
            pltpu.VMEM((tokens, KEYS), jnp.float32),
            pltpu.VMEM((tokens, VALS), jnp.float32),
            pltpu.VMEM((tokens, KEYS), jnp.float32),
            *line_scratch(pieces),
        ],
        compiler_params=pltpu.CompilerParams(
            collective_id=2, has_side_effects=True, vmem_limit_bytes=56 * 2**20
        ),
        cost_estimate=pl.CostEstimate(
            flops=60_000_000_000, bytes_accessed=220_000_000, transcendentals=0
        ),
        name="mix_backward",
    )(
        prefix_len,
        projected,
        cum,
        states,
        prefix_state,
        gated_grad,
        unit,
        scale,
        group_gain,
    )


FFN_BLOCK = 256
FFN_ROWS = 512


def ffn_kernel(
    rows_ref,
    grad_ref,
    mine_ref,
    other_ref,
    grad_mine_ref,
    grad_other_ref,
    weight_ref,
    out_ref,
    drows_ref,
    gate_sum_ref,
    up_sum_ref,
    down_sum_ref,
    pair_slots,
    down_slots,
    hidden_ref,
    dpair_ref,
    turned,
    given,
    taken,
    load_sem,
    sent_sem,
    got_sem,
):
    blocks = FF // FFN_BLOCK
    tokens = rows_ref.shape[0]
    other_core = {"core": 1 - lax.axis_index("core")}
    barrier = pltpu.get_barrier_semaphore()
    pl.semaphore_signal(barrier, inc=1, device_id=other_core, device_id_type=MESH)
    pl.semaphore_wait(barrier, 1)
    first, second = slice(0, FFN_BLOCK), slice(FFN_BLOCK, 2 * FFN_BLOCK)

    def load(block, part):
        begin = pl.multiple_of(part * FF + block * FFN_BLOCK, FFN_BLOCK)
        slot = lax.rem(block, 2)
        target = down_slots.at[slot] if part == 2 else pair_slots.at[slot, :, (first, second)[part]]
        return pltpu.make_async_copy(
            weight_ref.at[:, pl.ds(begin, FFN_BLOCK)], target, load_sem.at[slot, part]
        )

    def give(block):
        return pltpu.make_async_remote_copy(
            src_ref=given.at[lax.rem(block, 2)],
            dst_ref=taken.at[block],
            send_sem=sent_sem.at[block],
            recv_sem=got_sem.at[block],
            device_id=other_core,
            device_id_type=MESH,
        )

    def take(block):
        give(block).wait_recv()
        columns = pl.ds(pl.multiple_of(block * FFN_BLOCK, FFN_BLOCK), FFN_BLOCK)
        for part, sum_ref in enumerate((gate_sum_ref, up_sum_ref, down_sum_ref)):
            at = slice(part * FFN_BLOCK, (part + 1) * FFN_BLOCK)
            sum_ref[:, columns] = low(wide(sum_ref[:, columns]) + wide(taken[block, :, at]))

    for part in range(3):
        load(0, part).start()

    def turn(i, carry):
        begin = pl.multiple_of(i * FFN_BLOCK, FFN_BLOCK)
        at = pl.ds(begin, FFN_BLOCK)
        for which, ref in enumerate((mine_ref, other_ref, grad_mine_ref, grad_other_ref)):
            turned[which, :, at] = jnp.transpose(ref[at, :])
        out_ref[at, :] = jnp.zeros((FFN_BLOCK, out_ref.shape[1]), jnp.float32)
        drows_ref[at, :] = jnp.zeros((FFN_BLOCK, out_ref.shape[1]), jnp.float32)
        return carry

    lax.fori_loop(0, tokens // FFN_BLOCK, turn, 0)

    def one(block, carry):
        slot = lax.rem(block, 2)

        @pl.when(block < blocks - 1)
        def _():
            for part in range(3):
                load(block + 1, part).start()

        @pl.when(block > 1)
        def _():
            give(block - 2).wait_send()

        for part in range(3):
            load(block, part).wait()
        columns = pl.ds(pl.multiple_of(block * FFN_BLOCK, FFN_BLOCK), FFN_BLOCK)
        for tile in range(tokens // FFN_ROWS):
            at = slice(tile * FFN_ROWS, (tile + 1) * FFN_ROWS)
            both = nn(rows_ref[at], pair_slots[slot])
            dhidden = nn(grad_ref[at], down_slots[slot])
            gate = both[:, first]
            up = both[:, second]
            logistic = 0.5 * jnp.tanh(0.5 * gate) + 0.5
            active = gate * logistic
            hidden_ref[at] = low(active * up)
            dpair_ref[at, first] = low(dhidden * up * (logistic + active * (1.0 - logistic)))
            dpair_ref[at, second] = low(dhidden * active)
        for tile in range(tokens // FFN_ROWS):
            at = slice(tile * FFN_ROWS, (tile + 1) * FFN_ROWS)
            out_ref[at] += nt(hidden_ref[at], down_slots[slot])
            drows_ref[at] += nt(dpair_ref[at], pair_slots[slot])
        given[slot, :, : 2 * FFN_BLOCK] = low(nn(turned[1], dpair_ref[...]))
        given[slot, :, 2 * FFN_BLOCK :] = low(nn(turned[3], hidden_ref[...]))
        give(block).start()
        pair = nn(turned[0], dpair_ref[...])
        gate_sum_ref[:, columns] = low(pair[:, first])
        up_sum_ref[:, columns] = low(pair[:, second])
        down_sum_ref[:, columns] = low(nn(turned[2], hidden_ref[...]))

        @pl.when(block > 0)
        def _():
            take(block - 1)

        return carry

    lax.fori_loop(0, blocks, one, 0)
    take(blocks - 1)
    give(blocks - 2).wait_send()
    give(blocks - 1).wait_send()


def ffn_both(rows, grad, row_halves, grad_halves, weights):
    tokens, width = rows.shape
    half = width // 2
    blocks = FF // FFN_BLOCK
    share = jax.ShapeDtypeStruct((half, FF), jnp.bfloat16)
    total = jax.ShapeDtypeStruct((tokens, width), jnp.float32)
    return pl.pallas_call(
        ffn_kernel,
        out_shape=(total, total, share, share, share),
        in_specs=whole_specs(6) + [pl.BlockSpec(memory_space=pl.ANY)],
        out_specs=tuple(whole_specs(5)),
        scratch_shapes=[
            pltpu.VMEM((2, width, 2 * FFN_BLOCK), jnp.bfloat16),
            pltpu.VMEM((2, width, FFN_BLOCK), jnp.bfloat16),
            pltpu.VMEM((tokens, FFN_BLOCK), jnp.bfloat16),
            pltpu.VMEM((tokens, 2 * FFN_BLOCK), jnp.bfloat16),
            pltpu.VMEM((4, half, tokens), jnp.bfloat16),
            pltpu.VMEM((2, half, 3 * FFN_BLOCK), jnp.bfloat16),
            pltpu.VMEM((blocks, half, 3 * FFN_BLOCK), jnp.bfloat16),
            pltpu.SemaphoreType.DMA((2, 3)),
            pltpu.SemaphoreType.DMA((blocks,)),
            pltpu.SemaphoreType.DMA((blocks,)),
        ],
        compiler_params=pltpu.CompilerParams(
            collective_id=5, has_side_effects=True, vmem_limit_bytes=58 * 2**20
        ),
        name="ffn_both",
    )(rows, grad, *row_halves, *grad_halves, weights)


EXTRA = 128


def physical_axes(mesh):
    shape = mesh.devices.shape
    names = []
    sizes = []
    for axis, extent in enumerate(shape):
        line = np.moveaxis(mesh.devices, axis, 0).reshape(extent, -1)[:, 0]
        places = [tuple(d.coords) + (d.core_on_chip,) for d in line]
        parts = []
        for dim, label in enumerate(("x", "y", "z", "core")):
            values = [p[dim] for p in places]
            if len(set(values)) > 1:
                step = next(i for i in range(extent) if values[i] != values[0])
                parts.append((step, label, len(set(values))))
        for step, label, size in sorted(parts, reverse=True):
            names.append(label)
            sizes.append(size)
    return tuple(names), tuple(sizes)


def pack_small(norm1_gain, norm2_gain, down, up, bias, group):
    rows = down.shape[0]

    def column(vector):
        return jnp.pad(vector, (0, rows - vector.shape[0]))[:, None]

    pieces = [
        down,
        column(norm1_gain),
        column(norm2_gain),
        column(bias),
        column(group),
        jnp.zeros((rows, 4), down.dtype),
        up.T.reshape(rows, 8),
        jnp.zeros((rows, EXTRA - 32), down.dtype),
    ]
    return jnp.concatenate(pieces, axis=1)


def unpack_small(small, devices):
    rows = small.shape[0] // devices
    by_device = small.reshape(devices, rows, EXTRA)
    down = small[:, :16]
    gain_one = small[:, 16]
    gain_two = small[:, 17]
    bias = by_device[:, : KEYS // devices, 18].reshape(KEYS)
    group = by_device[:, : HEAD_V // devices, 19].reshape(HEAD_V)
    up = small[:, 24:32].reshape(KEYS, 16).T
    return down, gain_one, gain_two, bias, group, up


def pack_small_grads(down, gain_one, gain_two, bias, group, up, devices):
    rows = gain_one.shape[0] // devices

    def column(vector):
        parts = vector.reshape(devices, -1)
        parts = jnp.pad(parts, ((0, 0), (0, rows - parts.shape[1])))
        return parts.reshape(devices * rows, 1)

    pieces = [
        down,
        gain_one[:, None],
        gain_two[:, None],
        column(bias),
        column(group),
        jnp.zeros((rows * devices, 4), jnp.float32),
        up.T.reshape(rows * devices, 8),
        jnp.zeros((rows * devices, EXTRA - 32), jnp.float32),
    ]
    return jnp.concatenate(pieces, axis=1)


def core_halves(rows, names, sizes):
    width = rows.shape[1]
    at = names.index("core")
    before = int(np.prod(sizes[:at], initial=1))
    after = width // before // sizes[at]
    core = lax.axis_index("core")

    def half(which):
        return jnp.concatenate(
            [
                lax.dynamic_slice_in_dim(rows, (2 * i + which) * after, after, 1)
                for i in range(before)
            ],
            axis=1,
        )

    return half(core), half(1 - core)


def swap_cores(values):
    return lax.ppermute(values, "core", [(0, 1), (1, 0)])


def pair_sum(halves, gradient):
    mine, other = halves
    taken = swap_cores(flat_grad(other, gradient).astype(jnp.bfloat16))
    return (flat_grad(mine, gradient) + taken.astype(jnp.float32)).astype(jnp.bfloat16)


def flat_grad(inputs, gradient):
    return jnp.einsum("td,te->de", inputs, gradient, preferred_element_type=jnp.float32)


def by_chip(values, names, sizes):
    chips = tuple(size for name, size in zip(names, sizes) if name != "core")
    return values.reshape(*chips, -1, values.shape[-1])


def pass_along(values, left, name):
    at = left.index(name)
    size = values.shape[at]
    own = lax.axis_index(name)
    arrived = []
    for shift in range(1, size):
        given = lax.dynamic_index_in_dim(values, lax.rem(own + shift, size), at, False)
        arrived.append(
            lax.ppermute(given, name, [(i, (i + shift) % size) for i in range(size)])
        )
    return arrived


def take_in(values, arrived, left, name):
    at = left.index(name)
    total = lax.dynamic_index_in_dim(values, lax.axis_index(name), at, False).astype(jnp.float32)
    for term in arrived:
        total = total + term.astype(jnp.float32)
    return total, [other for other in left if other != name]


def reduce_kernel(plan, *refs):
    inputs, jobs, sizes, slots = plan
    count = len(jobs)
    in_refs = refs[:inputs]
    outputs = max(job[4] for job in jobs) + 1
    out_refs = refs[inputs : inputs + outputs]
    scratch = refs[inputs + outputs :]
    send_sem, recv_sem = scratch[-2:]
    scratch = list(scratch[:-2])

    reached = sorted({name for job in jobs for name in job[3]})
    barrier = pltpu.get_barrier_semaphore()
    peers = 0
    for name in reached:
        for shift in range(1, sizes[name]):
            peer = lax.rem(lax.axis_index(name) + shift, sizes[name])
            pl.semaphore_signal(barrier, inc=1, device_id={name: peer}, device_id_type=MESH)
            peers += 1
    pl.semaphore_wait(barrier, peers)

    class Job:
        pass

    work = []
    slot = 0
    for which, columns, axes, order, out, out_columns in jobs:
        job = Job()
        job.left = list(axes)
        job.order = order
        job.out = out_refs[out]
        job.out_columns = slice(*out_columns)
        job.source = in_refs[which]
        job.columns = slice(*columns)
        job.got = [scratch.pop(0) for _ in order]
        job.kept = [scratch.pop(0) for _ in order[:-1]]
        job.slots = []
        for name in order:
            job.slots.append(slot)
            slot += sizes[name] - 1
        work.append(job)

    def part(job, index):
        at = job.left.index(job.order[job.step])
        lead = [slice(None)] * len(job.left)
        lead[at] = index
        return job.source.at[(*lead, slice(None), job.columns)]

    def copies(job):
        name = job.order[job.step]
        own = lax.axis_index(name)
        for shift in range(1, sizes[name]):
            peer = lax.rem(own + shift, sizes[name])
            at = job.slots[job.step] + shift - 1
            yield pltpu.make_async_remote_copy(
                src_ref=part(job, peer),
                dst_ref=job.got[job.step].at[shift - 1],
                send_sem=send_sem.at[at],
                recv_sem=recv_sem.at[at],
                device_id={name: peer},
                device_id_type=MESH,
            )

    def start(job):
        for copy in copies(job):
            copy.start()

    def add(job):
        name = job.order[job.step]
        at = job.left.index(name)
        own = lax.axis_index(name)
        rest = [n for n in job.left if n != name]
        last = job.step == len(job.order) - 1
        total = int(np.prod([sizes[n] for n in rest], initial=1))
        got = job.got[job.step]
        for copy in copies(job):
            copy.wait()
        source, columns, step = job.source, job.columns, job.step

        def one(i, carry):
            index = []
            for n in reversed(rest):
                index.insert(0, lax.rem(i, sizes[n]))
                i = lax.div(i, sizes[n])
            lead = list(index)
            lead.insert(at, own)
            value = source[(*lead, slice(None), columns)].astype(jnp.float32)
            for shift in range(1, sizes[name]):
                value = value + got[(shift - 1, *index)].astype(jnp.float32)
            if last:
                job.out[:, job.out_columns] = value
            else:
                job.kept[step][tuple(index)] = value.astype(jnp.bfloat16)
            return carry

        if total == 1:
            one(jnp.int32(0), 0)
        else:
            lax.fori_loop(0, total, one, 0)
        job.left = rest
        if not last:
            job.source = job.kept[step]
            job.columns = slice(None)
            job.step += 1
            start(job)

    for job in work:
        job.step = 0
        start(job)
    for step in range(max(len(job.order) for job in work)):
        for job in work:
            if len(job.order) > step:
                add(job)


def reduce_rest(arrays, jobs, sizes, rows, widths, collective):
    scratch = []
    slots = 0
    for which, (begin, end), axes, order, out, out_columns in jobs:
        left = list(axes)
        kept = []
        got = []
        for name in order:
            left.remove(name)
            shape = tuple(sizes[n] for n in left)
            got.append(pltpu.VMEM((sizes[name] - 1, *shape, rows, end - begin), jnp.bfloat16))
            kept.append(pltpu.VMEM((*shape, rows, end - begin), jnp.bfloat16))
            slots += sizes[name] - 1
        scratch += got + kept[:-1]
    scratch += [pltpu.SemaphoreType.DMA((slots,))] * 2
    return pl.pallas_call(
        partial(reduce_kernel, (len(arrays), jobs, sizes, slots)),
        out_shape=tuple(jax.ShapeDtypeStruct((rows, width), jnp.float32) for width in widths),
        in_specs=whole_specs(len(arrays)),
        out_specs=tuple(whole_specs(len(widths))),
        scratch_shapes=scratch,
        compiler_params=pltpu.CompilerParams(
            collective_id=collective, has_side_effects=True, vmem_limit_bytes=40 * 2**20
        ),
        name="reduce_rest",
    )(*arrays)


def chip_orders(names):
    first, second, last = [name for name in names if name != "core"]
    return (first, second, last), (second, last, first), (last, first, second)


def two_orders(names):
    first, second, last = [name for name in names if name != "core"]
    return (first, second, last), (second, last, first)


def last_orders(names):
    first, second, last = [name for name in names if name != "core"]
    return (first, second, last), (second, first, last)


def local(
    names,
    sizes,
    seq_axes,
    tokens,
    prefix_len,
    norm1_gain,
    query_weight,
    key_weight,
    value_weight,
    gate_weight,
    decay_down,
    decay_up,
    decay_bias,
    group_gain,
    out_weight,
    norm2_gain,
    ffn_gate,
    ffn_up,
    ffn_down,
    out_grad,
):
    devices = int(np.prod(sizes))
    orders = chip_orders(names)
    wide_order, long_order, late_order = (order[::-1] for order in orders)
    small_shard = pack_small(norm1_gain, norm2_gain, decay_down, decay_up, decay_bias, group_gain)
    first, small_full = gather_first(
        names,
        sizes,
        (query_weight, key_weight, value_weight, gate_weight, small_shard),
        (3072, EXTRA),
        (
            (3, 0, (0, 1024), (2048, 3072), wide_order),
            (4, 1, (0, EXTRA), (0, EXTRA), wide_order),
            (0, 0, (0, 128), (0, 128), wide_order),
            (2, 0, (0, 1024), (1024, 2048), long_order),
            (0, 0, (128, 384), (128, 384), long_order),
            (1, 0, (0, 512), (512, 1024), late_order),
            (0, 0, (384, 512), (384, 512), late_order),
        ),
    )
    ffn_shard = jnp.concatenate([ffn_gate, ffn_up, ffn_down.T, out_weight], axis=1)
    ffn_full = lax.all_gather(ffn_shard, names, axis=0, tiled=True)
    weight_o = ffn_full[:, 3 * FF :]
    mixer_full = first.reshape(-1, 3072)
    small_full = small_full.reshape(-1, EXTRA)
    weight_down, gain_one, gain_two, bias_full, gain_group, weight_up = unpack_small(
        small_full, devices
    )
    seq_count, tok_count, feature_count = tokens.shape
    rows = seq_count * tok_count
    resid_in = tokens.reshape(rows, feature_count).astype(jnp.float32)
    scale_one = rms_scale(resid_in)
    unit_one = resid_in * scale_one
    normed = (unit_one * gain_one.astype(jnp.float32)).astype(jnp.bfloat16)
    projected = project(normed, mixer_full).astype(jnp.bfloat16)
    lowrank = project(normed, weight_down).astype(jnp.bfloat16)
    logits = project(lowrank, weight_up) + bias_full.astype(jnp.float32)
    decays = jax.nn.log_sigmoid(logits) / 16.0
    wide_gain = jnp.broadcast_to(gain_group.astype(jnp.float32)[None], (8, HEAD_V))
    gated_rows, unit_group, scale_group, cum, states, prefix_state = mix_forward(
        seq_axes, prefix_len, projected, decays, wide_gain
    )
    resid_mid = resid_in + project(gated_rows, weight_o)
    scale_two = rms_scale(resid_mid)
    unit_two = resid_mid * scale_two
    normed_two = (unit_two * gain_two.astype(jnp.float32)).astype(jnp.bfloat16)
    out_grad = out_grad.reshape(rows, feature_count)
    grad_out = out_grad.astype(jnp.float32)
    ffn_out, grad_normed_two, gate_sum, up_sum, down_sum = ffn_both(
        normed_two,
        out_grad,
        core_halves(normed_two, names, sizes),
        core_halves(out_grad, names, sizes),
        ffn_full,
    )
    layer_out = (resid_mid + ffn_out).astype(jnp.bfloat16)
    gain_two_grad = jnp.sum(grad_normed_two * unit_two, axis=0)
    grad_mid = grad_out + rms_back(
        grad_normed_two * gain_two.astype(jnp.float32), unit_two, scale_two
    )
    grad_branch = grad_mid.astype(jnp.bfloat16)
    gated_grad = back_project(grad_branch, weight_o).astype(jnp.bfloat16)
    out_sum = pair_sum(core_halves(gated_rows, names, sizes), grad_branch)
    groups = (
        jnp.concatenate([gate_sum, out_sum, down_sum[:, :896]], axis=1),
        jnp.concatenate([up_sum, down_sum[:, 896:]], axis=1),
    )
    groups, gated_grad = lax.optimization_barrier((groups, gated_grad))
    chips = [name for name in names if name != "core"]
    orders = two_orders(names)
    lefts = [chips] * 2
    groups = [by_chip(group, names, sizes) for group in groups]
    arrived = [pass_along(g, left, order[0]) for g, left, order in zip(groups, lefts, orders)]
    grad_projected, grad_decay, group_grad = mix_backward(
        seq_axes,
        prefix_len,
        projected,
        cum,
        states,
        prefix_state,
        gated_grad,
        unit_group,
        scale_group,
        wide_gain,
    )
    arrived, grad_projected, grad_decay = lax.optimization_barrier(
        (arrived, grad_projected, grad_decay)
    )
    taken = [
        take_in(g, more, left, order[0])
        for g, more, left, order in zip(groups, arrived, lefts, orders)
    ]
    groups = [total.astype(jnp.bfloat16) for total, _ in taken]
    lefts = [left for _, left in taken]
    arrived = [pass_along(g, left, order[1]) for g, left, order in zip(groups, lefts, orders)]
    late = flat_grad(normed, grad_projected).astype(jnp.bfloat16)
    grad_logits = (grad_decay * jax.nn.sigmoid(-logits) / 16.0).astype(jnp.bfloat16)
    bias_grad = jnp.sum(grad_logits.astype(jnp.float32), axis=0)
    up_rank_grad = flat_grad(lowrank, grad_logits)
    grad_lowrank = back_project(grad_logits, weight_up).astype(jnp.bfloat16)
    down_rank_grad = flat_grad(normed, grad_lowrank)
    grad_normed = back_project(grad_projected, mixer_full) + back_project(
        grad_lowrank, weight_down
    )
    gain_one_grad = jnp.sum(grad_normed * unit_one, axis=0)
    tokens_grad = grad_mid + rms_back(
        grad_normed * gain_one.astype(jnp.float32), unit_one, scale_one
    )
    small_grads = pack_small_grads(
        down_rank_grad,
        gain_one_grad,
        gain_two_grad,
        bias_grad,
        group_grad[0],
        up_rank_grad,
        devices,
    ).astype(jnp.bfloat16)
    arrived, late, small_grads, tokens_grad = lax.optimization_barrier(
        (arrived, late, small_grads, tokens_grad)
    )
    groups = [
        take_in(g, more, left, order[1])[0].astype(jnp.bfloat16)
        for g, more, left, order in zip(groups, arrived, lefts, orders)
    ]
    own_rows = feature_count // devices
    late = late.reshape(*sizes, own_rows, -1)
    small_grads = small_grads.reshape(*sizes, own_rows, -1)
    size_of = dict(zip(names, sizes))
    ends = last_orders(names)
    jobs = [
        (which, columns, names, ("core", *order), which, columns)
        for which, columns, order in (
            (2, (0, 1536), ends[0]),
            (2, (1536, 3072), ends[1]),
            (3, (0, EXTRA), ends[0]),
        )
    ] + [
        (i, (0, groups[i].shape[-1]), (order[2],), (order[2],), i, (0, groups[i].shape[-1]))
        for i, order in enumerate(orders)
    ]
    first_group, second_group, mine, small = reduce_rest(
        (*groups, late, small_grads), jobs, size_of, own_rows, (4736, 4736, 3072, EXTRA), 3
    )
    shape = tokens.shape
    return (
        layer_out.reshape(shape),
        tokens_grad.reshape(shape),
        small[:, 16],
        mine[:, :512],
        mine[:, 512:1024],
        mine[:, 1024:2048],
        mine[:, 2048:],
        small[:, :16],
        small[:, 24:32].reshape(KEYS // devices, 16).T,
        small[: KEYS // devices, 18],
        small[: HEAD_V // devices, 19],
        first_group[:, FF : FF + VALS],
        small[:, 17],
        first_group[:, :FF],
        second_group[:, :FF],
        jnp.concatenate([first_group[:, FF + VALS :], second_group[:, FF:]], axis=1).T,
    )


def solution(mesh):
    names, sizes = physical_axes(mesh)
    cut = next(
        i for i in range(len(sizes) + 1) if np.prod(sizes[:i], initial=1) == mesh.shape["dp"]
    )
    dp, seq = names[:cut], names[cut:]
    split = Mesh(mesh.devices.reshape(sizes), names)
    return jax.shard_map(
        partial(local, names, sizes, tuple(zip(seq, sizes[cut:]))),
        mesh=split,
        in_specs=(
            P(dp, seq, None),
            P(dp),
            P(names),
            P(names, None),
            P(names, None),
            P(names, None),
            P(names, None),
            P(names, None),
            P(None, names),
            P(names),
            P(names),
            P(names, None),
            P(names),
            P(names, None),
            P(names, None),
            P(None, names),
            P(dp, seq, None),
        ),
        out_specs=(
            P(dp, seq, None),
            P(dp, seq, None),
            P(names),
            P(names, None),
            P(names, None),
            P(names, None),
            P(names, None),
            P(names, None),
            P(None, names),
            P(names),
            P(names),
            P(names, None),
            P(names),
            P(names, None),
            P(names, None),
            P(None, names),
        ),
        check_vma=False,
    )
```

```python
from functools import partial

import jax
import jax.numpy as jnp
import numpy as np
from jax import lax
from jax.experimental import pallas as pl
from jax.experimental.pallas import tpu as pltpu
from jax.sharding import Mesh
from jax.sharding import PartitionSpec as P

KEYS = 512
VALS = 1024
HEADS = 4
SPAN = 64
HEAD_K = 128
HEAD_V = 256
FF = 2816


norm_eps = 1e-05


def project(inputs, weight):
    return jnp.einsum("td,de->te", inputs, weight, preferred_element_type=jnp.float32)


def back_project(gradient, weight):
    return jnp.einsum("te,de->td", gradient, weight, preferred_element_type=jnp.float32)


def rms_scale(values):
    return lax.rsqrt(jnp.mean(values * values, axis=-1, keepdims=True) + norm_eps)


def rms_back(grad_unit, unit_rows, scale_rows):
    return scale_rows * (
        grad_unit - unit_rows * jnp.mean(grad_unit * unit_rows, axis=-1, keepdims=True)
    )


CHUNK = 128
MESH = pl.DeviceIdType.MESH


def nn(a, b):
    return lax.dot_general(a, b, (((1,), (0,)), ((), ())), preferred_element_type=jnp.float32)


def nt(a, b):
    return lax.dot_general(a, b, (((1,), (1,)), ((), ())), preferred_element_type=jnp.float32)


def tn(a, b):
    return lax.dot_general(a, b, (((0,), (0,)), ((), ())), preferred_element_type=jnp.float32)


def low(values):
    return values.astype(jnp.bfloat16)


def wide(values):
    return values.astype(jnp.float32)


def three_way(ones, values):
    first = low(values)
    left = values - wide(first)
    second = low(left)
    third = low(left - wide(second))
    return nn(ones, first) + nn(ones, second) + nn(ones, third)


def logistic_of(values):
    return 0.5 * jnp.tanh(0.5 * values) + 0.5


def iota(shape, dim):
    return lax.broadcasted_iota(jnp.int32, shape, dim)


def place_on(axes):
    place = 0
    for name, size in axes:
        place = place * size + lax.axis_index(name)
    return place


def device_at(axes, place):
    where = {}
    for name, size in reversed(axes):
        where[name] = lax.rem(place, size)
        place = lax.div(place, size)
    return where


def line_length(axes):
    return int(np.prod([size for _, size in axes]))


def greet(axes, place, count, extra=0):
    barrier = pltpu.get_barrier_semaphore()

    @pl.when(place > 0)
    def _():
        pl.semaphore_signal(
            barrier, inc=1, device_id=device_at(axes, place - 1), device_id_type=MESH
        )

    @pl.when(place < count - 1)
    def _():
        pl.semaphore_signal(
            barrier, inc=1, device_id=device_at(axes, place + 1), device_id_type=MESH
        )

    @pl.when(jnp.logical_or(place == 0, place == count - 1))
    def _():
        pl.semaphore_wait(barrier, 1 + extra)

    @pl.when(jnp.logical_and(place > 0, place < count - 1))
    def _():
        pl.semaphore_wait(barrier, 2 + extra)


def send(source, target, send_sem, recv_sem, axes, place):
    return pltpu.make_async_remote_copy(
        src_ref=source,
        dst_ref=target,
        send_sem=send_sem,
        recv_sem=recv_sem,
        device_id=device_at(axes, place),
        device_id_type=MESH,
    )


class Gather:
    def __init__(self, names, sizes, pieces, local_sem, send_sem, recv_sem, pair_send, pair_recv):
        self.names = names
        self.sizes = dict(zip(names, sizes))
        self.pieces = pieces
        self.sems = local_sem, send_sem, recv_sem, pair_send, pair_recv
        self.steps = len(pieces[0][4])

    def region(self, piece, known, at):
        lead = []
        for name in self.names:
            if name in known:
                lead.append(slice(None))
            elif name in at:
                lead.append(at[name])
            else:
                lead.append(lax.axis_index(name))
        _, whole, _, columns, _ = piece
        return whole.at[(*lead, slice(None), slice(*columns))]

    def local(self, i):
        shard, _, columns, _, _ = self.pieces[i]
        return pltpu.make_async_copy(
            shard.at[:, slice(*columns)], self.region(self.pieces[i], (), {}), self.sems[0].at[i]
        )

    def copies(self, i, step):
        piece = self.pieces[i]
        order = piece[4]
        name = order[step]
        own = lax.axis_index(name)
        base = (i * self.steps + step) * 3
        for shift in range(1, self.sizes[name]):
            peer = lax.rem(own + shift, self.sizes[name])
            here = self.region(piece, order[:step], {})
            yield pltpu.make_async_remote_copy(
                src_ref=here,
                dst_ref=here,
                send_sem=self.sems[1].at[base + shift - 1],
                recv_sem=self.sems[2].at[base + shift - 1],
                device_id={name: peer},
                device_id_type=MESH,
            )

    def pair(self, i, step, shift):
        piece = self.pieces[i]
        order = piece[4]
        if step < 0:
            here = self.region(piece, (), {})
            at = 0
        else:
            name = order[step]
            source = lax.rem(lax.axis_index(name) + self.sizes[name] - shift, self.sizes[name])
            here = self.region(piece, order[:step], {name: source})
            at = 1 + step * 3 + shift - 1
        at += i * (1 + 3 * self.steps)
        return pltpu.make_async_remote_copy(
            src_ref=here,
            dst_ref=here,
            send_sem=self.sems[3].at[at],
            recv_sem=self.sems[4].at[at],
            device_id={"core": 1 - lax.axis_index("core")},
            device_id_type=MESH,
        )

    def begin(self):
        for i in range(len(self.pieces)):
            self.local(i).start()
        for i in range(len(self.pieces)):
            self.local(i).wait()
            for copy in self.copies(i, 0):
                copy.start()
            self.pair(i, -1, 0).start()

    def advance(self, step):
        for i, piece in enumerate(self.pieces):
            for copy in self.copies(i, step):
                copy.wait_recv()
            if step < self.steps - 1:
                for copy in self.copies(i, step + 1):
                    copy.start()
            for shift in range(1, self.sizes[piece[4][step]]):
                self.pair(i, step, shift).start()

    def end(self):
        for i, piece in enumerate(self.pieces):
            for step in range(self.steps):
                for copy in self.copies(i, step):
                    copy.wait_send()
                for shift in range(1, self.sizes[piece[4][step]]):
                    self.pair(i, step, shift).wait()
            self.pair(i, -1, 0).wait()

    @staticmethod
    def scratch(count):
        return [
            pltpu.SemaphoreType.DMA((count,)),
            pltpu.SemaphoreType.DMA((count * 9,)),
            pltpu.SemaphoreType.DMA((count * 9,)),
            pltpu.SemaphoreType.DMA((count * 10,)),
            pltpu.SemaphoreType.DMA((count * 10,)),
        ]


def signal_axes(names, sizes):
    barrier = pltpu.get_barrier_semaphore()
    peers = 0
    for name, size in zip(names, sizes):
        for shift in range(1, size):
            peer = lax.rem(lax.axis_index(name) + shift, size)
            pl.semaphore_signal(barrier, inc=1, device_id={name: peer}, device_id_type=MESH)
            peers += 1
    return peers


def gather_kernel(plan, *refs):
    names, sizes, inputs, outputs, pieces = plan
    wholes = refs[inputs : inputs + outputs]
    peers = signal_axes(names, sizes)
    pl.semaphore_wait(pltpu.get_barrier_semaphore(), peers)
    gather = Gather(
        names,
        sizes,
        [(refs[i], wholes[o], cols, to, order) for i, o, cols, to, order in pieces],
        *refs[inputs + outputs :],
    )
    gather.begin()
    for step in range(gather.steps):
        gather.advance(step)
    gather.end()


def gather_first(names, sizes, shards, widths, pieces):
    rows = shards[0].shape[0]
    anywhere = pl.BlockSpec(memory_space=pl.ANY)
    return pl.pallas_call(
        partial(gather_kernel, (names, sizes, len(shards), len(widths), pieces)),
        out_shape=tuple(
            jax.ShapeDtypeStruct((*sizes, rows, width), jnp.bfloat16) for width in widths
        ),
        in_specs=[anywhere] * len(shards),
        out_specs=(anywhere,) * len(widths),
        scratch_shapes=Gather.scratch(len(pieces)),
        compiler_params=pltpu.CompilerParams(collective_id=4, has_side_effects=True),
        name="gather_first",
    )(*shards)


def row_places(count):
    return iota((count, HEAD_K), 0)


def both_ways(seqs, place, count, go_right, go_left):
    behind = count - 1 - place

    def step(seq, carry):
        for head in range(HEADS):

            @pl.when(seq < seqs)
            def _():
                go_right(seq, head)

            @pl.when(jnp.logical_and(seq >= behind, seq < behind + seqs))
            def _():
                go_left(seq - behind, head)

        return carry

    lax.fori_loop(0, seqs + count - 1, step, 0)


def prefix_weights(cum, end_local, count):
    rows = row_places(count)
    owner = jnp.logical_and(end_local >= 0, end_local < count)
    end_cum = jnp.sum(jnp.where(rows == end_local, cum, 0.0), axis=0, keepdims=True)
    keep = jnp.logical_and(rows <= end_local, rows <= jnp.where(owner, count, -1))
    weights = jnp.where(keep, jnp.exp(jnp.where(keep, end_cum - cum, 0.0)), 0.0)
    return weights, jnp.exp(end_cum) * jnp.where(owner, 1.0, 0.0)


def chunk_parts(cum, chunk):
    begin = chunk * CHUNK
    piece = cum[begin : begin + CHUNK]
    if chunk:
        piece = piece - cum[begin - 1 : begin]
    return piece, piece[CHUNK - 1 :], piece[CHUNK // 2 - 1 : CHUNK // 2]


def query_columns(head):
    return slice(head * HEAD_K, (head + 1) * HEAD_K)


def key_columns(head):
    return slice(KEYS + head * HEAD_K, KEYS + (head + 1) * HEAD_K)


def value_columns(head):
    return slice(2 * KEYS + head * HEAD_V, 2 * KEYS + (head + 1) * HEAD_V)


def gate_columns(head):
    begin = 2 * KEYS + VALS + head * HEAD_V
    return slice(begin, begin + HEAD_V)


def forward_kernel(plan, *refs):
    axes = plan
    prefix_ref, proj_ref, decay_ref, gain_ref = refs[:4]
    gated_ref, unit_ref, scale_ref, cum_ref, state_ref, prefix_state_ref = refs[4:10]
    mixed_ref, kv_ref, part_ref, edge_ref, *line = refs[10:]
    right_out, right_in, left_out, left_in, right_sent, right_got, left_sent, left_got = line
    count = line_length(axes)
    place = place_on(axes)
    seqs = prefix_ref.shape[0]
    toks = proj_ref.shape[0] // seqs
    chunks = toks // CHUNK
    greet(axes, place, count)
    lower = low(jnp.where(iota((CHUNK, CHUNK), 0) >= iota((CHUNK, CHUNK), 1), 1.0, 0.0))
    causal = iota((CHUNK, CHUNK), 0) >= iota((CHUNK, CHUNK), 1)

    def to_right(i):
        return send(right_out.at[i], right_in.at[i], right_sent.at[i], right_got.at[i], axes, place + 1)

    def to_left(i):
        return send(left_out.at[i], left_in.at[i], left_sent.at[i], left_got.at[i], axes, place - 1)

    def states_of(seq, carry):
        rows = pl.ds(pl.multiple_of(seq * toks, toks), toks)
        end_local = prefix_ref[seq] - 1 - place * toks
        locals_ = []
        for head in range(HEADS):
            i = seq * HEADS + head
            keys = query_columns(head)
            before = jnp.zeros((1, HEAD_K), jnp.float32)
            key = wide(proj_ref[rows, key_columns(head)])
            value = proj_ref[rows, value_columns(head)]
            decay = decay_ref[rows, keys]
            pieces = []
            local = jnp.zeros((HEAD_V, HEAD_K), jnp.float32)
            for chunk in range(chunks):
                at = slice(chunk * CHUNK, (chunk + 1) * CHUNK)
                piece = three_way(lower, decay[at])
                total = piece[CHUNK - 1 :]
                share = tn(value[at], low(key[at] * jnp.exp(total - piece)))
                kv_ref[i, chunk] = share
                local = jnp.exp(total) * local + share
                pieces.append(piece + before)
                before = before + total
            cum = jnp.concatenate(pieces, axis=0)
            cum_ref[rows, keys] = cum
            weights, edge = prefix_weights(cum, end_local, toks)
            part_ref[i] = tn(value, low(key * weights))
            edge_ref[i] = jnp.broadcast_to(edge, (8, HEAD_K))
            locals_.append(low(local))

        @pl.when(place == 0)
        def _():
            for head in range(HEADS):
                i = seq * HEADS + head
                right_out[i] = locals_[head]
                if count > 1:
                    to_right(i).start()

        return carry

    lax.fori_loop(0, seqs, states_of, 0)

    def go_right(seq, head):
        rows = pl.ds(pl.multiple_of(seq * toks, toks), toks)
        i = seq * HEADS + head
        vals = slice(head * HEAD_V, (head + 1) * HEAD_V)
        cum = cum_ref[rows, query_columns(head)]

        @pl.when(place == 0)
        def _():
            right_in[i] = jnp.zeros((HEAD_V, HEAD_K), jnp.bfloat16)

        @pl.when(place > 0)
        def _():
            send(
                right_out.at[i], right_in.at[i], right_sent.at[i], right_got.at[i], axes, place - 1
            ).wait_recv()

        state = wide(right_in[i])
        part = part_ref[i] + edge_ref[i][:1] * state
        part_ref[i] = part
        for chunk in range(chunks):
            state_ref[i, chunk] = low(state)
            state = jnp.exp(chunk_parts(cum, chunk)[1]) * state + kv_ref[i, chunk]
        state_ref[i, chunks] = low(state)

        @pl.when(jnp.logical_and(place > 0, place < count - 1))
        def _():
            right_out[i] = low(state)
            to_right(i).start()

        if count > 1:

            @pl.when(place == count - 1)
            def _():
                left_out[i] = low(part)
                to_left(i).start()

        query = wide(proj_ref[rows, query_columns(head)])
        key = wide(proj_ref[rows, key_columns(head)])
        value = proj_ref[rows, value_columns(head)]
        for chunk in range(chunks):
            at = slice(chunk * CHUNK, (chunk + 1) * CHUNK)
            piece, total, middle = chunk_parts(cum, chunk)
            raw = nt(
                low(query[at] * jnp.exp(piece - middle)), low(key[at] * jnp.exp(middle - piece))
            )
            mixed_ref[pl.ds(seq * toks + chunk * CHUNK, CHUNK), vals] = nn(
                low(jnp.where(causal, raw, 0.0)), value[at]
            ) + nt(low(query[at] * jnp.exp(piece)), state_ref[i, chunk])

    def go_left(seq, head):
        rows = pl.ds(pl.multiple_of(seq * toks, toks), toks)
        end_local = prefix_ref[seq] - 1 - place * toks
        inside = iota((toks, HEAD_V), 0) <= end_local
        i = seq * HEADS + head
        vals = slice(head * HEAD_V, (head + 1) * HEAD_V)

        @pl.when(place < count - 1)
        def _():
            send(
                left_out.at[i], left_in.at[i], left_sent.at[i], left_got.at[i], axes, place + 1
            ).wait_recv()

        @pl.when(place == count - 1)
        def _():
            left_in[i] = jnp.zeros((HEAD_V, HEAD_K), jnp.bfloat16)

        whole = low(part_ref[i] + wide(left_in[i]))

        @pl.when(jnp.logical_and(place > 0, place < count - 1))
        def _():
            left_out[i] = whole
            to_left(i).start()

        prefix_state_ref[i] = whole
        mixed = jnp.where(
            inside, nt(proj_ref[rows, query_columns(head)], whole), mixed_ref[rows, vals]
        )
        scale = lax.rsqrt(jnp.mean(mixed * mixed, axis=1, keepdims=True) + norm_eps)
        unit = mixed * scale
        gate = wide(proj_ref[rows, gate_columns(head)])
        gated_ref[rows, vals] = low(unit * gain_ref[:1] * gate * logistic_of(gate))
        unit_ref[rows, vals] = low(unit)
        scale_ref[rows, slice(head, head + 1)] = scale

    both_ways(seqs, place, count, go_right, go_left)

    def finish(i, carry):
        @pl.when(place < count - 1)
        def _():
            to_right(i).wait_send()

        @pl.when(place > 0)
        def _():
            to_left(i).wait_send()

        return carry

    lax.fori_loop(0, seqs * HEADS, finish, 0)


def backward_kernel(
    axes,
    prefix_ref,
    proj_ref,
    cum_ref,
    state_ref,
    prefix_state_ref,
    gated_grad_ref,
    unit_ref,
    scale_ref,
    gain_ref,
    dproj_ref,
    ddecay_ref,
    gain_grad_ref,
    grad_ref,
    local_ref,
    acc_ref,
    dk_part,
    dv_part,
    dcum_part,
    right_out,
    right_in,
    left_out,
    left_in,
    right_sent,
    right_got,
    left_sent,
    left_got,
):
    count = line_length(axes)
    place = place_on(axes)
    seqs = prefix_ref.shape[0]
    toks = proj_ref.shape[0] // seqs
    chunks = toks // CHUNK
    greet(axes, place, count)
    causal = iota((CHUNK, CHUNK), 0) >= iota((CHUNK, CHUNK), 1)
    upper = low(jnp.where(iota((toks, toks), 0) <= iota((toks, toks), 1), 1.0, 0.0))

    def to_right(i):
        return send(right_out.at[i], right_in.at[i], right_sent.at[i], right_got.at[i], axes, place + 1)

    def to_left(i):
        return send(left_out.at[i], left_in.at[i], left_sent.at[i], left_got.at[i], axes, place - 1)

    def shares_of(seq, carry):
        rows = pl.ds(pl.multiple_of(seq * toks, toks), toks)
        end_local = prefix_ref[seq] - 1 - place * toks
        inside = iota((toks, HEAD_V), 0) <= end_local
        shares = []
        gain = gain_ref[:1]
        gain_grad = jnp.zeros((1, HEAD_V), jnp.float32)
        for head in range(HEADS):
            i = seq * HEADS + head
            vals = slice(head * HEAD_V, (head + 1) * HEAD_V)
            cum = cum_ref[rows, query_columns(head)]
            query = proj_ref[rows, query_columns(head)]
            gate = wide(proj_ref[rows, gate_columns(head)])
            logistic = logistic_of(gate)
            unit = wide(unit_ref[rows, vals])
            gated_grad = wide(gated_grad_ref[rows, vals])
            through = gated_grad * unit
            active = gate * logistic
            dproj_ref[rows, gate_columns(head)] = low(
                through * gain * (logistic + active * (1.0 - logistic))
            )
            gain_grad = gain_grad + jnp.sum(through * active, axis=0, keepdims=True)
            weighted = gated_grad * active * gain
            grad = scale_ref[rows, slice(head, head + 1)] * (
                weighted - unit * jnp.mean(weighted * unit, axis=1, keepdims=True)
            )
            grad_ref[rows, vals] = low(grad)
            share = tn(low(jnp.where(inside, grad, 0.0)), query)
            acc_ref[i] = share
            shares.append(low(share))
            later = low(jnp.where(inside, 0.0, grad))
            for chunk in range(chunks):
                at = slice(chunk * CHUNK, (chunk + 1) * CHUNK)
                piece, total, middle = chunk_parts(cum, chunk)
                local_ref[i, chunk] = tn(later[at], low(wide(query[at]) * jnp.exp(piece)))
        gain_grad_ref[:1] += gain_grad

        @pl.when(place == 0)
        def _():
            for head in range(HEADS):
                i = seq * HEADS + head
                right_out[i] = shares[head]
                if count > 1:
                    to_right(i).start()

        return carry

    gain_grad_ref[...] = jnp.zeros_like(gain_grad_ref)
    lax.fori_loop(0, seqs, shares_of, 0)

    def go_right(seq, head):
        rows = pl.ds(pl.multiple_of(seq * toks, toks), toks)
        end_local = prefix_ref[seq] - 1 - place * toks
        inside = iota((toks, HEAD_V), 0) <= end_local
        at_end = iota((toks, HEAD_K), 0) == end_local
        i = seq * HEADS + head
        cum = cum_ref[rows, query_columns(head)]

        @pl.when(place == 0)
        def _():
            right_in[i] = jnp.zeros((HEAD_V, HEAD_K), jnp.bfloat16)

        @pl.when(place > 0)
        def _():
            send(
                right_out.at[i], right_in.at[i], right_sent.at[i], right_got.at[i], axes, place - 1
            ).wait_recv()

        acc = acc_ref[i] + wide(right_in[i])
        narrow_acc = low(acc)

        @pl.when(jnp.logical_and(place > 0, place < count - 1))
        def _():
            right_out[i] = narrow_acc
            to_right(i).start()

        weights, edge = prefix_weights(cum, end_local, toks)
        local = jnp.zeros((HEAD_V, HEAD_K), jnp.float32)
        starts = []
        for chunk in reversed(range(chunks)):
            starts.append(low(local))
            local = jnp.exp(chunk_parts(cum, chunk)[1]) * local + local_ref[i, chunk]
        starts = starts[::-1]
        local = local + edge * acc
        acc_ref[i] = local
        if count > 1:

            @pl.when(place == count - 1)
            def _():
                left_out[i] = low(local)
                to_left(i).start()

        keys = query_columns(head)
        vals = slice(head * HEAD_V, (head + 1) * HEAD_V)
        query = wide(proj_ref[rows, query_columns(head)])
        key = wide(proj_ref[rows, key_columns(head)])
        value = proj_ref[rows, value_columns(head)]
        grad = wide(grad_ref[rows, vals])
        later = low(jnp.where(inside, 0.0, grad))
        prefix_state = prefix_state_ref[i]
        weighted = low(key * weights)
        dk_all = weights * nn(value, narrow_acc)
        dv_all = nt(weighted, narrow_acc)
        dq_all = nn(low(jnp.where(inside, grad, 0.0)), prefix_state)
        dqs, dks, dvs, dcs = [], [], [], []
        for chunk in range(chunks):
            at = slice(chunk * CHUNK, (chunk + 1) * CHUNK)
            piece, total, middle = chunk_parts(cum, chunk)
            rise = jnp.exp(piece - middle)
            fall = jnp.exp(middle - piece)
            q_in = low(query[at] * rise)
            k_in = low(key[at] * fall)
            scores = low(jnp.where(causal, nt(q_in, k_in), 0.0))
            d_scores = low(jnp.where(causal, nt(later[at], value[at]), 0.0))
            dq_in = nn(d_scores, k_in)
            dk_in = tn(d_scores, q_in)
            dq_state = jnp.exp(piece) * nn(later[at], state_ref[i, chunk])
            dk_state = dk_all[at]
            dv = tn(scores, later[at]) + dv_all[at]
            if chunk < chunks - 1:
                to_end = jnp.exp(total - piece)
                dk_state = to_end * nn(value[at], starts[chunk]) + dk_state
                dv = dv + nt(low(key[at] * to_end), starts[chunk])
            dqs.append(rise * dq_in + dq_state + dq_all[at])
            dks.append(fall * dk_in + dk_state)
            dvs.append(dv)
            dcs.append(
                wide(q_in) * dq_in
                - wide(k_in) * dk_in
                + query[at] * dq_state
                - key[at] * dk_state
            )
        dproj_ref[rows, query_columns(head)] = low(jnp.concatenate(dqs, axis=0))
        dk_part[rows, keys] = jnp.concatenate(dks, axis=0)
        dv_part[rows, vals] = jnp.concatenate(dvs, axis=0)
        turn = jnp.sum(wide(narrow_acc) * wide(prefix_state), axis=0, keepdims=True)
        dcum_part[rows, keys] = jnp.concatenate(dcs, axis=0) + jnp.where(at_end, turn, 0.0)

    def go_left(seq, head):
        rows = pl.ds(pl.multiple_of(seq * toks, toks), toks)
        i = seq * HEADS + head
        keys = query_columns(head)
        vals = slice(head * HEAD_V, (head + 1) * HEAD_V)

        @pl.when(place < count - 1)
        def _():
            send(
                left_out.at[i], left_in.at[i], left_sent.at[i], left_got.at[i], axes, place + 1
            ).wait_recv()

        @pl.when(place == count - 1)
        def _():
            left_in[i] = jnp.zeros((HEAD_V, HEAD_K), jnp.bfloat16)

        @pl.when(jnp.logical_and(place > 0, place < count - 1))
        def _():
            last = cum_ref[rows, keys][toks - 1 :]
            left_out[i] = low(jnp.exp(last) * wide(left_in[i]) + acc_ref[i])
            to_left(i).start()

        cum = cum_ref[rows, keys]
        key = wide(proj_ref[rows, key_columns(head)])
        value = proj_ref[rows, value_columns(head)]
        after = left_in[i]
        to_end = jnp.exp(cum[toks - 1 :] - cum)
        dk_more = to_end * nn(value, after)
        dproj_ref[rows, key_columns(head)] = low(dk_part[rows, keys] + dk_more)
        dproj_ref[rows, value_columns(head)] = low(
            dv_part[rows, vals] + nt(low(key * to_end), after)
        )
        carry_row = jnp.sum(wide(after) * wide(state_ref[i, chunks]), axis=0, keepdims=True)
        dcum = dcum_part[rows, keys] - key * dk_more
        ddecay_ref[rows, keys] = three_way(upper, dcum) + carry_row

    both_ways(seqs, place, count, go_right, go_left)

    def finish(i, carry):
        @pl.when(place < count - 1)
        def _():
            to_right(i).wait_send()

        @pl.when(place > 0)
        def _():
            to_left(i).wait_send()

        return carry

    lax.fori_loop(0, seqs * HEADS, finish, 0)


def line_scratch(pieces):
    block = pltpu.VMEM((pieces, HEAD_V, HEAD_K), jnp.bfloat16)
    return [block] * 4 + [pltpu.SemaphoreType.DMA((pieces,))] * 4


def whole_specs(count):
    return [pl.BlockSpec(memory_space=pltpu.VMEM)] * count


def mix_forward(axes, prefix_len, projected, decays, group_gain):
    tokens = projected.shape[0]
    seqs = prefix_len.shape[0]
    heads = seqs * HEADS
    chunks = tokens // seqs // CHUNK
    state = (heads, HEAD_V, HEAD_K)
    return pl.pallas_call(
        partial(forward_kernel, axes),
        out_shape=(
            jax.ShapeDtypeStruct((tokens, VALS), jnp.bfloat16),
            jax.ShapeDtypeStruct((tokens, VALS), jnp.bfloat16),
            jax.ShapeDtypeStruct((tokens, 128), jnp.float32),
            jax.ShapeDtypeStruct((tokens, KEYS), jnp.float32),
            jax.ShapeDtypeStruct((heads, chunks + 1, HEAD_V, HEAD_K), jnp.bfloat16),
            jax.ShapeDtypeStruct(state, jnp.bfloat16),
        ),
        in_specs=[pl.BlockSpec(memory_space=pltpu.SMEM)] + whole_specs(3),
        out_specs=tuple(whole_specs(6)),
        scratch_shapes=[
            pltpu.VMEM((tokens, VALS), jnp.float32),
            pltpu.VMEM((heads, chunks, HEAD_V, HEAD_K), jnp.float32),
            pltpu.VMEM(state, jnp.float32),
            pltpu.VMEM((heads, 8, HEAD_K), jnp.float32),
            *line_scratch(heads),
        ],
        compiler_params=pltpu.CompilerParams(
            collective_id=1, has_side_effects=True, vmem_limit_bytes=50 * 2**20
        ),
        cost_estimate=pl.CostEstimate(
            flops=60_000_000_000, bytes_accessed=220_000_000, transcendentals=0
        ),
        name="mix_forward",
    )(prefix_len, projected, decays, group_gain)


def mix_backward(
    axes, prefix_len, projected, cum, states, prefix_state, gated_grad, unit, scale, group_gain
):
    tokens = projected.shape[0]
    seqs = prefix_len.shape[0]
    pieces = seqs * HEADS
    chunks = tokens // seqs // CHUNK
    state = (pieces, HEAD_V, HEAD_K)
    return pl.pallas_call(
        partial(backward_kernel, axes),
        out_shape=(
            jax.ShapeDtypeStruct(projected.shape, jnp.bfloat16),
            jax.ShapeDtypeStruct((tokens, KEYS), jnp.float32),
            jax.ShapeDtypeStruct((8, HEAD_V), jnp.float32),
        ),
        in_specs=[pl.BlockSpec(memory_space=pltpu.SMEM)] + whole_specs(8),
        out_specs=tuple(whole_specs(3)),
        scratch_shapes=[
            pltpu.VMEM((tokens, VALS), jnp.bfloat16),
            pltpu.VMEM((pieces, chunks, HEAD_V, HEAD_K), jnp.float32),
            pltpu.VMEM(state, jnp.float32),
            pltpu.VMEM((tokens, KEYS), jnp.float32),
            pltpu.VMEM((tokens, VALS), jnp.float32),
            pltpu.VMEM((tokens, KEYS), jnp.float32),
            *line_scratch(pieces),
        ],
        compiler_params=pltpu.CompilerParams(
            collective_id=2, has_side_effects=True, vmem_limit_bytes=56 * 2**20
        ),
        cost_estimate=pl.CostEstimate(
            flops=60_000_000_000, bytes_accessed=220_000_000, transcendentals=0
        ),
        name="mix_backward",
    )(
        prefix_len,
        projected,
        cum,
        states,
        prefix_state,
        gated_grad,
        unit,
        scale,
        group_gain,
    )


FFN_BLOCK = 256
FFN_ROWS = 512


def ffn_kernel(
    rows_ref,
    grad_ref,
    mine_ref,
    other_ref,
    grad_mine_ref,
    grad_other_ref,
    weight_ref,
    out_ref,
    drows_ref,
    gate_sum_ref,
    up_sum_ref,
    down_sum_ref,
    pair_slots,
    down_slots,
    hidden_ref,
    dpair_ref,
    turned,
    given,
    taken,
    load_sem,
    sent_sem,
    got_sem,
):
    blocks = FF // FFN_BLOCK
    tokens = rows_ref.shape[0]
    other_core = {"core": 1 - lax.axis_index("core")}
    barrier = pltpu.get_barrier_semaphore()
    pl.semaphore_signal(barrier, inc=1, device_id=other_core, device_id_type=MESH)
    pl.semaphore_wait(barrier, 1)
    first, second = slice(0, FFN_BLOCK), slice(FFN_BLOCK, 2 * FFN_BLOCK)

    def load(block, part):
        begin = pl.multiple_of(part * FF + block * FFN_BLOCK, FFN_BLOCK)
        slot = lax.rem(block, 2)
        target = down_slots.at[slot] if part == 2 else pair_slots.at[slot, :, (first, second)[part]]
        return pltpu.make_async_copy(
            weight_ref.at[:, pl.ds(begin, FFN_BLOCK)], target, load_sem.at[slot, part]
        )

    def give(block):
        return pltpu.make_async_remote_copy(
            src_ref=given.at[lax.rem(block, 2)],
            dst_ref=taken.at[block],
            send_sem=sent_sem.at[block],
            recv_sem=got_sem.at[block],
            device_id=other_core,
            device_id_type=MESH,
        )

    def take(block):
        give(block).wait_recv()
        columns = pl.ds(pl.multiple_of(block * FFN_BLOCK, FFN_BLOCK), FFN_BLOCK)
        for part, sum_ref in enumerate((gate_sum_ref, up_sum_ref, down_sum_ref)):
            at = slice(part * FFN_BLOCK, (part + 1) * FFN_BLOCK)
            sum_ref[:, columns] = low(wide(sum_ref[:, columns]) + wide(taken[block, :, at]))

    for part in range(3):
        load(0, part).start()

    def turn(i, carry):
        begin = pl.multiple_of(i * FFN_BLOCK, FFN_BLOCK)
        at = pl.ds(begin, FFN_BLOCK)
        for which, ref in enumerate((mine_ref, other_ref, grad_mine_ref, grad_other_ref)):
            turned[which, :, at] = jnp.transpose(ref[at, :])
        out_ref[at, :] = jnp.zeros((FFN_BLOCK, out_ref.shape[1]), jnp.float32)
        drows_ref[at, :] = jnp.zeros((FFN_BLOCK, out_ref.shape[1]), jnp.float32)
        return carry

    lax.fori_loop(0, tokens // FFN_BLOCK, turn, 0)

    def one(block, carry):
        slot = lax.rem(block, 2)

        @pl.when(block < blocks - 1)
        def _():
            for part in range(3):
                load(block + 1, part).start()

        @pl.when(block > 1)
        def _():
            give(block - 2).wait_send()

        for part in range(3):
            load(block, part).wait()
        columns = pl.ds(pl.multiple_of(block * FFN_BLOCK, FFN_BLOCK), FFN_BLOCK)
        for tile in range(tokens // FFN_ROWS):
            at = slice(tile * FFN_ROWS, (tile + 1) * FFN_ROWS)
            both = nn(rows_ref[at], pair_slots[slot])
            dhidden = nn(grad_ref[at], down_slots[slot])
            gate = both[:, first]
            up = both[:, second]
            logistic = 0.5 * jnp.tanh(0.5 * gate) + 0.5
            active = gate * logistic
            hidden_ref[at] = low(active * up)
            dpair_ref[at, first] = low(dhidden * up * (logistic + active * (1.0 - logistic)))
            dpair_ref[at, second] = low(dhidden * active)
        for tile in range(tokens // FFN_ROWS):
            at = slice(tile * FFN_ROWS, (tile + 1) * FFN_ROWS)
            out_ref[at] += nt(hidden_ref[at], down_slots[slot])
            drows_ref[at] += nt(dpair_ref[at], pair_slots[slot])
        given[slot, :, : 2 * FFN_BLOCK] = low(nn(turned[1], dpair_ref[...]))
        given[slot, :, 2 * FFN_BLOCK :] = low(nn(turned[3], hidden_ref[...]))
        give(block).start()
        pair = nn(turned[0], dpair_ref[...])
        gate_sum_ref[:, columns] = low(pair[:, first])
        up_sum_ref[:, columns] = low(pair[:, second])
        down_sum_ref[:, columns] = low(nn(turned[2], hidden_ref[...]))

        @pl.when(block > 0)
        def _():
            take(block - 1)

        return carry

    lax.fori_loop(0, blocks, one, 0)
    take(blocks - 1)
    give(blocks - 2).wait_send()
    give(blocks - 1).wait_send()


def ffn_both(rows, grad, row_halves, grad_halves, weights):
    tokens, width = rows.shape
    half = width // 2
    blocks = FF // FFN_BLOCK
    share = jax.ShapeDtypeStruct((half, FF), jnp.bfloat16)
    total = jax.ShapeDtypeStruct((tokens, width), jnp.float32)
    return pl.pallas_call(
        ffn_kernel,
        out_shape=(total, total, share, share, share),
        in_specs=whole_specs(6) + [pl.BlockSpec(memory_space=pl.ANY)],
        out_specs=tuple(whole_specs(5)),
        scratch_shapes=[
            pltpu.VMEM((2, width, 2 * FFN_BLOCK), jnp.bfloat16),
            pltpu.VMEM((2, width, FFN_BLOCK), jnp.bfloat16),
            pltpu.VMEM((tokens, FFN_BLOCK), jnp.bfloat16),
            pltpu.VMEM((tokens, 2 * FFN_BLOCK), jnp.bfloat16),
            pltpu.VMEM((4, half, tokens), jnp.bfloat16),
            pltpu.VMEM((2, half, 3 * FFN_BLOCK), jnp.bfloat16),
            pltpu.VMEM((blocks, half, 3 * FFN_BLOCK), jnp.bfloat16),
            pltpu.SemaphoreType.DMA((2, 3)),
            pltpu.SemaphoreType.DMA((blocks,)),
            pltpu.SemaphoreType.DMA((blocks,)),
        ],
        compiler_params=pltpu.CompilerParams(
            collective_id=5, has_side_effects=True, vmem_limit_bytes=58 * 2**20
        ),
        name="ffn_both",
    )(rows, grad, *row_halves, *grad_halves, weights)


EXTRA = 128


def physical_axes(mesh):
    shape = mesh.devices.shape
    names = []
    sizes = []
    for axis, extent in enumerate(shape):
        line = np.moveaxis(mesh.devices, axis, 0).reshape(extent, -1)[:, 0]
        places = [tuple(d.coords) + (d.core_on_chip,) for d in line]
        parts = []
        for dim, label in enumerate(("x", "y", "z", "core")):
            values = [p[dim] for p in places]
            if len(set(values)) > 1:
                step = next(i for i in range(extent) if values[i] != values[0])
                parts.append((step, label, len(set(values))))
        for step, label, size in sorted(parts, reverse=True):
            names.append(label)
            sizes.append(size)
    return tuple(names), tuple(sizes)


def pack_small(norm1_gain, norm2_gain, down, up, bias, group):
    rows = down.shape[0]

    def column(vector):
        return jnp.pad(vector, (0, rows - vector.shape[0]))[:, None]

    pieces = [
        down,
        column(norm1_gain),
        column(norm2_gain),
        column(bias),
        column(group),
        jnp.zeros((rows, 4), down.dtype),
        up.T.reshape(rows, 8),
        jnp.zeros((rows, EXTRA - 32), down.dtype),
    ]
    return jnp.concatenate(pieces, axis=1)


def unpack_small(small, devices):
    rows = small.shape[0] // devices
    by_device = small.reshape(devices, rows, EXTRA)
    down = small[:, :16]
    gain_one = small[:, 16]
    gain_two = small[:, 17]
    bias = by_device[:, : KEYS // devices, 18].reshape(KEYS)
    group = by_device[:, : HEAD_V // devices, 19].reshape(HEAD_V)
    up = small[:, 24:32].reshape(KEYS, 16).T
    return down, gain_one, gain_two, bias, group, up


def pack_small_grads(down, gain_one, gain_two, bias, group, up, devices):
    rows = gain_one.shape[0] // devices

    def column(vector):
        parts = vector.reshape(devices, -1)
        parts = jnp.pad(parts, ((0, 0), (0, rows - parts.shape[1])))
        return parts.reshape(devices * rows, 1)

    pieces = [
        down,
        gain_one[:, None],
        gain_two[:, None],
        column(bias),
        column(group),
        jnp.zeros((rows * devices, 4), jnp.float32),
        up.T.reshape(rows * devices, 8),
        jnp.zeros((rows * devices, EXTRA - 32), jnp.float32),
    ]
    return jnp.concatenate(pieces, axis=1)


def core_halves(rows, names, sizes):
    width = rows.shape[1]
    at = names.index("core")
    before = int(np.prod(sizes[:at], initial=1))
    after = width // before // sizes[at]
    core = lax.axis_index("core")

    def half(which):
        return jnp.concatenate(
            [
                lax.dynamic_slice_in_dim(rows, (2 * i + which) * after, after, 1)
                for i in range(before)
            ],
            axis=1,
        )

    return half(core), half(1 - core)


def swap_cores(values):
    return lax.ppermute(values, "core", [(0, 1), (1, 0)])


def pair_sum(halves, gradient):
    mine, other = halves
    taken = swap_cores(flat_grad(other, gradient).astype(jnp.bfloat16))
    return (flat_grad(mine, gradient) + taken.astype(jnp.float32)).astype(jnp.bfloat16)


def flat_grad(inputs, gradient):
    return jnp.einsum("td,te->de", inputs, gradient, preferred_element_type=jnp.float32)


def by_chip(values, names, sizes):
    chips = tuple(size for name, size in zip(names, sizes) if name != "core")
    return values.reshape(*chips, -1, values.shape[-1])


def pass_along(values, left, name):
    at = left.index(name)
    size = values.shape[at]
    own = lax.axis_index(name)
    arrived = []
    for shift in range(1, size):
        given = lax.dynamic_index_in_dim(values, lax.rem(own + shift, size), at, False)
        arrived.append(
            lax.ppermute(given, name, [(i, (i + shift) % size) for i in range(size)])
        )
    return arrived


def take_in(values, arrived, left, name):
    at = left.index(name)
    total = lax.dynamic_index_in_dim(values, lax.axis_index(name), at, False).astype(jnp.float32)
    for term in arrived:
        total = total + term.astype(jnp.float32)
    return total, [other for other in left if other != name]


def reduce_kernel(plan, *refs):
    inputs, jobs, sizes, slots = plan
    count = len(jobs)
    in_refs = refs[:inputs]
    outputs = max(job[4] for job in jobs) + 1
    out_refs = refs[inputs : inputs + outputs]
    scratch = refs[inputs + outputs :]
    send_sem, recv_sem = scratch[-2:]
    scratch = list(scratch[:-2])

    reached = sorted({name for job in jobs for name in job[3]})
    barrier = pltpu.get_barrier_semaphore()
    peers = 0
    for name in reached:
        for shift in range(1, sizes[name]):
            peer = lax.rem(lax.axis_index(name) + shift, sizes[name])
            pl.semaphore_signal(barrier, inc=1, device_id={name: peer}, device_id_type=MESH)
            peers += 1
    pl.semaphore_wait(barrier, peers)

    class Job:
        pass

    work = []
    slot = 0
    for which, columns, axes, order, out, out_columns in jobs:
        job = Job()
        job.left = list(axes)
        job.order = order
        job.out = out_refs[out]
        job.out_columns = slice(*out_columns)
        job.source = in_refs[which]
        job.columns = slice(*columns)
        job.got = [scratch.pop(0) for _ in order]
        job.kept = [scratch.pop(0) for _ in order[:-1]]
        job.slots = []
        for name in order:
            job.slots.append(slot)
            slot += sizes[name] - 1
        work.append(job)

    def part(job, index):
        at = job.left.index(job.order[job.step])
        lead = [slice(None)] * len(job.left)
        lead[at] = index
        return job.source.at[(*lead, slice(None), job.columns)]

    def copies(job):
        name = job.order[job.step]
        own = lax.axis_index(name)
        for shift in range(1, sizes[name]):
            peer = lax.rem(own + shift, sizes[name])
            at = job.slots[job.step] + shift - 1
            yield pltpu.make_async_remote_copy(
                src_ref=part(job, peer),
                dst_ref=job.got[job.step].at[shift - 1],
                send_sem=send_sem.at[at],
                recv_sem=recv_sem.at[at],
                device_id={name: peer},
                device_id_type=MESH,
            )

    def start(job):
        for copy in copies(job):
            copy.start()

    def add(job):
        name = job.order[job.step]
        at = job.left.index(name)
        own = lax.axis_index(name)
        rest = [n for n in job.left if n != name]
        last = job.step == len(job.order) - 1
        total = int(np.prod([sizes[n] for n in rest], initial=1))
        got = job.got[job.step]
        for copy in copies(job):
            copy.wait()
        source, columns, step = job.source, job.columns, job.step

        def one(i, carry):
            index = []
            for n in reversed(rest):
                index.insert(0, lax.rem(i, sizes[n]))
                i = lax.div(i, sizes[n])
            lead = list(index)
            lead.insert(at, own)
            value = source[(*lead, slice(None), columns)].astype(jnp.float32)
            for shift in range(1, sizes[name]):
                value = value + got[(shift - 1, *index)].astype(jnp.float32)
            if last:
                job.out[:, job.out_columns] = value
            else:
                job.kept[step][tuple(index)] = value.astype(jnp.bfloat16)
            return carry

        if total == 1:
            one(jnp.int32(0), 0)
        else:
            lax.fori_loop(0, total, one, 0)
        job.left = rest
        if not last:
            job.source = job.kept[step]
            job.columns = slice(None)
            job.step += 1
            start(job)

    for job in work:
        job.step = 0
        start(job)
    for step in range(max(len(job.order) for job in work)):
        for job in work:
            if len(job.order) > step:
                add(job)


def reduce_rest(arrays, jobs, sizes, rows, widths, collective):
    scratch = []
    slots = 0
    for which, (begin, end), axes, order, out, out_columns in jobs:
        left = list(axes)
        kept = []
        got = []
        for name in order:
            left.remove(name)
            shape = tuple(sizes[n] for n in left)
            got.append(pltpu.VMEM((sizes[name] - 1, *shape, rows, end - begin), jnp.bfloat16))
            kept.append(pltpu.VMEM((*shape, rows, end - begin), jnp.bfloat16))
            slots += sizes[name] - 1
        scratch += got + kept[:-1]
    scratch += [pltpu.SemaphoreType.DMA((slots,))] * 2
    return pl.pallas_call(
        partial(reduce_kernel, (len(arrays), jobs, sizes, slots)),
        out_shape=tuple(jax.ShapeDtypeStruct((rows, width), jnp.float32) for width in widths),
        in_specs=whole_specs(len(arrays)),
        out_specs=tuple(whole_specs(len(widths))),
        scratch_shapes=scratch,
        compiler_params=pltpu.CompilerParams(
            collective_id=collective, has_side_effects=True, vmem_limit_bytes=40 * 2**20
        ),
        name="reduce_rest",
    )(*arrays)


def chip_orders(names):
    first, second, last = [name for name in names if name != "core"]
    return (first, second, last), (second, last, first), (last, first, second)


def two_orders(names):
    first, second, last = [name for name in names if name != "core"]
    return (first, second, last), (second, last, first)


def last_orders(names):
    first, second, last = [name for name in names if name != "core"]
    return (first, second, last), (second, first, last)


def local(
    names,
    sizes,
    seq_axes,
    tokens,
    prefix_len,
    norm1_gain,
    query_weight,
    key_weight,
    value_weight,
    gate_weight,
    decay_down,
    decay_up,
    decay_bias,
    group_gain,
    out_weight,
    norm2_gain,
    ffn_gate,
    ffn_up,
    ffn_down,
    out_grad,
):
    devices = int(np.prod(sizes))
    orders = chip_orders(names)
    wide_order, long_order, late_order = (order[::-1] for order in orders)
    small_shard = pack_small(norm1_gain, norm2_gain, decay_down, decay_up, decay_bias, group_gain)
    first, small_full = gather_first(
        names,
        sizes,
        (query_weight, key_weight, value_weight, gate_weight, small_shard),
        (3072, EXTRA),
        (
            (3, 0, (0, 1024), (2048, 3072), wide_order),
            (4, 1, (0, EXTRA), (0, EXTRA), wide_order),
            (0, 0, (0, 128), (0, 128), wide_order),
            (2, 0, (0, 1024), (1024, 2048), long_order),
            (0, 0, (128, 384), (128, 384), long_order),
            (1, 0, (0, 512), (512, 1024), late_order),
            (0, 0, (384, 512), (384, 512), late_order),
        ),
    )
    ffn_shard = jnp.concatenate([ffn_gate, ffn_up, ffn_down.T, out_weight], axis=1)
    ffn_full = lax.all_gather(ffn_shard, names, axis=0, tiled=True)
    weight_o = ffn_full[:, 3 * FF :]
    mixer_full = first.reshape(-1, 3072)
    small_full = small_full.reshape(-1, EXTRA)
    weight_down, gain_one, gain_two, bias_full, gain_group, weight_up = unpack_small(
        small_full, devices
    )
    seq_count, tok_count, feature_count = tokens.shape
    rows = seq_count * tok_count
    resid_in = tokens.reshape(rows, feature_count).astype(jnp.float32)
    scale_one = rms_scale(resid_in)
    unit_one = resid_in * scale_one
    normed = (unit_one * gain_one.astype(jnp.float32)).astype(jnp.bfloat16)
    projected = project(normed, mixer_full).astype(jnp.bfloat16)
    lowrank = project(normed, weight_down).astype(jnp.bfloat16)
    logits = project(lowrank, weight_up) + bias_full.astype(jnp.float32)
    decays = jax.nn.log_sigmoid(logits) / 16.0
    wide_gain = jnp.broadcast_to(gain_group.astype(jnp.float32)[None], (8, HEAD_V))
    gated_rows, unit_group, scale_group, cum, states, prefix_state = mix_forward(
        seq_axes, prefix_len, projected, decays, wide_gain
    )
    resid_mid = resid_in + project(gated_rows, weight_o)
    scale_two = rms_scale(resid_mid)
    unit_two = resid_mid * scale_two
    normed_two = (unit_two * gain_two.astype(jnp.float32)).astype(jnp.bfloat16)
    out_grad = out_grad.reshape(rows, feature_count)
    grad_out = out_grad.astype(jnp.float32)
    ffn_out, grad_normed_two, gate_sum, up_sum, down_sum = ffn_both(
        normed_two,
        out_grad,
        core_halves(normed_two, names, sizes),
        core_halves(out_grad, names, sizes),
        ffn_full,
    )
    layer_out = (resid_mid + ffn_out).astype(jnp.bfloat16)
    gain_two_grad = jnp.sum(grad_normed_two * unit_two, axis=0)
    grad_mid = grad_out + rms_back(
        grad_normed_two * gain_two.astype(jnp.float32), unit_two, scale_two
    )
    grad_branch = grad_mid.astype(jnp.bfloat16)
    gated_grad = back_project(grad_branch, weight_o).astype(jnp.bfloat16)
    out_sum = pair_sum(core_halves(gated_rows, names, sizes), grad_branch)
    groups = (
        jnp.concatenate([gate_sum, out_sum, down_sum[:, :896]], axis=1),
        jnp.concatenate([up_sum, down_sum[:, 896:]], axis=1),
    )
    groups, gated_grad = lax.optimization_barrier((groups, gated_grad))
    chips = [name for name in names if name != "core"]
    orders = two_orders(names)
    lefts = [chips] * 2
    groups = [by_chip(group, names, sizes) for group in groups]
    arrived = [pass_along(g, left, order[0]) for g, left, order in zip(groups, lefts, orders)]
    grad_projected, grad_decay, group_grad = mix_backward(
        seq_axes,
        prefix_len,
        projected,
        cum,
        states,
        prefix_state,
        gated_grad,
        unit_group,
        scale_group,
        wide_gain,
    )
    arrived, grad_projected, grad_decay = lax.optimization_barrier(
        (arrived, grad_projected, grad_decay)
    )
    taken = [
        take_in(g, more, left, order[0])
        for g, more, left, order in zip(groups, arrived, lefts, orders)
    ]
    groups = [total.astype(jnp.bfloat16) for total, _ in taken]
    lefts = [left for _, left in taken]
    arrived = [pass_along(g, left, order[1]) for g, left, order in zip(groups, lefts, orders)]
    late = flat_grad(normed, grad_projected).astype(jnp.bfloat16)
    grad_logits = (grad_decay * jax.nn.sigmoid(-logits) / 16.0).astype(jnp.bfloat16)
    bias_grad = jnp.sum(grad_logits.astype(jnp.float32), axis=0)
    up_rank_grad = flat_grad(lowrank, grad_logits)
    grad_lowrank = back_project(grad_logits, weight_up).astype(jnp.bfloat16)
    down_rank_grad = flat_grad(normed, grad_lowrank)
    grad_normed = back_project(grad_projected, mixer_full) + back_project(
        grad_lowrank, weight_down
    )
    gain_one_grad = jnp.sum(grad_normed * unit_one, axis=0)
    tokens_grad = grad_mid + rms_back(
        grad_normed * gain_one.astype(jnp.float32), unit_one, scale_one
    )
    small_grads = pack_small_grads(
        down_rank_grad,
        gain_one_grad,
        gain_two_grad,
        bias_grad,
        group_grad[0],
        up_rank_grad,
        devices,
    ).astype(jnp.bfloat16)
    arrived, late, small_grads, tokens_grad = lax.optimization_barrier(
        (arrived, late, small_grads, tokens_grad)
    )
    groups = [
        take_in(g, more, left, order[1])[0].astype(jnp.bfloat16)
        for g, more, left, order in zip(groups, arrived, lefts, orders)
    ]
    own_rows = feature_count // devices
    late = late.reshape(*sizes, own_rows, -1)
    small_grads = small_grads.reshape(*sizes, own_rows, -1)
    size_of = dict(zip(names, sizes))
    ends = last_orders(names)
    jobs = [
        (2, (begin, begin + 768), names, ("core", *order), 2, (begin, begin + 768))
        for begin, order in zip(range(0, 3072, 768), ends * 2)
    ] + [
        (3, (0, EXTRA), names, ("core", *ends[0]), 3, (0, EXTRA)),
    ] + [
        (i, (0, groups[i].shape[-1]), (order[2],), (order[2],), i, (0, groups[i].shape[-1]))
        for i, order in enumerate(orders)
    ]
    first_group, second_group, mine, small = reduce_rest(
        (*groups, late, small_grads), jobs, size_of, own_rows, (4736, 4736, 3072, EXTRA), 3
    )
    shape = tokens.shape
    return (
        layer_out.reshape(shape),
        tokens_grad.reshape(shape),
        small[:, 16],
        mine[:, :512],
        mine[:, 512:1024],
        mine[:, 1024:2048],
        mine[:, 2048:],
        small[:, :16],
        small[:, 24:32].reshape(KEYS // devices, 16).T,
        small[: KEYS // devices, 18],
        small[: HEAD_V // devices, 19],
        first_group[:, FF : FF + VALS],
        small[:, 17],
        first_group[:, :FF],
        second_group[:, :FF],
        jnp.concatenate([first_group[:, FF + VALS :], second_group[:, FF:]], axis=1).T,
    )


def solution(mesh):
    names, sizes = physical_axes(mesh)
    cut = next(
        i for i in range(len(sizes) + 1) if np.prod(sizes[:i], initial=1) == mesh.shape["dp"]
    )
    dp, seq = names[:cut], names[cut:]
    split = Mesh(mesh.devices.reshape(sizes), names)
    return jax.shard_map(
        partial(local, names, sizes, tuple(zip(seq, sizes[cut:]))),
        mesh=split,
        in_specs=(
            P(dp, seq, None),
            P(dp),
            P(names),
            P(names, None),
            P(names, None),
            P(names, None),
            P(names, None),
            P(names, None),
            P(None, names),
            P(names),
            P(names),
            P(names, None),
            P(names),
            P(names, None),
            P(names, None),
            P(None, names),
            P(dp, seq, None),
        ),
        out_specs=(
            P(dp, seq, None),
            P(dp, seq, None),
            P(names),
            P(names, None),
            P(names, None),
            P(names, None),
            P(names, None),
            P(names, None),
            P(None, names),
            P(names),
            P(names),
            P(names, None),
            P(names),
            P(names, None),
            P(names, None),
            P(None, names),
        ),
        check_vma=False,
    )
```
